32 devices in a mesh: fsdp: 4 (over y, core), context: 2 (over x), tensor: 4 (over z).
Axes of the slice: x: 2, y: 2, z: 4, core: 2. Of those that a mesh axis runs over, the one named last changes fastest.
Arguments:
- tokens: bfloat16 [2048, 1024], P(('fsdp', 'context')), may hold values from -6 to 6
- grad_out: bfloat16 [2048, 1024], P(('fsdp', 'context')), may hold values from -6 to 6
- lengths: int32 [8], replicated, may hold values from 1 to 1024, 2048 in all
- deal: int32 [2048], replicated, may hold values from 0 to 2047, each once
- adapter_of: int32 [8], replicated, may hold values from 0 to 7
- attention_gain: bfloat16 [1024], replicated, may hold values from 0.5 to 1.5
- attention_proj: bfloat16 [1024, 3, 1024], P('fsdp', None, 'tensor'), may hold values from -0.1875 to 0.1875
- attention_out: bfloat16 [1024, 1024], P('tensor', 'fsdp'), may hold values from -1 to 1
- feed_gain: bfloat16 [1024], replicated, may hold values from 0.5 to 1.5
- feed_in: bfloat16 [1024, 2, 2624], P('fsdp', None, 'tensor'), may hold values from -0.1875 to 0.1875
- feed_out: bfloat16 [2624, 1024], P('tensor', 'fsdp'), may hold values from -0.125 to 0.125
- attention_proj_down: bfloat16 [8, 1024, 16], replicated, may hold values from -0.1875 to 0.1875
- attention_proj_up: bfloat16 [8, 16, 3, 1024], P(None, None, None, 'tensor'), may hold values from -1.5 to 1.5
- attention_out_down: bfloat16 [8, 1024, 16], P(None, 'tensor'), may hold values from -1 to 1
- attention_out_up: bfloat16 [8, 16, 1024], replicated, may hold values from -1.5 to 1.5
- feed_in_down: bfloat16 [8, 1024, 16], replicated, may hold values from -0.1875 to 0.1875
- feed_in_up: bfloat16 [8, 16, 2, 2624], P(None, None, None, 'tensor'), may hold values from -1.5 to 1.5
- feed_out_down: bfloat16 [8, 2624, 16], P(None, 'tensor'), may hold values from -0.125 to 0.125
- feed_out_up: bfloat16 [8, 16, 1024], replicated, may hold values from -1.5 to 1.5
Outputs:
- output: bfloat16 [2048, 1024], P(('fsdp', 'context'))
- grad_tokens: bfloat16 [2048, 1024], P(('fsdp', 'context'))
- grad_attention_proj_down: float32 [8, 1024, 16], replicated
- grad_attention_proj_up: float32 [8, 16, 3, 1024], P(None, None, None, 'tensor')
- grad_attention_out_down: float32 [8, 1024, 16], P(None, 'tensor')
- grad_attention_out_up: float32 [8, 16, 1024], replicated
- grad_feed_in_down: float32 [8, 1024, 16], replicated
- grad_feed_in_up: float32 [8, 16, 2, 2624], P(None, None, None, 'tensor')
- grad_feed_out_down: float32 [8, 2624, 16], P(None, 'tensor')
- grad_feed_out_up: float32 [8, 16, 1024], replicated
The draws below stay inside these ranges and needn't reach their ends.
Inputs may be any that keep to these rules, and one draw needn't show every extreme that they name: lengths of the 8 sequences, packed end to end in order; they sum to 2048 and the largest is 1024. Each packed token once; row p of tokens and grad_out holds packed token deal[p].
All inputs are finite; a program needn't handle non-finite values.
Results may differ from the reference program's by a relative error of at most 0.025.
Values may be sent and summed in bfloat16 or wider, within the bound.
No kernel may reach another device: no remote copies, remote signals or barrier semaphores. Data moves between devices by JAX's collectives and lax.ppermute only.
A program may use at most 192 MiB of HBM per device.

```python
import math
import jax
import jax.numpy as jnp
import numpy as np
from jax import lax

D = 1024
HEADS = 16
HEAD_DIM = 64
FF = 2624
RANK = 16
NSET = 8
TOKENS = 2048
SEQS = 8
MAXLEN = 1024


def place_ends(drawn, own_key, smallest, top_value):
    shape = drawn.shape
    index_at = [jax.random.randint(jax.random.fold_in(own_key, axis), (), 0, shape[axis]) for axis in range(len(shape))]
    drawn = drawn.at[tuple(index_at)].set(smallest)
    longest = shape.index(max(shape))
    index_at[longest] = (index_at[longest] + 1) % shape[longest]
    return drawn.at[tuple(index_at)].set(top_value)


def block_levels(stream_key, extent, split, low, largest):
    factor_of = 1.0
    for axis_at, blocks in split:
        heights = jax.random.uniform(jax.random.fold_in(jax.random.fold_in(stream_key, 6), axis_at), (blocks,), jnp.float32, low / len(split), largest / len(split))
        factor_of = factor_of * jnp.repeat(jnp.exp(heights), extent[axis_at] // blocks).reshape((-1,) + (1,) * (len(extent) - 1 - axis_at))
    return factor_of


def split_up(count, total, reach, lean):
    portions = [(1 << 20) // math.isqrt(rank ** lean) + 1 for rank in range(2, count + 1)]
    spare, counts = total - reach - (count - 1), [1] * (count - 1)
    while spare > 0:
        candidates = [i for i in range(count - 1) if counts[i] < reach]
        pool, remaining = sum([portions[i] for i in candidates]), spare
        for i in candidates:
            extra = min(reach - counts[i], max(1, remaining * portions[i] // pool), spare)
            counts[i] = counts[i] + extra
            spare = spare - extra
    return np.array([reach] + counts)


def uneven_parts(stream_key, amount, total, most, lean):
    if amount == 2:
        one = jax.random.randint(stream_key, (), max(1, total - most), min(most, total - 1) + 1)
        return jnp.stack([one, total - one])
    sizes = jnp.asarray(split_up(amount, total, most, lean), jnp.int32)
    twos = (amount - 1) // 2
    giver, receiver = sizes[1:1 + 2 * twos:2], sizes[2:2 + 2 * twos:2]
    margin = jnp.minimum(giver - 1, most - receiver)
    shifted = jax.random.randint(jax.random.fold_in(stream_key, 1), (twos,), 0, 1 << 20) % (margin + 1)
    sizes = sizes.at[1:1 + 2 * twos:2].set(giver - shifted).at[2:2 + 2 * twos:2].set(receiver + shifted)
    return sizes[jax.random.permutation(jax.random.fold_in(stream_key, 2), amount)]


def scatter_about(own_key, shape, deviation, reach, cuts=(), kind=jnp.bfloat16):
    values = jax.random.normal(own_key, shape, jnp.float32) * deviation
    if len(cuts) > 0:
        values = block_levels(own_key, shape, cuts, -0.22, 0.18) * values
    return jnp.clip(values, min=-reach, max=reach).astype(kind)


def setup_inputs(seed: int = 0) -> dict:
    key_of = jax.random.split(jax.random.key(seed), 20)
    tokens = scatter_about(key_of[0], (TOKENS, D), 1.0, 6.0, ((0, 8),))
    grad_out = scatter_about(key_of[1], (TOKENS, D), 1.0, 6.0, ((0, 8),))
    lengths = uneven_parts(key_of[2], SEQS, TOKENS, MAXLEN, 2).astype(jnp.int32)
    deal = jax.random.permutation(key_of[3], TOKENS).astype(jnp.int32)
    adapter_of = place_ends(jax.random.randint(key_of[4], (SEQS,), 0, NSET), jax.random.fold_in(key_of[4], 1), 0, NSET - 1).astype(jnp.int32)
    attention_gain = jnp.clip(1.0 + 0.1 * jax.random.normal(key_of[5], (D,), jnp.float32), 0.5, 1.5).astype(jnp.bfloat16)
    attention_proj = scatter_about(key_of[6], (D, 3, D), D ** -0.5, 0.1875, ((0, 4), (2, 4)))
    attention_out = scatter_about(key_of[7], (D, D), (D // 32) ** -0.5, 1.0, ((0, 4), (1, 4)))
    feed_gain = jnp.clip(1.0 + 0.1 * jax.random.normal(key_of[8], (D,), jnp.float32), 0.5, 1.5).astype(jnp.bfloat16)
    feed_in = scatter_about(key_of[9], (D, 2, FF), D ** -0.5, 0.1875, ((0, 4), (2, 4)))
    feed_out = scatter_about(key_of[10], (FF, D), FF ** -0.5, 0.125, ((0, 4), (1, 4)))
    attention_proj_down = scatter_about(key_of[11], (NSET, D, RANK), D ** -0.5, 0.1875)
    attention_proj_up = scatter_about(key_of[12], (NSET, RANK, 3, D), RANK ** -0.5, 1.5, ((3, 4),))
    attention_out_down = scatter_about(key_of[13], (NSET, D, RANK), (D // 32) ** -0.5, 1.0, ((1, 4),))
    attention_out_up = scatter_about(key_of[14], (NSET, RANK, D), RANK ** -0.5, 1.5)
    feed_in_down = scatter_about(key_of[15], (NSET, D, RANK), D ** -0.5, 0.1875)
    feed_in_up = scatter_about(key_of[16], (NSET, RANK, 2, FF), RANK ** -0.5, 1.5, ((3, 4),))
    feed_out_down = scatter_about(key_of[17], (NSET, FF, RANK), FF ** -0.5, 0.125, ((1, 4),))
    feed_out_up = scatter_about(key_of[18], (NSET, RANK, D), RANK ** -0.5, 1.5)
    return {"tokens": tokens, "grad_out": grad_out, "lengths": lengths, "deal": deal, "adapter_of": adapter_of, "attention_gain": attention_gain, "attention_proj": attention_proj, "attention_out": attention_out, "feed_gain": feed_gain, "feed_in": feed_in, "feed_out": feed_out, "attention_proj_down": attention_proj_down, "attention_proj_up": attention_proj_up, "attention_out_down": attention_out_down, "attention_out_up": attention_out_up, "feed_in_down": feed_in_down, "feed_in_up": feed_in_up, "feed_out_down": feed_out_down, "feed_out_up": feed_out_up}


@jax.custom_vjp
def low(v):
    return lax.optimization_barrier(v.astype(jnp.bfloat16)).astype(jnp.float32)

@jax.custom_vjp
def low_back(v):
    return v

def low_keep(v):
    return (low(v), None)

def low_pass(kept, upstream_gradient):
    return (upstream_gradient,)

def back_keep(v):
    return (v, None)

def back_low(kept, upstream_gradient):
    return (low(upstream_gradient),)
low.defvjp(low_keep, low_pass)
low_back.defvjp(back_keep, back_low)

def both_ways(value):
    return low_back(low(value))

def product(left, right):
    return jnp.dot(left, right, precision=lax.Precision.HIGHEST, preferred_element_type=jnp.float32)

def layer_norm(values, norm_gain):
    row_average = lax.optimization_barrier(jnp.mean(values, axis=1, keepdims=True))
    centered_input = values - row_average
    inverse_deviation = lax.rsqrt(lax.optimization_barrier(jnp.mean(centered_input * centered_input, axis=1, keepdims=True)) + 1e-05)
    return centered_input * inverse_deviation * norm_gain

def flat_down(table):
    return jnp.transpose(table, (1, 0, 2)).reshape(table.shape[1], table.shape[0] * table.shape[2])

def flat_up(table):
    return table.reshape(table.shape[0] * table.shape[1], -1)

def locate(lengths, deal):
    ends = jnp.cumsum(lengths).astype(jnp.int32)
    starts = (ends - lengths).astype(jnp.int32)
    segment = lax.optimization_barrier(jnp.sum((deal[:, None] >= ends[None, :]).astype(jnp.int32), axis=1)).astype(jnp.int32)
    member = segment[:, None] == jnp.arange(lengths.shape[0], dtype=jnp.int32)[None, :]
    place = (deal - lax.optimization_barrier(jnp.sum(jnp.where(member, starts[None, :], 0), axis=1))).astype(jnp.int32)
    return (segment, place)

def rotary(place, half):
    steps = jnp.arange(half, dtype=jnp.float32)
    freq = jnp.exp(steps * (-math.log(160000.0) / half))
    angle = place.astype(jnp.float32)[:, None] * freq[None, :]
    return (jnp.cos(angle)[:, None, :], jnp.sin(angle)[:, None, :])

def rotate(values, cosine, sine):
    half = values.shape[-1] // 2
    first, second = (values[..., :half], values[..., half:])
    return jnp.concatenate([first * cosine - second * sine, second * cosine + first * sine], axis=-1)

def attend(query, key, value, segment):
    count = query.shape[0]
    block = math.gcd(count, 256)
    scale = query.shape[2] ** (-0.5)

    def one_block(inputs):
        rows_q, seg_q = inputs
        scores = jnp.einsum('qhd,khd->hqk', rows_q, key, precision=lax.Precision.HIGHEST) * scale
        scores = low_back(scores)
        mask = (seg_q[:, None] == segment[None, :])[None]
        scores = jnp.where(mask, scores, -1e+30)
        highest = lax.optimization_barrier(jnp.max(scores, axis=2, keepdims=True))
        weights = jnp.exp(scores - highest)
        prob = weights / lax.optimization_barrier(jnp.sum(weights, axis=2, keepdims=True))
        return jnp.einsum('hqk,khd->qhd', low(prob), value, precision=lax.Precision.HIGHEST)
    number = count // block
    heads, size = (query.shape[1], query.shape[2])
    result = lax.map(jax.checkpoint(one_block), (query.reshape(number, block, heads, size), segment.reshape(number, block)))
    return result.reshape(count, heads, size)

def reference(tokens, grad_out, lengths, deal, adapter_of, attention_gain, attention_proj, attention_out, feed_gain, feed_in, feed_out, attention_proj_down, attention_proj_up, attention_out_down, attention_out_up, feed_in_down, feed_in_up, feed_out_down, feed_out_up):
    single = jnp.float32
    segment, place = locate(lengths, deal)
    member = segment[:, None] == jnp.arange(lengths.shape[0], dtype=jnp.int32)[None, :]
    chosen = lax.optimization_barrier(jnp.sum(jnp.where(member, adapter_of[None, :], 0), axis=1)).astype(jnp.int32)
    picked = jnp.repeat((chosen[:, None] == jnp.arange(NSET, dtype=jnp.int32)[None, :]).astype(single), RANK, axis=1)
    cosine, sine = rotary(place, HEAD_DIM // 2)
    first_norm_gain = attention_gain.astype(single)
    second_norm_gain = feed_gain.astype(single)
    proj_weight = attention_proj.astype(single).reshape(D, 3 * D)
    out_weight = attention_out.astype(single)
    in_weight = feed_in.astype(single).reshape(D, 2 * FF)
    down_weight = feed_out.astype(single)

    def forward(residual_stream, proj_down, proj_up, out_down, out_up, in_down, in_up, last_down, last_up):
        normed_one = low(layer_norm(residual_stream, first_norm_gain))
        adapted_q = both_ways(picked * product(normed_one, flat_down(proj_down)))
        proj = low_back(product(normed_one, proj_weight) + product(adapted_q, flat_up(proj_up)))
        proj = proj.reshape(TOKENS, 3, HEADS, HEAD_DIM)
        query = low(rotate(proj[:, 0], cosine, sine))
        key = low(rotate(proj[:, 1], cosine, sine))
        value = low(proj[:, 2])
        attended = attend(query, key, value, segment)
        heads_out = both_ways(attended.reshape(TOKENS, D))
        adapted_o = both_ways(picked * product(heads_out, flat_down(out_down)))
        branch = low_back(product(heads_out, out_weight) + product(adapted_o, flat_up(out_up)))
        middle_hidden = residual_stream + branch
        normed_two = low(layer_norm(middle_hidden, second_norm_gain))
        adapted_i = both_ways(picked * product(normed_two, flat_down(in_down)))
        gates = low_back(product(normed_two, in_weight) + product(adapted_i, flat_up(in_up))).reshape(TOKENS, 2, FF)
        activity = low(jax.nn.gelu(gates[:, 0], approximate=False) * gates[:, 1])
        adapted_d = both_ways(picked * product(activity, flat_down(last_down)))
        feed = low_back(product(activity, down_weight) + product(adapted_d, flat_up(last_up)))
        return middle_hidden + feed
    primals = (tokens.astype(single), attention_proj_down.astype(single), attention_proj_up.astype(single), attention_out_down.astype(single), attention_out_up.astype(single), feed_in_down.astype(single), feed_in_up.astype(single), feed_out_down.astype(single), feed_out_up.astype(single))
    output, pullback = jax.vjp(forward, *primals)
    grads = pullback(grad_out.astype(single))
    return (output.astype(jnp.bfloat16), grads[0].astype(jnp.bfloat16), grads[1], grads[2], grads[3], grads[4], grads[5], grads[6], grads[7], grads[8])
```

```python
import math

import jax
import jax.numpy as jnp
from jax import lax
from jax.experimental import pallas as pl
from jax.experimental.pallas import tpu as pltpu
from jax.sharding import PartitionSpec as P

HEAD_DIM = 64


rope_base = 160000.0
epsilon = 1e-05
negative = -1e30
single = jnp.float32
low = jnp.bfloat16
scale = HEAD_DIM ** (-0.5)
token_axes = ("fsdp", "context")
every_axis = ("fsdp", "context", "tensor")


def nn(left, right):
    return lax.dot_general(
        left, right, (((1,), (0,)), ((), ())), preferred_element_type=jnp.float32
    )


def nt(left, right):
    return lax.dot_general(
        left, right, (((1,), (1,)), ((), ())), preferred_element_type=jnp.float32
    )


def tn(left, right):
    return lax.dot_general(
        left, right, (((0,), (0,)), ((), ())), preferred_element_type=jnp.float32
    )


def call(body, outs, ids, args, scratch=(), vmem=40, name=None):
    whole = pl.BlockSpec(memory_space=pltpu.VMEM)
    return pl.pallas_call(
        body,
        out_shape=[jax.ShapeDtypeStruct(shape, kind) for shape, kind in outs],
        in_specs=[pl.BlockSpec(memory_space=pltpu.SMEM)] + [whole] * len(args),
        out_specs=[whole] * len(outs),
        scratch_shapes=list(scratch),
        compiler_params=pltpu.CompilerParams(vmem_limit_bytes=vmem << 20),
        name=name,
    )(ids, *args)


def swap_pairs(axis, size, bit):
    return [(i, i ^ bit) for i in range(size)]


def layer_norm_rows(values):
    centered = values - jnp.mean(values, axis=1, keepdims=True)
    rstd = lax.rsqrt(jnp.mean(centered * centered, axis=1, keepdims=True) + epsilon)
    return (centered * rstd, rstd)


def layer_norm_back(upstream, gain, xhat, rstd):
    scaled = upstream * gain
    return rstd * (
        scaled
        - jnp.mean(scaled, axis=1, keepdims=True)
        - xhat * jnp.mean(scaled * xhat, axis=1, keepdims=True)
    )


def swap_halves(u):
    width = u.shape[1]
    half = HEAD_DIM // 2
    lane = lax.broadcasted_iota(jnp.int32, (1, width), 1)
    return jnp.where(
        lane % HEAD_DIM < half, pltpu.roll(u, width - half, 1), pltpu.roll(u, half, 1)
    )


def head_row(width, head):
    lane = lax.broadcasted_iota(jnp.int32, (1, width), 1)
    return (lane // HEAD_DIM == head).astype(single)


def each_chunk(parts, stride, step):
    base = 0
    for at, part in enumerate(parts):
        groups = part.shape[0] // stride
        if groups == 1:
            step(base, at, 0)
        else:

            def inner(j, carry, base=base, at=at):
                step(base + j, at, pl.multiple_of(j * stride, 16))
                return carry

            lax.fori_loop(0, groups, inner, 0)
        base += groups


def cols_of(ids_ref, k, width):
    return pl.ds(pl.multiple_of((ids_ref[0] ^ k) * width, 128), width)


def rows_of(ids_ref, k, height):
    return pl.ds(pl.multiple_of((ids_ref[2] ^ k) * height, 16), height)


def join_rows(ids_ref, dst_ref, mine_ref, other_ref):
    size = mine_ref.shape[0]
    dst_ref[pl.ds(ids_ref[1] * size, size)] = mine_ref[...]
    dst_ref[pl.ds((1 - ids_ref[1]) * size, size)] = other_ref[...]


def join_cols(ids_ref, dst_ref, mine_ref, other_ref):
    size = mine_ref.shape[1]
    dst_ref[:, pl.ds(pl.multiple_of(ids_ref[1] * size, 128), size)] = mine_ref[...]
    dst_ref[:, pl.ds(pl.multiple_of((1 - ids_ref[1]) * size, 128), size)] = other_ref[...]


def project_body(ids_ref, x_ref, aq_ref, up_ref, cos_ref, sin_ref, *refs):
    weights, out_ref = (refs[:-1], refs[-1])
    part = weights[0].shape[1]
    width = weights[0].shape[2]
    for j in range(3):
        acc = nn(aq_ref[...], up_ref[j])
        for k, w_ref in enumerate(weights):
            acc = acc + nn(x_ref[:, cols_of(ids_ref, k, part)], w_ref[j])
        if j < 2:
            acc = acc * cos_ref[...] + swap_halves(acc) * sin_ref[...]
        out_ref[:, j * width : (j + 1) * width] = acc.astype(low)


def attend_body(parts_n, ids_ref, own_ref, segc_ref, segr_ref, *refs):
    parts = refs[:parts_n]
    heads_ref, att_ref, lcol_ref, s_ref, m_ref, l_ref, o_ref = refs[parts_n:]
    count = own_ref.shape[0]
    width = att_ref.shape[1]
    lane = lax.broadcasted_iota(jnp.int32, (1, 128), 1)
    lcol_ref[...] = jnp.zeros_like(lcol_ref)
    att_ref[...] = jnp.zeros_like(att_ref)

    def head(h, carry):
        hm = head_row(width, h)
        q = own_ref[:, :width] * (hm * scale).astype(low)
        m_ref[...] = jnp.full_like(m_ref, negative)
        l_ref[...] = jnp.zeros_like(l_ref)
        o_ref[...] = jnp.zeros_like(o_ref)

        def scores(j, at, start):
            s = nt(q, parts[at][pl.ds(start, count), width : 2 * width])
            s = jnp.where(segc_ref[...] == segr_ref[pl.ds(j, 1), :], s, negative)
            s_ref[j] = s
            m_ref[...] = jnp.maximum(m_ref[...], s)

        each_chunk(parts, count, scores)
        top = jnp.max(m_ref[...], axis=1, keepdims=True)

        def weigh(j, at, start):
            p = jnp.exp(s_ref[j] - top)
            l_ref[...] = l_ref[...] + p
            o_ref[...] = o_ref[...] + nn(
                p.astype(low), parts[at][pl.ds(start, count), 2 * width : 3 * width]
            )

        each_chunk(parts, count, weigh)
        mass = jnp.sum(l_ref[...], axis=1, keepdims=True)
        att_ref[...] = att_ref[...] + o_ref[...] * (hm / mass)
        lcol_ref[...] = jnp.where(lane == h, top + jnp.log(mass), lcol_ref[...])
        return carry

    lax.fori_loop(0, width // HEAD_DIM, head, 0)
    heads_ref[...] = att_ref[...].astype(low)


def middle_body(ids_ref, *refs):
    heads = refs[0:4]
    wown, wnear, wa, wb, wc, wd = refs[4:10]
    od_ref, ou_ref, tokens_ref, gain_ref, go_ref, picked_ref = refs[10:16]
    iown, inear, ia, ib, ic, idd = refs[16:22]
    idn_ref, iu_ref = refs[22:24]
    lown, lnear, la, lb, lc, ld = refs[24:30]
    ldn_ref, lup_ref = refs[30:32]
    m0, m1, m2, m3, ao_ref, ai_ref, gad_ref, n2_ref, act_ref, gg_ref, mid_ref = refs[32:43]
    wide_ref, w2, w3, i2, i3, l2, l3 = refs[43:]
    join_rows(ids_ref, w2, wa, wb)
    join_rows(ids_ref, w3, wc, wd)
    join_rows(ids_ref, i2, ia, ib)
    join_rows(ids_ref, i3, ic, idd)
    join_cols(ids_ref, l2, la, lb)
    join_cols(ids_ref, l3, lc, ld)
    h0 = heads[0]
    w0 = wown
    outs_w = [wown, wnear, w2, w3]
    ins_w = [iown, inear, i2, i3]
    lasts_w = [lown, lnear, l2, l3]
    part = w0.shape[1]
    span = h0.shape[1]
    width = tokens_ref.shape[1]
    picked = picked_ref[...].astype(single)
    adapt = nt(h0[...], od_ref[0])
    for k in range(1, len(heads)):
        adapt = adapt + nt(heads[k][...], od_ref[k])
    ao = (picked * adapt).astype(low)
    ao_ref[...] = ao
    for k, w_ref in enumerate(outs_w):
        acc = nn(h0[...], w_ref[:span, :])
        for r in range(1, len(heads)):
            acc = acc + nn(heads[r][...], w_ref[r * span : (r + 1) * span, :])
        wide_ref[:, cols_of(ids_ref, k, part)] = acc
    middle = tokens_ref[...].astype(single) + wide_ref[:, :width] + nn(ao, ou_ref[...])
    wide_ref[:, :width] = middle
    quarter = mid_ref.shape[0]
    mid_ref[...] = wide_ref[rows_of(ids_ref, 0, quarter), :width]
    xhat, _ = layer_norm_rows(middle)
    n2 = (xhat * gain_ref[...]).astype(low)
    n2_ref[...] = n2
    ai = (picked * nt(n2, idn_ref[...])).astype(low)
    ai_ref[...] = ai
    gate = nn(ai, iu_ref[0])
    mult = nn(ai, iu_ref[1])
    for k, w_ref in enumerate(ins_w):
        x = n2_ref[:, cols_of(ids_ref, k, part)]
        gate = gate + nt(x, w_ref[0])
        mult = mult + nt(x, w_ref[1])
    phi = 0.5 * (1.0 + lax.erf(gate * (2.0**-0.5)))
    gated = gate * phi
    act_ref[...] = (gated * mult).astype(low)
    slope = phi + gate * jnp.exp(-0.5 * gate * gate) * (1.0 / math.sqrt(2.0 * math.pi))
    go = go_ref[...]
    gad = (nt(go, lup_ref[...]).astype(low).astype(single) * picked).astype(low)
    gad_ref[...] = gad
    ga = nn(gad, ldn_ref[...])
    for k, w_ref in enumerate(lasts_w):
        ga = ga + nt(go_ref[:, cols_of(ids_ref, k, part)], w_ref[...])
    gg0 = (slope * (ga * mult)).astype(low)
    gg1 = (ga * gated).astype(low)
    gg_ref[0] = gg0
    gg_ref[1] = gg1
    for k, w_ref in enumerate(ins_w):
        wide_ref[:, cols_of(ids_ref, k, part)] = nn(gg0, w_ref[0]) + nn(gg1, w_ref[1])
    wide_ref[:, width:] = nt(gg0, iu_ref[0]) + nt(gg1, iu_ref[1])
    for k, m_ref in enumerate([m0, m1, m2, m3]):
        m_ref[...] = wide_ref[rows_of(ids_ref, k, quarter), :].astype(low)


def feed_body(ids_ref, act_ref, ldn_ref, gai_ref, lown, lnear, la, lb, lc, ld, m0, m1, m2, m3, wide_ref, l2, l3):
    join_cols(ids_ref, l2, la, lb)
    join_cols(ids_ref, l3, lc, ld)
    part = lown.shape[1]
    quarter = m0.shape[0]
    act = act_ref[...]
    for k, w_ref in enumerate([lown, lnear, l2, l3]):
        wide_ref[:, cols_of(ids_ref, k, part)] = nn(act, w_ref[...])
    ranks = ldn_ref.shape[0]
    width = wide_ref.shape[1] - ranks
    wide_ref[:, width:] = nt(act, ldn_ref[...])
    for k, m_ref in enumerate([m0, m1, m2, m3]):
        m_ref[:, : width + ranks] = wide_ref[rows_of(ids_ref, k, quarter), :].astype(low)
        m_ref[:, width + ranks :] = gai_ref[...]


def turn_body(
    ids_ref, p0, p1, p2, p3, picked_ref, idn_ref, mid_ref, gain_ref, go_ref, ou_ref, w0, w1, wa, wb, wc, wd, od_ref,
    a0, a1, a2, a3, gm_ref, gb_ref, gai_ref, w2, w3,
):
    join_rows(ids_ref, w2, wa, wb)
    join_rows(ids_ref, w3, wc, wd)
    quarter = p0.shape[0]
    width = mid_ref.shape[1]
    part = w0.shape[1]
    rows = rows_of(ids_ref, 0, quarter)
    picked = picked_ref[rows, :].astype(single)
    total = p0[...].astype(single) + p1[...].astype(single) + p2[...].astype(single) + p3[...].astype(single)
    gai = (total[:, width:].astype(low).astype(single) * picked).astype(low)
    gai_ref[...] = gai
    upstream = total[:, :width] + nn(gai, idn_ref[...])
    xhat, rstd = layer_norm_rows(mid_ref[...])
    gm = go_ref[rows, :].astype(single) + layer_norm_back(upstream, gain_ref[...], xhat, rstd)
    gm_ref[...] = gm
    gb = gm.astype(low)
    gb_ref[...] = gb
    gao = (nt(gb, ou_ref[...]).astype(low).astype(single) * picked).astype(low)
    grads = [nn(gao, od_ref[k]) for k in range(4)]
    for k, w_ref in enumerate([w0, w1, w2, w3]):
        x = gb_ref[:, cols_of(ids_ref, k, part)]
        for r in range(4):
            span = od_ref.shape[2]
            grads[r] = grads[r] + nt(x, w_ref[r * span : (r + 1) * span, :])
    for k, a_ref in enumerate([a0, a1, a2, a3]):
        span = od_ref.shape[2]
        a_ref[:, :span] = grads[k].astype(low)
        a_ref[:, span:] = gao


def out_body(ids_ref, p0, p1, p2, p3, picked_ref, mid_ref, lup_ref, out_ref):
    quarter = p0.shape[0]
    width = mid_ref.shape[1]
    ranks = lup_ref.shape[0]
    rows = rows_of(ids_ref, 0, quarter)
    picked = picked_ref[rows, :].astype(single)
    total = p0[:, : width + ranks].astype(single)
    for p_ref in (p1, p2, p3):
        total = total + p_ref[:, : width + ranks].astype(single)
    ad = (picked * total[:, width:]).astype(low)
    out_ref[:, :width] = (mid_ref[...] + total[:, :width] + nn(ad, lup_ref[...])).astype(low)
    out_ref[:, width:] = ad


def collect_body(ids_ref, a0, a1, a2, a3, att_ref, lcol_ref, msg_ref, dcol_ref, gao_ref):
    quarter = a0.shape[0]
    count, width = att_ref.shape
    for k, a_ref in enumerate([a0, a1, a2, a3]):
        msg_ref[rows_of(ids_ref, k, quarter), :] = a_ref[:, :width]
        gao_ref[rows_of(ids_ref, k, quarter), :] = a_ref[:, width:]
    both = msg_ref[:count, :].astype(single) * att_ref[...]
    heads = width // HEAD_DIM
    lane = lax.broadcasted_iota(jnp.int32, (1, 128), 1)
    dcol = jnp.zeros((count, 128), single)
    pair = lcol_ref[...]
    for h in range(heads):
        delta = jnp.sum(both * head_row(width, h), axis=1, keepdims=True)
        dcol = jnp.where(lane == h, delta, dcol)
        pair = jnp.where(lane == heads + h, delta, pair)
    dcol_ref[...] = dcol
    rows = jnp.transpose(pair)[:8, :]
    first = rows.astype(low).astype(single)
    rest = rows - first
    second = rest.astype(low).astype(single)
    third = rest - second
    tail = jnp.concatenate([first, second, third, jnp.zeros_like(first)], axis=0)
    msg_ref[count:, :] = tail.astype(low)


def query_body(parts_n, ids_ref, own_ref, msg_ref, lcol_ref, dcol_ref, segc_ref, segr_ref, *refs):
    parts = refs[:parts_n]
    dq_ref, acc_ref = refs[parts_n:]
    count = own_ref.shape[0]
    width = dq_ref.shape[1]
    lane = lax.broadcasted_iota(jnp.int32, (1, 128), 1)
    dq_ref[...] = jnp.zeros_like(dq_ref)

    def head(h, carry):
        hm = head_row(width, h)
        q = own_ref[:, :width] * (hm * scale).astype(low)
        do = msg_ref[:count, :] * hm.astype(low)
        lse = jnp.sum(jnp.where(lane == h, lcol_ref[...], 0.0), axis=1, keepdims=True)
        delta = jnp.sum(jnp.where(lane == h, dcol_ref[...], 0.0), axis=1, keepdims=True)
        acc_ref[...] = jnp.zeros_like(acc_ref)

        def step(j, at, start):
            k = parts[at][pl.ds(start, count), width : 2 * width]
            v = parts[at][pl.ds(start, count), 2 * width : 3 * width]
            s = jnp.where(segc_ref[...] == segr_ref[pl.ds(j, 1), :], nt(q, k) - lse, negative)
            ds = (jnp.exp(s) * (nt(do, v) - delta)).astype(low)
            acc_ref[...] = acc_ref[...] + nn(ds, k)

        each_chunk(parts, count, step)
        dq_ref[...] = dq_ref[...] + acc_ref[...] * (hm * scale)
        return carry

    lax.fori_loop(0, width // HEAD_DIM, head, 0)


def key_body(
    parts_n, ids_ref, own_ref, segc_ref, segr_ref, dq_ref, cos_ref, sin_ref, up_ref, picked_ref, w0, w1, w2, w3, *refs
):
    parts = refs[:parts_n]
    msgs = refs[parts_n : 2 * parts_n]
    m0, m1, m2, m3, gp_ref, paq_ref, stat_ref, dk_ref, dv_ref, kacc_ref, vacc_ref, wide_ref = refs[2 * parts_n :]
    count = own_ref.shape[0]
    width = dq_ref.shape[1]
    heads = width // HEAD_DIM
    tail = 32
    dk_ref[...] = jnp.zeros_like(dk_ref)
    dv_ref[...] = jnp.zeros_like(dv_ref)

    def stats(j, at, start):
        e = msgs[at][pl.ds(start + count, tail), :].astype(single)
        stat_ref[j] = e[:8] + e[8:16] + e[16:24]

    each_chunk(msgs, count + tail, stats)

    def head(h, carry):
        hm = head_row(width, h)
        k = own_ref[:, width : 2 * width] * (hm * scale).astype(low)
        v = own_ref[:, 2 * width : 3 * width] * hm.astype(low)
        kacc_ref[...] = jnp.zeros_like(kacc_ref)
        vacc_ref[...] = jnp.zeros_like(vacc_ref)

        def step(j, at, start):
            q = parts[at][pl.ds(start, count), :width]
            mstart = start // count * (count + tail) if isinstance(start, int) else pl.multiple_of((start // count) * (count + tail), 16)
            do = msgs[at][pl.ds(mstart, count), :]
            lse = stat_ref[j, pl.ds(h, 1), :]
            delta = stat_ref[j, pl.ds(heads + h, 1), :]
            s = jnp.where(segc_ref[...] == segr_ref[pl.ds(j, 1), :], nt(k, q) - lse, negative)
            p = jnp.exp(s)
            vacc_ref[...] = vacc_ref[...] + nn(p.astype(low), do)
            ds = (p * (nt(v, do) - delta)).astype(low)
            kacc_ref[...] = kacc_ref[...] + nn(ds, q)

        each_chunk(parts, count, step)
        dk_ref[...] = dk_ref[...] + kacc_ref[...] * (hm * scale)
        dv_ref[...] = dv_ref[...] + vacc_ref[...] * hm
        return carry

    lax.fori_loop(0, heads, head, 0)
    cosine = cos_ref[...]
    sine = sin_ref[...]
    gq = (dq_ref[...] * cosine - swap_halves(dq_ref[...]) * sine).astype(low)
    gk = (dk_ref[...] * cosine - swap_halves(dk_ref[...]) * sine).astype(low)
    gv = dv_ref[...].astype(low)
    gp_ref[:, :width] = gq
    gp_ref[:, width : 2 * width] = gk
    gp_ref[:, 2 * width :] = gv
    part = w0.shape[1]
    full = wide_ref.shape[1] - up_ref.shape[1]
    for k, w_ref in enumerate([w0, w1, w2, w3]):
        wide_ref[:, cols_of(ids_ref, k, part)] = nt(gq, w_ref[0]) + nt(gk, w_ref[1]) + nt(gv, w_ref[2])
    adapt = nt(gq, up_ref[0]) + nt(gk, up_ref[1]) + nt(gv, up_ref[2])
    wide_ref[:, full:] = adapt
    paq_ref[...] = (adapt * picked_ref[...].astype(single)).astype(low)
    quarter = m0.shape[0]
    for k, m_ref in enumerate([m0, m1, m2, m3]):
        m_ref[...] = wide_ref[rows_of(ids_ref, k, quarter), :].astype(low)


def last_body(ids_ref, p0, p1, p2, p3, picked_ref, pdn_ref, tokens_ref, gain_ref, gm_ref, gt_ref):
    quarter = p0.shape[0]
    width = gm_ref.shape[1]
    rows = rows_of(ids_ref, 0, quarter)
    picked = picked_ref[rows, :].astype(single)
    total = p0[...].astype(single) + p1[...].astype(single) + p2[...].astype(single) + p3[...].astype(single)
    gaq = (total[:, width:].astype(low).astype(single) * picked).astype(low)
    upstream = total[:, :width] + nn(gaq, pdn_ref[...])
    xhat, rstd = layer_norm_rows(tokens_ref[rows, :].astype(single))
    gt_ref[...] = (gm_ref[...] + layer_norm_back(upstream, gain_ref[...], xhat, rstd)).astype(low)


def assemble_body(ids_ref, p0, p1, p2, p3, out_ref):
    quarter = p0.shape[0]
    width = out_ref.shape[1]
    for k, p_ref in enumerate([p0, p1, p2, p3]):
        out_ref[rows_of(ids_ref, k, quarter), :] = p_ref[:, :width]


def padded(size):
    return -(-size // 128) * 128


def grads_body(
    ids_ref, f0, f1, f2, f3, n2_ref, a0, a1, a2, a3, go_ref, ao_ref, gb_ref, paq_ref, n1_ref, gao_ref, heads_ref,
    ai_ref, gg_ref, gad_ref, act_ref, aq_ref, gp_ref, keep_ref, send_ref, gai_ref, ad_ref, all_ref,
):
    quarter = gb_ref.shape[0]
    ranks = gai_ref.shape[1]
    width = gb_ref.shape[1]
    part = width // 4
    hidden = act_ref.shape[1]
    for k, (f_ref, a_ref) in enumerate([(f0, a0), (f1, a1), (f2, a2), (f3, a3)]):
        gai_ref[rows_of(ids_ref, k, quarter), :] = f_ref[:, width + ranks :]
        ad_ref[rows_of(ids_ref, k, quarter), :] = a_ref[:, width:]
    mine = pl.ds(pl.multiple_of(ids_ref[2] * part, 128), part)
    at = 0

    def put(value):
        nonlocal at
        size = value.shape[1]
        all_ref[:, at : at + size] = value
        if padded(size) != size:
            all_ref[:, at + size : at + padded(size)] = jnp.zeros((ranks, padded(size) - size), single)
        at += padded(size)

    put(tn(gai_ref[...], n2_ref[:, mine]))
    put(tn(ad_ref[...], go_ref[:, mine]))
    put(tn(ao_ref[rows_of(ids_ref, 0, quarter), :], gb_ref[...]))
    put(tn(paq_ref[...], n1_ref[...]))
    put(tn(gao_ref[...], heads_ref[...]))
    put(tn(aq_ref[...], gp_ref[...]))
    put(tn(ai_ref[...], gg_ref[0]))
    put(tn(ai_ref[...], gg_ref[1]))
    put(tn(gad_ref[...], act_ref[...]))
    half = ranks // 2
    keep_ref[...] = all_ref[pl.ds(pl.multiple_of(ids_ref[3] * half, 16), half), :].astype(low)
    send_ref[...] = all_ref[pl.ds(pl.multiple_of((1 - ids_ref[3]) * half, 16), half), :].astype(low)


def fold_body(ids_ref, keep_ref, got_ref, r0, r1, r2, r3, sum_ref):
    sum_ref[...] = keep_ref[...].astype(single) + got_ref[...].astype(single)
    size = r0.shape[0]
    for k, r_ref in enumerate([r0, r1, r2, r3]):
        r_ref[...] = sum_ref[pl.ds(pl.multiple_of((ids_ref[4] ^ k) * size, 16), size), :].astype(low)


def total_body(shared, ids_ref, p0, p1, p2, p3, z_ref, r_ref):
    total = p0[...].astype(single) + p1[...].astype(single) + p2[...].astype(single) + p3[...].astype(single)
    z_ref[...] = total[:, :shared].astype(low)
    r_ref[...] = total[:, shared:].astype(low)


def tensor_body(ids_ref, p0, p1, p2, p3, r_ref, out_ref):
    part = p0.shape[1] // 10
    width = 4 * part
    for k, p_ref in enumerate([p0, p1, p2, p3]):
        start = pl.multiple_of((ids_ref[2] ^ k) * part, 128)
        out_ref[:, pl.ds(start, part)] = p_ref[:, :part]
        out_ref[:, pl.ds(pl.multiple_of(start + width, 128), part)] = p_ref[:, part : 2 * part]
    total = p0[:, 2 * part :].astype(single)
    for p_ref in (p1, p2, p3):
        total = total + p_ref[:, 2 * part :].astype(single)
    out_ref[:, 2 * width : 4 * width] = total.astype(low)
    out_ref[:, 4 * width :] = r_ref[...]


def finish_body(ids_ref, *refs):
    pieces = refs[:8]
    outs = refs[8:]
    size = pieces[0].shape[0]
    for at, p_ref in enumerate(pieces):
        core = ids_ref[3] ^ (at // 4)
        start = pl.multiple_of(core * (4 * size) + (ids_ref[4] ^ (at % 4)) * size, 16)
        col = 0
        for out_ref in outs:
            span = out_ref.shape[1]
            out_ref[pl.ds(start, size), :] = p_ref[:, col : col + span].astype(single)
            col += padded(span)


def on_device(
    tokens,
    grad_out,
    lengths,
    deal,
    adapter_of,
    attention_gain,
    attention_proj,
    attention_out,
    feed_gain,
    feed_in,
    feed_out,
    attention_proj_down,
    attention_proj_up,
    attention_out_down,
    attention_out_up,
    feed_in_down,
    feed_in_up,
    feed_out_down,
    feed_out_up,
):
    fsdp_size = lax.axis_size("fsdp")
    context_size = lax.axis_size("context")
    tensor_size = lax.axis_size("tensor")
    count, width = tokens.shape
    total = deal.shape[0]
    sets, _, rank = attention_proj_down.shape
    ranks = sets * rank
    local_width = attention_proj.shape[2]
    hidden = feed_in.shape[2]
    f = lax.axis_index("fsdp")
    c = lax.axis_index("context")
    t = lax.axis_index("tensor")
    small = context_size == 2 and fsdp_size == 4
    half_at = c % 2
    chip = (f // 2) * 2 + half_at
    ids = jnp.stack([f, half_at, t, f % 2, chip]).astype(jnp.int32)
    quarter = count // tensor_size

    def over(axis, size, bit, value):
        return lax.ppermute(value, axis, swap_pairs(axis, size, bit))

    def near(value):
        return over("fsdp", fsdp_size, 1, value)

    def ahead(value):
        return over("fsdp", fsdp_size, 2, value)

    def across(value):
        return over("context", context_size, 1, value)

    def after(value, *others):
        return lax.optimization_barrier((value, *others))[0]

    def exchange(pieces):
        return [pieces[0]] + [over("tensor", tensor_size, k, pieces[k]) for k in range(1, tensor_size)]

    def spread(piece):
        return [piece] + [over("tensor", tensor_size, k, piece) for k in range(1, tensor_size)]

    proj_own = jnp.transpose(attention_proj, (1, 0, 2))
    in_own = jnp.transpose(feed_in, (1, 2, 0))
    proj_down = jnp.transpose(attention_proj_down, (0, 2, 1)).reshape(ranks, width)
    out_down_own = jnp.transpose(attention_out_down, (0, 2, 1)).reshape(ranks, local_width)
    in_down = jnp.transpose(feed_in_down, (0, 2, 1)).reshape(ranks, width)
    last_down = jnp.transpose(feed_out_down, (0, 2, 1)).reshape(ranks, hidden)
    proj_up = jnp.transpose(attention_proj_up, (2, 0, 1, 3)).reshape(3, ranks, local_width)
    out_up = attention_out_up.reshape(ranks, width)
    in_up = jnp.transpose(feed_in_up, (2, 0, 1, 3)).reshape(2, ranks, hidden)
    last_up = feed_out_up.reshape(ranks, width)

    proj_far = ahead(proj_own)
    proj_near = near(proj_own)

    seqs = lengths.shape[0]
    before = jnp.arange(seqs)[:, None] >= jnp.arange(seqs)[None, :]
    ends = jnp.sum(jnp.where(before, lengths[None, :], 0), axis=1)
    starts = ends - lengths
    segment_all = jnp.sum((deal[:, None] >= ends[None, :]).astype(jnp.int32), axis=1)
    first = (f * context_size + c) * count
    segment_rows = lax.dynamic_slice_in_dim(segment_all, first, count)
    deal_rows = lax.dynamic_slice_in_dim(deal, first, count)
    member = segment_rows[:, None] == jnp.arange(seqs, dtype=jnp.int32)[None, :]
    place = deal_rows - jnp.sum(jnp.where(member, starts[None, :], 0), axis=1)
    chosen = jnp.sum(jnp.where(member, adapter_of[None, :], 0), axis=1)
    set_of = jnp.arange(ranks, dtype=jnp.int32) // rank
    picked = (chosen[:, None] == set_of[None, :]).astype(low)
    half = HEAD_DIM // 2
    lane = jnp.arange(local_width, dtype=jnp.int32) % HEAD_DIM
    freq = jnp.exp((lane % half).astype(single) * (-math.log(rope_base) / half))
    angle = place.astype(single)[:, None] * freq[None, :]
    cos_full = jnp.cos(angle)
    sin_full = jnp.sin(angle) * jnp.where(lane < half, -1.0, 1.0).astype(single)[None, :]
    gain_one = attention_gain.astype(single)[None, :]
    gain_two = feed_gain.astype(single)[None, :]
    xhat_one, _ = layer_norm_rows(tokens.astype(single))
    normed_one = (xhat_one * gain_one).astype(low)
    adapted_q = (picked.astype(single) * nt(normed_one, proj_down)).astype(low)

    packed = spread(after(jnp.concatenate([attention_out, out_down_own], axis=0), adapted_q))
    in_near = near(after(in_own, adapted_q))
    last_near = near(after(feed_out, adapted_q))
    proj_w = [proj_own, proj_near, proj_far, near(proj_far)]

    (qkv,) = call(
        project_body,
        [((count, 3 * local_width), low)],
        ids,
        [normed_one, adapted_q, proj_up, cos_full, sin_full, *proj_w],
        name="project",
    )
    groups = segment_all.reshape(-1, count)

    def plane_gather(value):
        if not small:
            return [lax.all_gather(value, token_axes, axis=0, tiled=True)]
        corner = lax.ppermute(value, token_axes, swap_pairs(None, fsdp_size * context_size, 2 * context_size + 1))
        chips = [value, across(value), ahead(value), corner]
        return chips + [near(piece) for piece in chips]

    if small:
        order = jnp.stack(
            [(f ^ df) * context_size + (c ^ dc) for df, dc in
             ((0, 0), (0, 1), (2, 0), (2, 1), (1, 0), (1, 1), (3, 0), (3, 1))]
        )
        seg_row = groups[order]
    else:
        seg_row = groups
    seg_col = segment_rows[:, None]

    qkv_all = plane_gather(qkv)
    parts_n = len(qkv_all)
    chunks = total // count
    gathered = qkv_all[1:4]

    out_w_own = jnp.concatenate([value[:local_width] for value in packed], axis=0)
    out_down = jnp.stack([value[local_width:] for value in packed])
    in_half = lax.dynamic_index_in_dim(in_own, half_at, 0)
    last_half = lax.dynamic_slice_in_dim(feed_out, half_at * (feed_out.shape[1] // 2), feed_out.shape[1] // 2, 1)
    out_half = lax.dynamic_slice_in_dim(out_w_own, half_at * (width // 2), width // 2, 0)
    out_far = ahead(after(out_half, *gathered))
    in_far = ahead(after(in_half, *gathered))
    last_far = ahead(after(last_half, *gathered))

    square = pltpu.VMEM((count, count), single)
    slab = pltpu.VMEM((count, local_width), single)
    heads_out, attended, lse_col = call(
        lambda *refs: attend_body(parts_n, *refs),
        [((count, local_width), low), ((count, local_width), single), ((count, 128), single)],
        ids,
        [qkv, seg_col, seg_row, *qkv_all],
        scratch=[pltpu.VMEM((chunks, count, count), single), square, square, slab],
        vmem=60,
        name="attend",
    )
    heads = spread(heads_out)

    def halves(own, near_own, far):
        far = after(far, heads_out)
        rest = across(far)
        return [own, near_own, far, rest, near(far), near(rest)]

    out_w = halves(out_w_own, near(after(out_w_own, *gathered)), out_far)
    in_w = halves(in_own, in_near, in_far)
    last_w = halves(feed_out, last_near, last_far)
    wide = width + ranks
    piece = ((quarter, wide), low)
    full_out = [pltpu.VMEM((width, local_width), low)] * 2
    full_last = [pltpu.VMEM(feed_out.shape, low)] * 2
    mid_outs = call(
        middle_body,
        [piece] * 4
        + [((count, ranks), low)] * 3
        + [
            ((count, width), low),
            ((count, hidden), low),
            ((2, count, hidden), low),
            ((quarter, width), single),
        ],
        ids,
        [*heads, *out_w, out_down, out_up, tokens, gain_two, grad_out, picked, *in_w, in_down, in_up, *last_w,
         last_down, last_up],
        scratch=[pltpu.VMEM((count, wide), single), *full_out, *[pltpu.VMEM(in_own.shape, low)] * 2, *full_last],
        vmem=56,
        name="middle",
    )
    pieces = mid_outs[:4]
    adapted_o, adapted_i, grad_adapt_d, normed_two, activity, grad_gates, middle_q = mid_outs[4:]
    summed = exchange(pieces)
    turn = ((quarter, local_width + ranks), low)
    *turned, grad_mid, grad_branch, grad_adapt_i = call(
        turn_body,
        [turn] * 4 + [((quarter, width), single), ((quarter, width), low), ((quarter, ranks), low)],
        ids,
        [*summed, picked, in_down, middle_q, gain_two, grad_out, out_up, *out_w, out_down],
        scratch=full_out,
        name="turn",
    )
    arrived = exchange(turned)
    tail = 32
    message, delta_col, grad_adapt_o = call(
        collect_body,
        [((count + tail, local_width), low), ((count, 128), single), ((count, ranks), low)],
        ids,
        [*arrived, attended, lse_col],
        name="collect",
    )
    message_all = plane_gather(message)
    feed_piece = ((quarter, wide + ranks), low)
    feed_pieces = call(
        feed_body,
        [feed_piece] * 4,
        ids,
        [after(activity, message), last_down, grad_adapt_i, *last_w],
        scratch=[pltpu.VMEM((count, wide), single), *full_last],
        name="feed",
    )
    feed_summed = exchange(feed_pieces)
    (grad_query,) = call(
        lambda *refs: query_body(parts_n, *refs),
        [((count, local_width), single)],
        ids,
        [after(qkv, *feed_pieces), message, lse_col, delta_col, seg_col, seg_row, *qkv_all],
        scratch=[slab],
        vmem=60,
        name="queries",
    )
    (output_q,) = call(
        out_body,
        [((quarter, wide), low)],
        ids,
        [*feed_summed, picked, middle_q, last_up],
        name="outputs",
    )
    output_all = spread(output_q)
    *last_pieces, grad_proj, part_adapt_q = call(
        lambda *refs: key_body(parts_n, *refs),
        [piece] * 4 + [((count, 3 * local_width), low), ((count, ranks), low)],
        ids,
        [after(qkv, output_q), seg_col, seg_row, grad_query, cos_full, sin_full, proj_up, picked, *proj_w, *qkv_all,
         *message_all],
        scratch=[pltpu.VMEM((chunks, 8, count), single), slab, slab, slab, slab, pltpu.VMEM((count, wide), single)],
        vmem=60,
        name="keys",
    )
    last_summed = exchange(last_pieces)
    own_sizes = [width // tensor_size] * 2 + [width] * 2
    rest_sizes = [local_width, 3 * local_width] + [padded(hidden)] * 3
    columns = sum(own_sizes) + sum(rest_sizes)
    keep, send = call(
        grads_body,
        [((ranks // 2, columns), low)] * 2,
        ids,
        [*feed_summed, normed_two, *output_all, grad_out, adapted_o, grad_branch, part_adapt_q, normed_one,
         grad_adapt_o, heads_out, adapted_i, grad_gates, grad_adapt_d, activity, adapted_q, grad_proj],
        scratch=[pltpu.VMEM((count, ranks), low)] * 2 + [pltpu.VMEM((ranks, columns), single)],
        name="grads",
    )
    (grad_tokens_q,) = call(
        last_body,
        [((quarter, width), low)],
        ids,
        [*last_summed, picked, proj_down, tokens, gain_one, grad_mid],
        name="last",
    )
    tokens_all = spread(grad_tokens_q)
    (output,) = call(assemble_body, [((count, width), low)], ids, output_all, name="join_output")
    (grad_tokens,) = call(assemble_body, [((count, width), low)], ids, tokens_all, name="join_tokens")

    joint = 4 * width + sum(rest_sizes)
    finals = [((ranks, width), single)] * 4 + [((ranks, local_width), single), ((ranks, 3 * local_width), single)]
    finals = finals + [((ranks, hidden), single)] * 3
    if small:
        rows = ranks // 8
        strip = ((rows, columns), low)
        strips = call(
            fold_body,
            [strip] * 4,
            ids,
            [keep, near(send)],
            scratch=[pltpu.VMEM((ranks // 2, columns), single)],
            name="fold",
        )
        corner = lax.ppermute(strips[3], token_axes, swap_pairs(None, fsdp_size * context_size, 2 * context_size + 1))
        strips = [strips[0], across(strips[1]), ahead(strips[2]), corner]
        shared, rest = call(
            lambda *refs: total_body(sum(own_sizes), *refs),
            [((rows, sum(own_sizes)), low), ((rows, sum(rest_sizes)), low)],
            ids,
            strips,
            name="total",
        )
        (joined,) = call(
            tensor_body, [((rows, joint), low)], ids, [*spread(shared), rest], name="tensor_sum"
        )
        joined = plane_gather(joined)
        results = call(finish_body, finals, ids, joined, name="finish")
    else:
        pair = jnp.where(f % 2 == 0, jnp.concatenate([keep, send]), jnp.concatenate([send, keep]))
        pair = lax.psum(pair, token_axes)
        (joined,) = call(
            tensor_body,
            [((ranks, joint), low)],
            ids,
            [*spread(pair[:, : sum(own_sizes)]), pair[:, sum(own_sizes) :]],
            name="tensor_sum",
        )
        results = []
        col = 0
        for (_, span), _ in finals:
            results.append(joined[:, col : col + span].astype(single))
            col += padded(span)

    in_down_grad, last_up_grad, out_up_grad, proj_down_grad, out_down_grad, proj_up_grad, gate_up, mult_up, last_grad = results

    def down(grad):
        return jnp.transpose(grad.reshape(sets, rank, -1), (0, 2, 1))

    return (
        output,
        grad_tokens,
        down(proj_down_grad),
        proj_up_grad.reshape(sets, rank, 3, local_width),
        down(out_down_grad),
        out_up_grad.reshape(sets, rank, width),
        down(in_down_grad),
        jnp.stack([gate_up, mult_up], axis=1).reshape(sets, rank, 2, hidden),
        down(last_grad),
        last_up_grad.reshape(sets, rank, width),
    )


def solution(mesh):
    return jax.shard_map(
        on_device,
        mesh=mesh,
        in_specs=(
            P(("fsdp", "context"), None),
            P(("fsdp", "context"), None),
            P(),
            P(),
            P(),
            P(),
            P("fsdp", None, "tensor"),
            P("tensor", "fsdp"),
            P(),
            P("fsdp", None, "tensor"),
            P("tensor", "fsdp"),
            P(),
            P(None, None, None, "tensor"),
            P(None, "tensor", None),
            P(),
            P(),
            P(None, None, None, "tensor"),
            P(None, "tensor", None),
            P(),
        ),
        out_specs=(
            P(("fsdp", "context"), None),
            P(("fsdp", "context"), None),
            P(),
            P(None, None, None, "tensor"),
            P(None, "tensor", None),
            P(),
            P(),
            P(None, None, None, "tensor"),
            P(None, "tensor", None),
            P(),
        ),
        check_vma=False,
    )
```

```python
import math

import jax
import jax.numpy as jnp
from jax import lax
from jax.experimental import pallas as pl
from jax.experimental.pallas import tpu as pltpu
from jax.sharding import PartitionSpec as P

HEAD_DIM = 64


rope_base = 160000.0
epsilon = 1e-05
negative = -1e30
single = jnp.float32
low = jnp.bfloat16
scale = HEAD_DIM ** (-0.5)
token_axes = ("fsdp", "context")
every_axis = ("fsdp", "context", "tensor")


def nn(left, right):
    return lax.dot_general(
        left, right, (((1,), (0,)), ((), ())), preferred_element_type=jnp.float32
    )


def nt(left, right):
    return lax.dot_general(
        left, right, (((1,), (1,)), ((), ())), preferred_element_type=jnp.float32
    )


def tn(left, right):
    return lax.dot_general(
        left, right, (((0,), (0,)), ((), ())), preferred_element_type=jnp.float32
    )


def call(body, outs, ids, args, scratch=(), vmem=6, name=None, far=(), cost=0.0):
    whole = pl.BlockSpec(memory_space=pltpu.VMEM)
    return pl.pallas_call(
        body,
        out_shape=[jax.ShapeDtypeStruct(shape, kind) for shape, kind in outs],
        in_specs=[pl.BlockSpec(memory_space=pltpu.SMEM)]
        + [pl.BlockSpec(memory_space=pltpu.HBM) if at in far else whole for at in range(len(args))],
        out_specs=[whole] * len(outs),
        scratch_shapes=list(scratch),
        compiler_params=pltpu.CompilerParams(vmem_limit_bytes=vmem << 20),
        cost_estimate=pl.CostEstimate(flops=int(cost * 1e12) + 1, bytes_accessed=int(cost * 1e12) + 1, transcendentals=0),
        name=name,
    )(ids, *args)


def swap_pairs(axis, size, bit):
    return [(i, i ^ bit) for i in range(size)]


def layer_norm_rows(values):
    centered = values - jnp.mean(values, axis=1, keepdims=True)
    rstd = lax.rsqrt(jnp.mean(centered * centered, axis=1, keepdims=True) + epsilon)
    return (centered * rstd, rstd)


def layer_norm_back(upstream, gain, xhat, rstd):
    scaled = upstream * gain
    return rstd * (
        scaled
        - jnp.mean(scaled, axis=1, keepdims=True)
        - xhat * jnp.mean(scaled * xhat, axis=1, keepdims=True)
    )


def swap_halves(u):
    width = u.shape[1]
    half = HEAD_DIM // 2
    lane = lax.broadcasted_iota(jnp.int32, (1, width), 1)
    return jnp.where(
        lane % HEAD_DIM < half, pltpu.roll(u, width - half, 1), pltpu.roll(u, half, 1)
    )


def head_row(width, head):
    lane = lax.broadcasted_iota(jnp.int32, (1, width), 1)
    return (lane // HEAD_DIM == head).astype(single)


def each_chunk(parts, stride, step):
    base = 0
    for at, part in enumerate(parts):
        groups = part.shape[0] // stride
        if groups == 1:
            step(base, at, 0)
        else:

            def inner(j, carry, base=base, at=at):
                step(base + j, at, pl.multiple_of(j * stride, 16))
                return carry

            lax.fori_loop(0, groups, inner, 0)
        base += groups


def cols_of(ids_ref, k, width):
    return pl.ds(pl.multiple_of((ids_ref[0] ^ k) * width, 128), width)


def rows_of(ids_ref, k, height):
    return pl.ds(pl.multiple_of((ids_ref[2] ^ k) * height, 16), height)


def join_rows(ids_ref, dst_ref, mine_ref, other_ref):
    size = mine_ref.shape[0]
    dst_ref[pl.ds(ids_ref[1] * size, size)] = mine_ref[...]
    dst_ref[pl.ds((1 - ids_ref[1]) * size, size)] = other_ref[...]


def join_cols(ids_ref, dst_ref, mine_ref, other_ref):
    size = mine_ref.shape[1]
    dst_ref[:, pl.ds(pl.multiple_of(ids_ref[1] * size, 128), size)] = mine_ref[...]
    dst_ref[:, pl.ds(pl.multiple_of((1 - ids_ref[1]) * size, 128), size)] = other_ref[...]


def project_body(ids_ref, x_ref, aq_ref, up_ref, cos_ref, sin_ref, *refs):
    weights, q_ref, kv_ref = (refs[:-2], refs[-2], refs[-1])
    part = weights[0].shape[1]
    width = weights[0].shape[2]
    for j in range(3):
        acc = nn(aq_ref[...], up_ref[j])
        for k, w_ref in enumerate(weights):
            acc = acc + nn(x_ref[:, cols_of(ids_ref, k, part)], w_ref[j])
        if j < 2:
            acc = acc * cos_ref[...] + swap_halves(acc) * sin_ref[...]
        if j == 0:
            q_ref[...] = acc.astype(low)
        else:
            kv_ref[:, (j - 1) * width : j * width] = acc.astype(low)


def prepare_body(ids_ref, tokens_ref, gain_ref, down_ref, picked_ref, n1_ref, aq_ref):
    xhat, _ = layer_norm_rows(tokens_ref[...].astype(single))
    normed = (xhat * gain_ref[...]).astype(low)
    n1_ref[...] = normed
    aq_ref[...] = (picked_ref[...].astype(single) * nt(normed, down_ref[...])).astype(low)


def split_body(ids_ref, in_ref, last_ref, ihalf_ref, lhalf_ref):
    ihalf_ref[...] = in_ref[pl.ds(ids_ref[1], 1)]
    cols = lhalf_ref.shape[1]
    lhalf_ref[...] = last_ref[:, pl.ds(pl.multiple_of(ids_ref[1] * cols, 128), cols)]


def stack_body(ids_ref, p0, p1, p2, p3, full_ref, half_ref):
    rows = p0.shape[1]
    for k, p_ref in enumerate([p0, p1, p2, p3]):
        full_ref[k * rows : (k + 1) * rows, :] = p_ref[:rows, :]
    size = half_ref.shape[0]
    half_ref[...] = full_ref[pl.ds(pl.multiple_of(ids_ref[1] * size, 16), size), :]


def put_pieces(ids_ref, wide_ref, keep_ref, send_ref):
    quarter = keep_ref.shape[1]
    for at, (ref, k) in enumerate([(keep_ref, 0), (keep_ref, 2), (send_ref, 1), (send_ref, 3)]):
        ref[at % 2] = wide_ref[rows_of(ids_ref, k, quarter), :].astype(low)


def pair_body(ids_ref, keep_ref, got_ref, mine_ref, pass_ref):
    mine_ref[...] = keep_ref[0].astype(single) + got_ref[0].astype(single)
    pass_ref[...] = (keep_ref[1].astype(single) + got_ref[1].astype(single)).astype(low)


def attend_body(parts_n, ids_ref, q_ref, segc_ref, segr_ref, *refs):
    far_parts = refs[:parts_n]
    heads_ref, att_ref, lcol_ref, s_ref, m_ref, l_ref, o_ref = refs[parts_n : parts_n + 7]
    parts = refs[parts_n + 7 : -1]
    sems = refs[-1]
    copies = [pltpu.make_async_copy(src, dst, sems.at[n]) for n, (src, dst) in enumerate(zip(far_parts, parts))]
    for copy in copies:
        copy.start()
    for copy in copies:
        copy.wait()
    count = q_ref.shape[0]
    width = att_ref.shape[1]
    lane = lax.broadcasted_iota(jnp.int32, (1, 128), 1)
    lcol_ref[...] = jnp.zeros_like(lcol_ref)
    att_ref[...] = jnp.zeros_like(att_ref)

    def head(h, carry):
        hm = head_row(width, h)
        q = q_ref[...] * (hm * scale).astype(low)
        m_ref[...] = jnp.full_like(m_ref, negative)
        l_ref[...] = jnp.zeros_like(l_ref)
        o_ref[...] = jnp.zeros_like(o_ref)

        def scores(j, at, start):
            s = nt(q, parts[at][pl.ds(start, count), :width])
            s = jnp.where(segc_ref[...] == segr_ref[pl.ds(ids_ref[5 + j], 1), :], s, negative)
            s_ref[j] = s
            m_ref[...] = jnp.maximum(m_ref[...], s)

        each_chunk(parts, count, scores)
        top = jnp.max(m_ref[...], axis=1, keepdims=True)

        def weigh(j, at, start):
            p = jnp.exp(s_ref[j] - top)
            l_ref[...] = l_ref[...] + p
            o_ref[...] = o_ref[...] + nn(
                p.astype(low), parts[at][pl.ds(start, count), width:]
            )

        each_chunk(parts, count, weigh)
        mass = jnp.sum(l_ref[...], axis=1, keepdims=True)
        att_ref[...] = att_ref[...] + o_ref[...] * (hm / mass)
        lcol_ref[...] = jnp.where(lane == h, top + jnp.log(mass), lcol_ref[...])
        return carry

    lax.fori_loop(0, width // HEAD_DIM, head, 0)
    heads_ref[...] = att_ref[...].astype(low)


def middle_body(ids_ref, *refs):
    heads = refs[0:4]
    wown, wnear, wa, wb, wc, wd = refs[4:10]
    packs = refs[10:14]
    refs = refs[3:]
    ou_ref, tokens_ref, gain_ref, go_ref, picked_ref = refs[11:16]
    iown, inear, ia, ib, ic, idd = refs[16:22]
    idn_ref, iu_ref = refs[22:24]
    lown, lnear, la, lb, lc, ld = refs[24:30]
    ldn_ref, lup_ref = refs[30:32]
    keep_ref, send_ref, ao_ref, ai_ref, gad_ref, n2_ref, act_ref, gg_ref, mid_ref, wts, lts = refs[32:43]
    wide_ref, its, sems = refs[43:]
    mine, rest = (ids_ref[1], 1 - ids_ref[1])
    half = wa.shape[0]
    step = la.shape[1]

    def rows(k, at):
        return wts.at[k, pl.ds(pl.multiple_of(at * half, 16), half), :]

    def cols(k, at):
        return lts.at[k, :, pl.ds(pl.multiple_of(at * step, 128), step)]

    pairs = [
        (wown, wts.at[0]),
        (wnear, wts.at[1]),
        (wa, rows(2, mine)),
        (wb, rows(2, rest)),
        (wc, rows(3, mine)),
        (wd, rows(3, rest)),
        (iown, its.at[0]),
        (inear, its.at[1]),
        (ia, its.at[2, pl.ds(mine, 1)]),
        (ib, its.at[2, pl.ds(rest, 1)]),
        (ic, its.at[3, pl.ds(mine, 1)]),
        (idd, its.at[3, pl.ds(rest, 1)]),
        (lown, lts.at[0]),
        (lnear, lts.at[1]),
        (la, cols(2, mine)),
        (lb, cols(2, rest)),
        (lc, cols(3, mine)),
        (ld, cols(3, rest)),
    ]
    copies = [pltpu.make_async_copy(src, dst, sems.at[n]) for n, (src, dst) in enumerate(pairs)]
    for copy in copies:
        copy.start()
    h0 = heads[0]
    w0 = wown
    outs_w = [wts.at[k] for k in range(4)]
    ins_w = [its.at[k] for k in range(4)]
    lasts_w = [lts.at[k] for k in range(4)]
    part = w0.shape[1]
    span = h0.shape[1]
    width = tokens_ref.shape[1]
    picked = picked_ref[...].astype(single)
    span = h0.shape[1]
    adapt = nt(h0[...], packs[0][span:, :])
    for k in range(1, len(heads)):
        adapt = adapt + nt(heads[k][...], packs[k][span:, :])
    ao = (picked * adapt).astype(low)
    ao_ref[...] = ao
    for copy in copies[:6]:
        copy.wait()
    for k, w_ref in enumerate(outs_w):
        acc = nn(h0[...], w_ref[:span, :])
        for r in range(1, len(heads)):
            acc = acc + nn(heads[r][...], w_ref[r * span : (r + 1) * span, :])
        wide_ref[:, cols_of(ids_ref, k, part)] = acc
    middle = tokens_ref[...].astype(single) + wide_ref[:, :width] + nn(ao, ou_ref[...])
    wide_ref[:, :width] = middle
    quarter = mid_ref.shape[0]
    mid_ref[...] = wide_ref[rows_of(ids_ref, 0, quarter), :width]
    xhat, _ = layer_norm_rows(middle)
    n2 = (xhat * gain_ref[...]).astype(low)
    n2_ref[...] = n2
    ai = (picked * nt(n2, idn_ref[...])).astype(low)
    ai_ref[...] = ai
    for copy in copies[6:12]:
        copy.wait()
    gate = nn(ai, iu_ref[0])
    mult = nn(ai, iu_ref[1])
    for k, w_ref in enumerate(ins_w):
        x = n2_ref[:, cols_of(ids_ref, k, part)]
        gate = gate + nt(x, w_ref[0])
        mult = mult + nt(x, w_ref[1])
    phi = 0.5 * (1.0 + lax.erf(gate * (2.0**-0.5)))
    gated = gate * phi
    act_ref[...] = (gated * mult).astype(low)
    slope = phi + gate * jnp.exp(-0.5 * gate * gate) * (1.0 / math.sqrt(2.0 * math.pi))
    go = go_ref[...]
    gad = (nt(go, lup_ref[...]).astype(low).astype(single) * picked).astype(low)
    gad_ref[...] = gad
    for copy in copies[12:]:
        copy.wait()
    ga = nn(gad, ldn_ref[...])
    for k, w_ref in enumerate(lasts_w):
        ga = ga + nt(go_ref[:, cols_of(ids_ref, k, part)], w_ref[...])
    gg0 = (slope * (ga * mult)).astype(low)
    gg1 = (ga * gated).astype(low)
    gg_ref[0] = gg0
    gg_ref[1] = gg1
    for k, w_ref in enumerate(ins_w):
        wide_ref[:, cols_of(ids_ref, k, part)] = nn(gg0, w_ref[0]) + nn(gg1, w_ref[1])
    wide_ref[:, width:] = nt(gg0, iu_ref[0]) + nt(gg1, iu_ref[1])
    put_pieces(ids_ref, wide_ref, keep_ref, send_ref)


def feed_body(ids_ref, act_ref, ldn_ref, lts, keep_ref, send_ref, wide_ref):
    part = lts.shape[2]
    act = act_ref[...]
    wide_ref[:, wide_ref.shape[1] - ldn_ref.shape[0] :] = nt(act, ldn_ref[...])
    for k in range(4):
        wide_ref[:, cols_of(ids_ref, k, part)] = nn(act, lts[k])
    put_pieces(ids_ref, wide_ref, keep_ref, send_ref)


def turn_body(
    ids_ref, p0, p1, picked_ref, idn_ref, mid_ref, gain_ref, go_ref, ou_ref, wts, d0, d1, d2, d3,
    a0, a1, a2, a3, gm_ref, gb_ref, gai_ref,
):
    quarter = p0.shape[0]
    width = mid_ref.shape[1]
    part = wts.shape[2]
    rows = rows_of(ids_ref, 0, quarter)
    picked = picked_ref[rows, :].astype(single)
    total = p0[...] + p1[...].astype(single)
    gai = (total[:, width:].astype(low).astype(single) * picked).astype(low)
    gai_ref[...] = gai
    upstream = total[:, :width] + nn(gai, idn_ref[...])
    xhat, rstd = layer_norm_rows(mid_ref[...])
    gm = go_ref[rows, :].astype(single) + layer_norm_back(upstream, gain_ref[...], xhat, rstd)
    gm_ref[...] = gm
    gb = gm.astype(low)
    gb_ref[...] = gb
    gao = (nt(gb, ou_ref[...]).astype(low).astype(single) * picked).astype(low)
    span = d0.shape[1]
    grads = [nn(gao, d_ref[span:, :]) for d_ref in (d0, d1, d2, d3)]
    for k in range(4):
        w_ref = wts.at[k]
        x = gb_ref[:, cols_of(ids_ref, k, part)]
        for r in range(4):
            grads[r] = grads[r] + nt(x, w_ref[r * span : (r + 1) * span, :])
    for k, a_ref in enumerate([a0, a1, a2, a3]):
        a_ref[:, :span] = grads[k].astype(low)
        a_ref[:, span:] = gao


def out_body(ids_ref, p0, p1, picked_ref, mid_ref, lup_ref, out_ref, ad_ref):
    width = mid_ref.shape[1]
    picked = picked_ref[rows_of(ids_ref, 0, p0.shape[0]), :].astype(single)
    total = p0[...] + p1[...].astype(single)
    ad = (picked * total[:, width:]).astype(low)
    ad_ref[...] = ad
    out_ref[...] = (mid_ref[...] + total[:, :width] + nn(ad, lup_ref[...])).astype(low)


def collect_body(ids_ref, a0, a1, a2, a3, att_ref, lcol_ref, msg_ref, dcol_ref, gao_ref):
    quarter = a0.shape[0]
    count, width = att_ref.shape
    for k, a_ref in enumerate([a0, a1, a2, a3]):
        msg_ref[rows_of(ids_ref, k, quarter), :] = a_ref[:, :width]
        gao_ref[rows_of(ids_ref, k, quarter), :] = a_ref[:, width:]
    both = msg_ref[:count, :].astype(single) * att_ref[...]
    heads = width // HEAD_DIM
    lane = lax.broadcasted_iota(jnp.int32, (1, 128), 1)
    dcol = jnp.zeros((count, 128), single)
    pair = lcol_ref[...]
    for h in range(heads):
        delta = jnp.sum(both * head_row(width, h), axis=1, keepdims=True)
        dcol = jnp.where(lane == h, delta, dcol)
        pair = jnp.where(lane == heads + h, delta, pair)
    dcol_ref[...] = dcol
    rows = jnp.transpose(pair)[:8, :]
    first = rows.astype(low).astype(single)
    rest = rows - first
    second = rest.astype(low).astype(single)
    third = rest - second
    tail = jnp.concatenate([first, second, third, jnp.zeros_like(first)], axis=0)
    msg_ref[count:, :] = tail.astype(low)


def query_body(parts_n, ids_ref, q_ref, msg_ref, lcol_ref, dcol_ref, segc_ref, segr_ref, *refs):
    parts = refs[:parts_n]
    dq_ref, acc_ref = refs[parts_n:]
    count = q_ref.shape[0]
    width = dq_ref.shape[1]
    lane = lax.broadcasted_iota(jnp.int32, (1, 128), 1)
    dq_ref[...] = jnp.zeros_like(dq_ref)

    def head(h, carry):
        hm = head_row(width, h)
        q = q_ref[...] * (hm * scale).astype(low)
        do = msg_ref[:count, :] * hm.astype(low)
        lse = jnp.sum(jnp.where(lane == h, lcol_ref[...], 0.0), axis=1, keepdims=True)
        delta = jnp.sum(jnp.where(lane == h, dcol_ref[...], 0.0), axis=1, keepdims=True)
        acc_ref[...] = jnp.zeros_like(acc_ref)

        def step(j, at, start):
            k = parts[at][pl.ds(start, count), :width]
            v = parts[at][pl.ds(start, count), width:]
            s = jnp.where(segc_ref[...] == segr_ref[pl.ds(ids_ref[5 + j], 1), :], nt(q, k) - lse, negative)
            ds = (jnp.exp(s) * (nt(do, v) - delta)).astype(low)
            acc_ref[...] = acc_ref[...] + nn(ds, k)

        each_chunk(parts, count, step)
        dq_ref[...] = dq_ref[...] + acc_ref[...] * (hm * scale)
        return carry

    lax.fori_loop(0, width // HEAD_DIM, head, 0)


def key_body(
    parts_n, ids_ref, own_ref, segc_ref, segr_ref, dq_ref, cos_ref, sin_ref, up_ref, picked_ref, w0, w1, w2, w3, *refs
):
    parts = refs[:parts_n]
    msgs = refs[parts_n : 2 * parts_n]
    keep_ref, send_ref, gp_ref, paq_ref, stat_ref, dk_ref, dv_ref, kacc_ref, vacc_ref, wide_ref = refs[
        2 * parts_n : 2 * parts_n + 10
    ]
    far_msgs = msgs
    msgs = refs[2 * parts_n + 10 : -1]
    sems = refs[-1]
    copies = [pltpu.make_async_copy(src, dst, sems.at[n]) for n, (src, dst) in enumerate(zip(far_msgs, msgs))]
    for copy in copies:
        copy.start()
    for copy in copies:
        copy.wait()
    count = own_ref.shape[0]
    width = dq_ref.shape[1]
    heads = width // HEAD_DIM
    tail = 32
    dk_ref[...] = jnp.zeros_like(dk_ref)
    dv_ref[...] = jnp.zeros_like(dv_ref)

    def stats(j, at, start):
        e = msgs[at][pl.ds(start + count, tail), :].astype(single)
        stat_ref[j] = e[:8] + e[8:16] + e[16:24]

    each_chunk(msgs, count + tail, stats)

    def head(h, carry):
        hm = head_row(width, h)
        k = own_ref[:, :width] * (hm * scale).astype(low)
        v = own_ref[:, width:] * hm.astype(low)
        kacc_ref[...] = jnp.zeros_like(kacc_ref)
        vacc_ref[...] = jnp.zeros_like(vacc_ref)

        def step(j, at, start):
            q = parts[at][pl.ds(start, count), :]
            mstart = start // count * (count + tail) if isinstance(start, int) else pl.multiple_of((start // count) * (count + tail), 16)
            do = msgs[at][pl.ds(mstart, count), :]
            lse = stat_ref[j, pl.ds(h, 1), :]
            delta = stat_ref[j, pl.ds(heads + h, 1), :]
            s = jnp.where(segc_ref[...] == segr_ref[pl.ds(ids_ref[5 + j], 1), :], nt(k, q) - lse, negative)
            p = jnp.exp(s)
            vacc_ref[...] = vacc_ref[...] + nn(p.astype(low), do)
            ds = (p * (nt(v, do) - delta)).astype(low)
            kacc_ref[...] = kacc_ref[...] + nn(ds, q)

        each_chunk(parts, count, step)
        dk_ref[...] = dk_ref[...] + kacc_ref[...] * (hm * scale)
        dv_ref[...] = dv_ref[...] + vacc_ref[...] * hm
        return carry

    lax.fori_loop(0, heads, head, 0)
    cosine = cos_ref[...]
    sine = sin_ref[...]
    gq = (dq_ref[...] * cosine - swap_halves(dq_ref[...]) * sine).astype(low)
    gk = (dk_ref[...] * cosine - swap_halves(dk_ref[...]) * sine).astype(low)
    gv = dv_ref[...].astype(low)
    gp_ref[:, :width] = gq
    gp_ref[:, width : 2 * width] = gk
    gp_ref[:, 2 * width :] = gv
    part = w0.shape[1]
    full = wide_ref.shape[1] - up_ref.shape[1]
    for k, w_ref in enumerate([w0, w1, w2, w3]):
        wide_ref[:, cols_of(ids_ref, k, part)] = nt(gq, w_ref[0]) + nt(gk, w_ref[1]) + nt(gv, w_ref[2])
    adapt = nt(gq, up_ref[0]) + nt(gk, up_ref[1]) + nt(gv, up_ref[2])
    wide_ref[:, full:] = adapt
    paq_ref[...] = (adapt * picked_ref[...].astype(single)).astype(low)
    put_pieces(ids_ref, wide_ref, keep_ref, send_ref)


def last_body(ids_ref, p0, p1, picked_ref, pdn_ref, tokens_ref, gain_ref, gm_ref, gt_ref):
    quarter = p0.shape[0]
    width = gm_ref.shape[1]
    rows = rows_of(ids_ref, 0, quarter)
    picked = picked_ref[rows, :].astype(single)
    total = p0[...] + p1[...].astype(single)
    gaq = (total[:, width:].astype(low).astype(single) * picked).astype(low)
    upstream = total[:, :width] + nn(gaq, pdn_ref[...])
    xhat, rstd = layer_norm_rows(tokens_ref[rows, :].astype(single))
    gt_ref[...] = (gm_ref[...] + layer_norm_back(upstream, gain_ref[...], xhat, rstd)).astype(low)


def assemble_body(ids_ref, p0, p1, p2, p3, out_ref):
    quarter = p0.shape[0]
    width = out_ref.shape[1]
    for k, p_ref in enumerate([p0, p1, p2, p3]):
        out_ref[rows_of(ids_ref, k, quarter), :] = p_ref[:, :width]


def padded(size):
    return -(-size // 128) * 128


def lay_out(ids_ref, values, keep_ref, send_ref, all_ref):
    ranks = all_ref.shape[0]
    at = 0
    for value in values:
        size = value.shape[1]
        all_ref[:, at : at + size] = value
        if padded(size) != size:
            all_ref[:, at + size : at + padded(size)] = jnp.zeros((ranks, padded(size) - size), single)
        at += padded(size)
    half = ranks // 2
    keep_ref[...] = all_ref[pl.ds(pl.multiple_of(ids_ref[3] * half, 16), half), :].astype(low)
    send_ref[...] = all_ref[pl.ds(pl.multiple_of((1 - ids_ref[3]) * half, 16), half), :].astype(low)


def grads_body(
    ids_ref, gai_ref, n2_ref, ao_ref, gb_ref, ad_ref, go_ref, paq_ref, n1_ref, ai_ref, gg_ref, gad_ref, act_ref,
    aq_ref, gp_ref, gao_ref, heads_ref, keep_ref, send_ref, all_ref,
):
    rows = rows_of(ids_ref, 0, gb_ref.shape[0])
    values = [
        tn(gai_ref[...], n2_ref[rows, :]),
        tn(ao_ref[rows, :], gb_ref[...]),
        tn(ad_ref[...], go_ref[rows, :]),
        tn(paq_ref[...], n1_ref[...]),
        tn(ai_ref[...], gg_ref[0]),
        tn(ai_ref[...], gg_ref[1]),
        tn(gad_ref[...], act_ref[...]),
        tn(aq_ref[...], gp_ref[...]),
        tn(gao_ref[...], heads_ref[...]),
    ]
    lay_out(ids_ref, values, keep_ref, send_ref, all_ref)


def fold_body(ids_ref, keep_ref, got_ref, own_ref, send_ref, sum_ref):
    sum_ref[...] = keep_ref[...].astype(single) + got_ref[...].astype(single)
    size = own_ref.shape[1]
    first = 1 + ids_ref[3]
    second = 2 - ids_ref[3]
    for at, (ref, bits) in enumerate([(own_ref, 0), (own_ref, second), (send_ref, first), (send_ref, 3)]):
        block = ids_ref[4] ^ bits
        ref[at % 2] = sum_ref[pl.ds(pl.multiple_of(block * size, 16), size), :].astype(low)


def total_body(ids_ref, mine_ref, got_ref, z_ref, r_ref):
    total = mine_ref[...] + got_ref[...].astype(single)
    shared = z_ref.shape[1]
    z_ref[...] = total[:, :shared].astype(low)
    r_ref[...] = total[:, shared:].astype(low)


def add_body(ids_ref, own_ref, got_ref, out_ref):
    out_ref[...] = (own_ref[...].astype(single) + got_ref[...].astype(single)).astype(low)


def join_body(ids_ref, own_ref, got_ref, r_ref, out_ref):
    shared = own_ref.shape[1]
    out_ref[:, :shared] = (own_ref[...].astype(single) + got_ref[...].astype(single)).astype(low)
    out_ref[:, shared:] = r_ref[...]


def assemble_body(ids_ref, p0, p1, p2, p3, out_ref):
    quarter = p0.shape[0]
    width = out_ref.shape[1]
    for k, p_ref in enumerate([p0, p1, p2, p3]):
        out_ref[rows_of(ids_ref, k, quarter), :] = p_ref[:, :width]


def padded(size):
    return -(-size // 128) * 128


def finish_body(ids_ref, *refs):
    m0, m1, m2, n0, n1, n2 = refs[:6]
    outs = refs[6:]
    size = m0.shape[0]
    core = ids_ref[3]
    first = 1 + core
    second = 2 - core
    pieces = [(core, 0, m0, None), (core, second, m1, None), (core, first, m2, 0), (core, 3, m2, 1)]
    pieces = pieces + [(1 - core, 0, n0, None), (1 - core, first, n1, None), (1 - core, second, n2, 0), (1 - core, 3, n2, 1)]
    for side, bits, p_ref, at in pieces:
        block = side * 4 + (ids_ref[4] ^ bits)
        start = pl.multiple_of(block * size, 16)
        col = 0

        def read(span):
            return (p_ref[:, col : col + span] if at is None else p_ref[at, :, col : col + span]).astype(single)

        for out_ref in outs:
            if len(out_ref.shape) == 4:
                for j in range(3):
                    span = out_ref.shape[3]
                    out_ref[block, j] = read(span)
                    col += span
            elif len(out_ref.shape) == 3:
                for j in range(2):
                    span = out_ref.shape[2]
                    out_ref[pl.ds(start, size), j, :] = read(span)
                    col += padded(span)
            else:
                span = out_ref.shape[1]
                out_ref[pl.ds(start, size), :] = read(span)
                col += padded(span)


def on_device(
    tokens,
    grad_out,
    lengths,
    deal,
    adapter_of,
    attention_gain,
    attention_proj,
    attention_out,
    feed_gain,
    feed_in,
    feed_out,
    attention_proj_down,
    attention_proj_up,
    attention_out_down,
    attention_out_up,
    feed_in_down,
    feed_in_up,
    feed_out_down,
    feed_out_up,
):
    fsdp_size = lax.axis_size("fsdp")
    context_size = lax.axis_size("context")
    tensor_size = lax.axis_size("tensor")
    count, width = tokens.shape
    total = deal.shape[0]
    sets, _, rank = attention_proj_down.shape
    ranks = sets * rank
    local_width = attention_proj.shape[2]
    hidden = feed_in.shape[2]
    f = lax.axis_index("fsdp")
    c = lax.axis_index("context")
    t = lax.axis_index("tensor")
    small = context_size == 2 and fsdp_size == 4
    half_at = c % 2
    chip = (f // 2) * 2 + half_at
    chunks = total // count
    if small:
        order = [(f ^ df) * context_size + (c ^ dc) for df, dc in
                 ((0, 0), (0, 1), (2, 0), (2, 1), (1, 0), (1, 1), (3, 0), (3, 1))]
    else:
        order = list(range(chunks))
    ids = jnp.stack([jnp.asarray(value, jnp.int32) for value in [f, half_at, t, f % 2, chip, *order]])
    quarter = count // tensor_size

    def over(axis, size, bit, value):
        return lax.ppermute(value, axis, swap_pairs(axis, size, bit))

    def near(value):
        return over("fsdp", fsdp_size, 1, value)

    def ahead(value):
        return over("fsdp", fsdp_size, 2, value)

    def across(value):
        return over("context", context_size, 1, value)

    def after(value, *others):
        return lax.optimization_barrier((value, *others))[0]

    def exchange(pieces):
        return [pieces[0]] + [over("tensor", tensor_size, k, pieces[k]) for k in range(1, tensor_size)]

    def spread(piece):
        far = over("tensor", tensor_size, 2, piece)
        return [piece, over("tensor", tensor_size, 1, piece), far, over("tensor", tensor_size, 1, far)]

    def reduce_rows(keep, send, *others):
        got = over("tensor", tensor_size, 1, send)
        got, *others = lax.optimization_barrier((got, *others))
        mine, passed = call(
            pair_body, [(keep.shape[1:], single), (keep.shape[1:], low)], ids, [keep, got], name="pair"
        )
        return [mine, over("tensor", tensor_size, 2, passed)], others

    proj_own = jnp.transpose(attention_proj, (1, 0, 2))
    in_own = jnp.transpose(feed_in, (1, 2, 0))
    proj_down = jnp.transpose(attention_proj_down, (0, 2, 1)).reshape(ranks, width)
    out_down_own = jnp.transpose(attention_out_down, (0, 2, 1)).reshape(ranks, local_width)
    in_down = jnp.transpose(feed_in_down, (0, 2, 1)).reshape(ranks, width)
    last_down = jnp.transpose(feed_out_down, (0, 2, 1)).reshape(ranks, hidden)
    proj_up = jnp.transpose(attention_proj_up, (2, 0, 1, 3)).reshape(3, ranks, local_width)
    out_up = attention_out_up.reshape(ranks, width)
    last_up = feed_out_up.reshape(ranks, width)

    proj_far = ahead(proj_own)
    proj_near = near(proj_own)
    in_half, last_half = call(
        split_body,
        [((1, *in_own.shape[1:]), low), ((hidden, feed_out.shape[1] // 2), low)],
        ids,
        [in_own, feed_out],
        name="split",
        cost=2.0,
    )
    in_far = ahead(in_half)

    seqs = lengths.shape[0]
    before = jnp.arange(seqs)[:, None] >= jnp.arange(seqs)[None, :]
    ends = jnp.sum(jnp.where(before, lengths[None, :], 0), axis=1)
    starts = ends - lengths
    segment_all = jnp.sum((deal[:, None] >= ends[None, :]).astype(jnp.int32), axis=1)
    first = (f * context_size + c) * count
    segment_rows = lax.dynamic_slice_in_dim(segment_all, first, count)
    deal_rows = lax.dynamic_slice_in_dim(deal, first, count)
    member = segment_rows[:, None] == jnp.arange(seqs, dtype=jnp.int32)[None, :]
    place = deal_rows - jnp.sum(jnp.where(member, starts[None, :], 0), axis=1)
    chosen = jnp.sum(jnp.where(member, adapter_of[None, :], 0), axis=1)
    set_of = jnp.arange(ranks, dtype=jnp.int32) // rank
    picked = (chosen[:, None] == set_of[None, :]).astype(low)
    half = HEAD_DIM // 2
    lane = jnp.arange(local_width, dtype=jnp.int32) % HEAD_DIM
    freq = jnp.exp((lane % half).astype(single) * (-math.log(rope_base) / half))
    angle = place.astype(single)[:, None] * freq[None, :]
    cos_full = jnp.cos(angle)
    sin_full = jnp.sin(angle) * jnp.where(lane < half, -1.0, 1.0).astype(single)[None, :]
    gain_one = attention_gain.astype(single)[None, :]
    gain_two = feed_gain.astype(single)[None, :]
    normed_one, adapted_q = call(
        prepare_body,
        [((count, width), low), ((count, ranks), low)],
        ids,
        [after(tokens, in_half), gain_one, proj_down, picked],
        name="prepare",
        cost=5.0,
    )

    packed = spread(jnp.concatenate([after(attention_out, in_half), out_down_own], axis=0))
    proj_w = [proj_own, proj_near, proj_far, near(proj_far)]
    groups = segment_all.reshape(-1, count)
    seg_col = segment_rows[:, None]
    normed_one, groups, seg_col, picked = lax.optimization_barrier((normed_one, groups, seg_col, picked))
    in_up = jnp.transpose(feed_in_up, (2, 0, 1, 3)).reshape(2, ranks, hidden)

    query, keyval = call(
        project_body,
        [((count, local_width), low), ((count, 2 * local_width), low)],
        ids,
        [normed_one, adapted_q, proj_up, cos_full, sin_full, *proj_w],
        name="project",
        cost=3.0,
    )

    def plane_gather(value, other=None):
        if not small:
            return [lax.all_gather(value, token_axes, axis=0, tiled=True)]
        corner = lax.ppermute(value, token_axes, swap_pairs(None, fsdp_size * context_size, 2 * context_size + 1))
        chips = [value, across(value), ahead(value), corner]
        if other is None:
            return chips + [near(piece) for piece in chips]
        return chips + [near(value)] + [near(after(piece, other)) for piece in chips[1:]]

    in_near = near(after(in_own, proj_near))
    keyval, in_far, in_near = lax.optimization_barrier((keyval, in_far, in_near))
    last_near = near(after(feed_out, in_near))
    keyval_all = plane_gather(keyval)
    parts_n = len(keyval_all)
    gathered = keyval_all[1:4]
    out_w_own, out_half = call(
        stack_body,
        [((width, local_width), low), ((width // 2, local_width), low)],
        ids,
        [after(packed[0], keyval), *packed[1:]],
        name="stack",
    )
    out_near = near(out_w_own)
    in_up, gain_two, out_near, last_near = lax.optimization_barrier(
        (after(in_up, keyval), gain_two, out_near, last_near)
    )
    out_far = ahead(after(out_half, *gathered, out_near))
    last_far = ahead(after(last_half, *gathered, out_near))
    in_rest = across(after(in_far, *gathered, out_near))

    square = pltpu.VMEM((count, count), single)
    slab = pltpu.VMEM((count, local_width), single)
    heads_out, attended, lse_col = call(
        lambda *refs: attend_body(parts_n, *refs),
        [((count, local_width), low), ((count, local_width), single), ((count, 128), single)],
        ids,
        [after(query, in_up, gain_two), seg_col, groups, *keyval_all],
        scratch=[
            pltpu.VMEM((chunks, count, count), single),
            square,
            square,
            slab,
            *[pltpu.VMEM(value.shape, low) for value in keyval_all],
            pltpu.SemaphoreType.DMA((parts_n,)),
        ],
        far=range(3, 3 + parts_n),
        vmem=11 if small else 60,
        name="attend",
        cost=8.0,
    )
    heads_out, out_far, last_far, in_rest = lax.optimization_barrier((heads_out, out_far, last_far, in_rest))
    heads = spread(heads_out)
    out_rest = across(out_far)
    last_rest = across(last_far)
    out_late, in_late, last_late, in_rest = after((out_far, in_far, last_far, in_rest), heads[1])
    out_w = [out_w_own, out_near, out_far, out_rest, near(out_late), near(out_rest)]
    in_w = [in_own, in_near, in_far, in_rest, near(in_late), near(in_rest)]
    last_w = [feed_out, last_near, last_far, last_rest, near(last_late), near(last_rest)]
    wide = width + ranks
    piece = ((2, quarter, wide), low)
    mid_outs = call(
        middle_body,
        [piece] * 2
        + [((count, ranks), low)] * 3
        + [
            ((count, width), low),
            ((count, hidden), low),
            ((2, count, hidden), low),
            ((quarter, width), single),
            ((4, width, local_width), low),
            ((4, *feed_out.shape), low),
        ],
        ids,
        [*heads, *out_w, *packed, out_up, tokens, gain_two, grad_out, picked, *in_w, in_down, in_up, *last_w,
         last_down, last_up],
        scratch=[
            pltpu.VMEM((count, wide), single),
            pltpu.VMEM((4, *in_own.shape), low),
            pltpu.SemaphoreType.DMA((18,)),
        ],
        far=(*range(4, 10), *range(19, 25), *range(27, 33)),
        vmem=20 if small else 60,
        name="middle",
    )
    adapted_o, adapted_i, grad_adapt_d, normed_two, activity, grad_gates, middle_q, out_all, last_all = mid_outs[2:]
    if small:
        query_late = after(query, activity)
        summed, (query_x, query_y, query_n) = reduce_rows(
            *mid_outs[:2], across(query_late), ahead(query_late), near(query_late)
        )
        query_xy = ahead(query_x)
        query_all = [query, query_x, query_y, query_xy, query_n, near(query_x), near(query_y)]
    else:
        summed, _ = reduce_rows(*mid_outs[:2])
        query_all = plane_gather(query)
    feed_pieces = call(
        feed_body,
        [piece] * 2,
        ids,
        [after(activity, summed[0]), last_down, last_all],
        scratch=[pltpu.VMEM((count, wide), single)],
        name="feed",
    )
    summed, query_all, feed_pieces = lax.optimization_barrier((summed, query_all, feed_pieces))
    turn = ((quarter, local_width + ranks), low)
    *turned, grad_mid, grad_branch, grad_adapt_i = call(
        turn_body,
        [turn] * 4 + [((quarter, width), single), ((quarter, width), low), ((quarter, ranks), low)],
        ids,
        [*summed, picked, in_down, middle_q, gain_two, grad_out, out_up, out_all, *packed],
        vmem=6 if small else 40,
        name="turn",
        cost=3.0,
    )
    if small:
        query_all = query_all + [near(after(query_all[3], grad_mid))]
    arrived = exchange(turned)
    sizes = [width] * 4 + [padded(hidden)] * 3 + [3 * local_width, local_width]
    columns = sum(sizes)
    places = [(i, j) for i in range(fsdp_size) for j in range(context_size)]
    number = {place: at for at, place in enumerate(places)}
    side = {(i, j): (i, j ^ 1) for i, j in places}
    front = {(i, j): (i ^ 2, j) for i, j in places}
    one = [(number[p], number[front[p] if p[0] % 2 else side[p]]) for p in places]
    two = [(number[p], number[side[p] if p[0] % 2 else front[p]]) for p in places]
    rows = ranks // 8

    def fold_strips(keep, send):
        columns = keep.shape[1]
        return call(
            fold_body,
            [((2, rows, columns), low)] * 2,
            ids,
            [keep, near(send)],
            scratch=[pltpu.VMEM((ranks // 2, columns), single)],
            name="fold",
            cost=3.0,
        )

    def reduce_strips(own, got):
        columns = own.shape[2]
        mine, passed = call(
            pair_body,
            [((rows, columns), single), ((rows, columns), low)],
            ids,
            [own, got],
            name="pair_chips",
            cost=3.0,
        )
        return [mine, lax.ppermute(passed, token_axes, two)]

    (feed_mine, feed_got), _ = reduce_rows(*feed_pieces)
    arrived, query_all, feed_mine = lax.optimization_barrier((arrived, query_all, feed_mine))
    tail = 32
    message, delta_col, grad_adapt_o = call(
        collect_body,
        [((count + tail, local_width), low), ((count, 128), single), ((count, ranks), low)],
        ids,
        [*arrived, attended, lse_col],
        name="collect",
    )
    (grad_query,) = call(
        lambda *refs: query_body(parts_n, *refs),
        [((count, local_width), single)],
        ids,
        [query, message, lse_col, delta_col, seg_col, groups, *keyval_all],
        scratch=[slab],
        vmem=8 if small else 60,
        name="queries",
        cost=7.0,
    )
    message_all = plane_gather(message, grad_query)
    output_q, adapted_d = call(
        out_body,
        [((quarter, width), low), ((quarter, ranks), low)],
        ids,
        [feed_mine, after(feed_got, grad_query), picked, middle_q, last_up],
        name="outputs",
    )
    output_all = spread(output_q)
    *last_pieces, grad_proj, part_adapt_q = call(
        lambda *refs: key_body(parts_n, *refs),
        [piece] * 2 + [((count, 3 * local_width), low), ((count, ranks), low)],
        ids,
        [after(keyval, output_q), seg_col, groups, grad_query, cos_full, sin_full, proj_up, picked, *proj_w, *query_all, *message_all],
        scratch=[
            pltpu.VMEM((chunks, 8, count), single), slab, slab, slab, slab, pltpu.VMEM((count, wide), single),
            *[pltpu.VMEM(value.shape, low) for value in message_all],
            pltpu.SemaphoreType.DMA((parts_n,)),
        ],
        far=range(12 + parts_n, 12 + 2 * parts_n),
        vmem=14 if small else 60,
        name="keys",
        cost=10.0,
    )
    last_mine, last_got = reduce_rows(*last_pieces)[0]
    late = call(
        grads_body,
        [((ranks // 2, columns), low)] * 2,
        ids,
        [grad_adapt_i, normed_two, adapted_o, grad_branch, adapted_d, grad_out,
         after(part_adapt_q, output_all[1], output_all[2]), normed_one, adapted_i,
         grad_gates, grad_adapt_d, activity, adapted_q, grad_proj, grad_adapt_o, heads_out],
        scratch=[pltpu.VMEM((ranks, columns), single)],
        vmem=8 if small else 40,
        name="grads",
        cost=3.0,
    )
    (grad_tokens_q,) = call(
        last_body,
        [((quarter, width), low)],
        ids,
        [last_mine, last_got, picked, proj_down, tokens, gain_one, grad_mid],
        name="last",
    )
    finals = [((ranks, width), single)] * 4 + [((ranks, 2, hidden), single), ((ranks, hidden), single)]
    finals = finals + [((sets, 3, rank, local_width), single), ((ranks, local_width), single)]
    if small:
        late_own, late_out = fold_strips(*late)
        late_mine, late_got = reduce_strips(after(late_own, last_mine), lax.ppermute(late_out, token_axes, one))
        shared, rest = call(
            total_body,
            [((rows, 4 * width), low), ((rows, columns - 4 * width), low)],
            ids,
            [late_mine, after(late_got, last_got)],
            name="total",
        )
        (shared,) = call(
            add_body, [((rows, 4 * width), low)], ids, [shared, over("tensor", tensor_size, 1, shared)], name="add"
        )
        shared_far = over("tensor", tensor_size, 2, shared)
        tokens_all = spread(after(grad_tokens_q, shared))
        (output,) = call(assemble_body, [((count, width), low)], ids, output_all, name="join_output")
        rest, output = lax.optimization_barrier((rest, output))
        (joined,) = call(
            join_body,
            [((rows, columns), low)],
            ids,
            [shared, shared_far, rest],
            name="join",
        )
        beside = lax.ppermute(joined, token_axes, two)
        both = jnp.stack([joined, after(beside, tokens_all[1], tokens_all[2])])
        others = lax.ppermute(both, token_axes, one)
        strips = [joined, beside, after(others, tokens_all[3])]
        strips = strips + [near(value) for value in strips]
        results = call(finish_body, finals, ids, strips, name="finish")
    else:
        tokens_all = spread(grad_tokens_q)
        (output,) = call(assemble_body, [((count, width), low)], ids, output_all, name="join_output")
        pair = jnp.where(f % 2 == 0, jnp.concatenate(late), jnp.concatenate(late[::-1]))
        pair = lax.psum(pair, token_axes)
        joined = jnp.concatenate([lax.psum(pair[:, : 4 * width], "tensor"), pair[:, 4 * width :]], axis=1)
        cut = [0]
        for span in [width] * 4 + [padded(hidden)] * 3 + [3 * local_width, local_width]:
            cut.append(cut[-1] + span)
        slices = [joined[:, lo:hi].astype(single) for lo, hi in zip(cut, cut[1:])]
        *results, gate_up, mult_up, last_grad, proj_up_grad, out_down_grad = slices
        results = [*results, jnp.stack([gate_up[:, :hidden], mult_up[:, :hidden]], axis=1), last_grad[:, :hidden]]
        proj_up_grad = jnp.transpose(proj_up_grad.reshape(sets, rank, 3, local_width), (0, 2, 1, 3))
        results = [*results, proj_up_grad, out_down_grad]

    in_down_grad, out_up_grad, last_up_grad, proj_down_grad, in_up_grad, last_grad, proj_up_grad, out_down_grad = results
    (grad_tokens,) = call(assemble_body, [((count, width), low)], ids, tokens_all, name="join_tokens")


    def down(grad):
        return jnp.transpose(grad.reshape(sets, rank, -1), (0, 2, 1))

    return (
        output,
        grad_tokens,
        down(proj_down_grad),
        jnp.transpose(proj_up_grad, (0, 2, 1, 3)),
        down(out_down_grad),
        out_up_grad.reshape(sets, rank, width),
        down(in_down_grad),
        in_up_grad.reshape(sets, rank, 2, hidden),
        down(last_grad),
        last_up_grad.reshape(sets, rank, width),
    )


def solution(mesh):
    return jax.shard_map(
        on_device,
        mesh=mesh,
        in_specs=(
            P(("fsdp", "context"), None),
            P(("fsdp", "context"), None),
            P(),
            P(),
            P(),
            P(),
            P("fsdp", None, "tensor"),
            P("tensor", "fsdp"),
            P(),
            P("fsdp", None, "tensor"),
            P("tensor", "fsdp"),
            P(),
            P(None, None, None, "tensor"),
            P(None, "tensor", None),
            P(),
            P(),
            P(None, None, None, "tensor"),
            P(None, "tensor", None),
            P(),
        ),
        out_specs=(
            P(("fsdp", "context"), None),
            P(("fsdp", "context"), None),
            P(),
            P(None, None, None, "tensor"),
            P(None, "tensor", None),
            P(),
            P(),
            P(None, None, None, "tensor"),
            P(None, "tensor", None),
            P(),
        ),
        check_vma=False,
    )
```

```python
import math

import jax
import jax.numpy as jnp
from jax import lax
from jax.experimental import pallas as pl
from jax.experimental.pallas import tpu as pltpu
from jax.sharding import PartitionSpec as P

HEAD_DIM = 64


rope_base = 160000.0
epsilon = 1e-05
negative = -1e30
single = jnp.float32
low = jnp.bfloat16
scale = HEAD_DIM ** (-0.5)
token_axes = ("fsdp", "context")
every_axis = ("fsdp", "context", "tensor")


def nn(left, right):
    return lax.dot_general(
        left, right, (((1,), (0,)), ((), ())), preferred_element_type=jnp.float32
    )


def nt(left, right):
    return lax.dot_general(
        left, right, (((1,), (1,)), ((), ())), preferred_element_type=jnp.float32
    )


def tn(left, right):
    return lax.dot_general(
        left, right, (((0,), (0,)), ((), ())), preferred_element_type=jnp.float32
    )


def call(body, outs, ids, args, scratch=(), vmem=6, name=None, far=(), cost=0.0):
    whole = pl.BlockSpec(memory_space=pltpu.VMEM)
    return pl.pallas_call(
        body,
        out_shape=[jax.ShapeDtypeStruct(shape, kind) for shape, kind in outs],
        in_specs=[pl.BlockSpec(memory_space=pltpu.SMEM)]
        + [pl.BlockSpec(memory_space=pltpu.HBM) if at in far else whole for at in range(len(args))],
        out_specs=[whole] * len(outs),
        scratch_shapes=list(scratch),
        compiler_params=pltpu.CompilerParams(vmem_limit_bytes=vmem << 20),
        cost_estimate=pl.CostEstimate(flops=int(cost * 1e12) + 1, bytes_accessed=int(cost * 1e12) + 1, transcendentals=0),
        name=name,
    )(ids, *args)


def swap_pairs(axis, size, bit):
    return [(i, i ^ bit) for i in range(size)]


def layer_norm_rows(values):
    centered = values - jnp.mean(values, axis=1, keepdims=True)
    rstd = lax.rsqrt(jnp.mean(centered * centered, axis=1, keepdims=True) + epsilon)
    return (centered * rstd, rstd)


def layer_norm_back(upstream, gain, xhat, rstd):
    scaled = upstream * gain
    return rstd * (
        scaled
        - jnp.mean(scaled, axis=1, keepdims=True)
        - xhat * jnp.mean(scaled * xhat, axis=1, keepdims=True)
    )


def swap_halves(u):
    width = u.shape[1]
    half = HEAD_DIM // 2
    lane = lax.broadcasted_iota(jnp.int32, (1, width), 1)
    return jnp.where(
        lane % HEAD_DIM < half, pltpu.roll(u, width - half, 1), pltpu.roll(u, half, 1)
    )


def head_row(width, head):
    lane = lax.broadcasted_iota(jnp.int32, (1, width), 1)
    return (lane // HEAD_DIM == head).astype(single)


def start_copies(pairs, sems):
    copies = [pltpu.make_async_copy(src, dst, sems.at[n]) for n, (src, dst) in enumerate(pairs)]
    for copy in copies:
        copy.start()
    return copies


def loop(count, step, most=8):
    if count <= most:
        for number in range(count):
            step(number)
    else:

        def inner(number, carry):
            step(number)
            return carry

        lax.fori_loop(0, count, inner, 0)


def at_block(number, size):
    start = number * size
    return pl.ds(start if isinstance(start, int) else pl.multiple_of(start, 16), size)


def block_rows(count, total):
    return max(16, min(count, 2048 * count // total))


def cols_of(ids_ref, k, width):
    return pl.ds(pl.multiple_of((ids_ref[0] ^ k) * width, 128), width)


def rows_of(ids_ref, k, height):
    return pl.ds(pl.multiple_of((ids_ref[2] ^ k) * height, 16), height)


def join_rows(ids_ref, dst_ref, mine_ref, other_ref):
    size = mine_ref.shape[0]
    dst_ref[pl.ds(ids_ref[1] * size, size)] = mine_ref[...]
    dst_ref[pl.ds((1 - ids_ref[1]) * size, size)] = other_ref[...]


def join_cols(ids_ref, dst_ref, mine_ref, other_ref):
    size = mine_ref.shape[1]
    dst_ref[:, pl.ds(pl.multiple_of(ids_ref[1] * size, 128), size)] = mine_ref[...]
    dst_ref[:, pl.ds(pl.multiple_of((1 - ids_ref[1]) * size, 128), size)] = other_ref[...]


def project_body(ids_ref, x_ref, aq_ref, up_ref, cos_ref, sin_ref, *refs):
    weights, q_ref, kv_ref = (refs[:-2], refs[-2], refs[-1])
    part = weights[0].shape[1]
    width = weights[0].shape[2]
    for j in range(3):
        acc = nn(aq_ref[...], up_ref[j])
        for k, w_ref in enumerate(weights):
            acc = acc + nn(x_ref[:, cols_of(ids_ref, k, part)], w_ref[j])
        if j < 2:
            acc = acc * cos_ref[...] + swap_halves(acc) * sin_ref[...]
        if j == 0:
            q_ref[...] = acc.astype(low)
        else:
            kv_ref[:, (j - 1) * width : j * width] = acc.astype(low)


def prepare_body(ids_ref, tokens_ref, gain_ref, down_ref, picked_ref, n1_ref, aq_ref):
    xhat, _ = layer_norm_rows(tokens_ref[...].astype(single))
    normed = (xhat * gain_ref[...]).astype(low)
    n1_ref[...] = normed
    aq_ref[...] = (picked_ref[...].astype(single) * nt(normed, down_ref[...])).astype(low)


def split_body(ids_ref, in_ref, last_ref, ihalf_ref, lhalf_ref):
    ihalf_ref[...] = in_ref[pl.ds(ids_ref[1], 1)]
    cols = lhalf_ref.shape[1]
    lhalf_ref[...] = last_ref[:, pl.ds(pl.multiple_of(ids_ref[1] * cols, 128), cols)]


def stack_body(ids_ref, p0, p1, p2, p3, full_ref, half_ref):
    rows = p0.shape[1]
    for k, p_ref in enumerate([p0, p1, p2, p3]):
        full_ref[k * rows : (k + 1) * rows, :] = p_ref[:rows, :]
    size = half_ref.shape[0]
    half_ref[...] = full_ref[pl.ds(pl.multiple_of(ids_ref[1] * size, 16), size), :]


def put_pieces(ids_ref, wide_ref, keep_ref, send_ref):
    quarter = keep_ref.shape[1]
    for at, (ref, k) in enumerate([(keep_ref, 0), (keep_ref, 2), (send_ref, 1), (send_ref, 3)]):
        ref[at % 2] = wide_ref[rows_of(ids_ref, k, quarter), :].astype(low)


def pair_body(ids_ref, keep_ref, got_ref, mine_ref, pass_ref):
    mine_ref[...] = keep_ref[0].astype(single) + got_ref[0].astype(single)
    pass_ref[...] = (keep_ref[1].astype(single) + got_ref[1].astype(single)).astype(low)


def attend_body(parts_n, ids_ref, q_ref, segc_ref, groups_ref, *refs):
    parts = refs[:parts_n]
    heads_ref, att_ref, lcol_ref, kv_ref, many_ref, s_ref, sems = refs[parts_n:]
    count, width = q_ref.shape
    heads = width // HEAD_DIM
    chunk = groups_ref.shape[1]
    size = many_ref.shape[0] // heads
    base = 0
    pairs = []
    for part in parts:
        pairs.append((part, kv_ref.at[base : base + part.shape[0], :]))
        base += part.shape[0]
    copies = start_copies(pairs, sems)
    lane = lax.broadcasted_iota(jnp.int32, (1, 128), 1)
    waits = list(copies)

    def block(number):
        rows = at_block(number, size)
        for h in range(heads):
            many_ref[h * size : (h + 1) * size, :] = q_ref[rows, :] * (head_row(width, h) * scale).astype(low)

        def scores(j):
            if isinstance(j, int) and waits and len(copies) > 1:
                waits.pop(0).wait()
            cols = at_block(j, chunk)
            same = segc_ref[rows, :] == groups_ref[pl.ds(ids_ref[5 + j], 1), :]
            s = nt(many_ref[...], kv_ref[cols, :width])
            for h in range(heads):
                s_ref[h * size : (h + 1) * size, cols] = jnp.where(same, s[h * size : (h + 1) * size], negative)

        if len(copies) == 1 and waits:
            waits.pop(0).wait()
        loop(base // chunk, scores)
        total = jnp.zeros((size, width), single)
        lcol = jnp.zeros((size, 128), single)
        for h in range(heads):
            s = s_ref[h * size : (h + 1) * size, :]
            top = jnp.max(s, axis=1, keepdims=True)
            p = jnp.exp(s - top)
            mass = jnp.sum(p, axis=1, keepdims=True)
            total = total + nn(p.astype(low), kv_ref[:, width:]) * (head_row(width, h) / mass)
            lcol = jnp.where(lane == h, top + jnp.log(mass), lcol)
        att_ref[rows, :] = total
        lcol_ref[rows, :] = lcol
        heads_ref[rows, :] = total.astype(low)

    loop(count // size, block, 1)


def middle_body(ids_ref, *refs):
    heads = refs[0:4]
    wown, wnear, wa, wb, wc, wd = refs[4:10]
    packs = refs[10:14]
    refs = refs[3:]
    ou_ref, tokens_ref, gain_ref, go_ref, picked_ref = refs[11:16]
    iown, inear, ia, ib, ic, idd = refs[16:22]
    idn_ref, iu_ref = refs[22:24]
    lown, lnear, la, lb, lc, ld = refs[24:30]
    ldn_ref, lup_ref = refs[30:32]
    keep_ref, send_ref, ao_ref, ai_ref, gad_ref, n2_ref, act_ref, gg_ref, mid_ref, wts, lts = refs[32:43]
    wide_ref, its, sems = refs[43:]
    mine, rest = (ids_ref[1], 1 - ids_ref[1])
    half = wa.shape[0]
    step = la.shape[1]

    def rows(k, at):
        return wts.at[k, pl.ds(pl.multiple_of(at * half, 16), half), :]

    def cols(k, at):
        return lts.at[k, :, pl.ds(pl.multiple_of(at * step, 128), step)]

    pairs = [
        (wown, wts.at[0]),
        (wnear, wts.at[1]),
        (wa, rows(2, mine)),
        (wb, rows(2, rest)),
        (wc, rows(3, mine)),
        (wd, rows(3, rest)),
        (iown, its.at[0]),
        (inear, its.at[1]),
        (ia, its.at[2, pl.ds(mine, 1)]),
        (ib, its.at[2, pl.ds(rest, 1)]),
        (ic, its.at[3, pl.ds(mine, 1)]),
        (idd, its.at[3, pl.ds(rest, 1)]),
        (lown, lts.at[0]),
        (lnear, lts.at[1]),
        (la, cols(2, mine)),
        (lb, cols(2, rest)),
        (lc, cols(3, mine)),
        (ld, cols(3, rest)),
    ]
    copies = [pltpu.make_async_copy(src, dst, sems.at[n]) for n, (src, dst) in enumerate(pairs)]
    for copy in copies:
        copy.start()
    h0 = heads[0]
    w0 = wown
    outs_w = [wts.at[k] for k in range(4)]
    ins_w = [its.at[k] for k in range(4)]
    lasts_w = [lts.at[k] for k in range(4)]
    part = w0.shape[1]
    span = h0.shape[1]
    width = tokens_ref.shape[1]
    picked = picked_ref[...].astype(single)
    span = h0.shape[1]
    adapt = nt(h0[...], packs[0][span:, :])
    for k in range(1, len(heads)):
        adapt = adapt + nt(heads[k][...], packs[k][span:, :])
    ao = (picked * adapt).astype(low)
    ao_ref[...] = ao
    for copy in copies[:6]:
        copy.wait()
    for k, w_ref in enumerate(outs_w):
        acc = nn(h0[...], w_ref[:span, :])
        for r in range(1, len(heads)):
            acc = acc + nn(heads[r][...], w_ref[r * span : (r + 1) * span, :])
        wide_ref[:, cols_of(ids_ref, k, part)] = acc
    middle = tokens_ref[...].astype(single) + wide_ref[:, :width] + nn(ao, ou_ref[...])
    wide_ref[:, :width] = middle
    quarter = mid_ref.shape[0]
    mid_ref[...] = wide_ref[rows_of(ids_ref, 0, quarter), :width]
    xhat, _ = layer_norm_rows(middle)
    n2 = (xhat * gain_ref[...]).astype(low)
    n2_ref[...] = n2
    ai = (picked * nt(n2, idn_ref[...])).astype(low)
    ai_ref[...] = ai
    for copy in copies[6:12]:
        copy.wait()
    gate = nn(ai, iu_ref[0])
    mult = nn(ai, iu_ref[1])
    for k, w_ref in enumerate(ins_w):
        x = n2_ref[:, cols_of(ids_ref, k, part)]
        gate = gate + nt(x, w_ref[0])
        mult = mult + nt(x, w_ref[1])
    phi = 0.5 * (1.0 + lax.erf(gate * (2.0**-0.5)))
    gated = gate * phi
    act_ref[...] = (gated * mult).astype(low)
    slope = phi + gate * jnp.exp(-0.5 * gate * gate) * (1.0 / math.sqrt(2.0 * math.pi))
    go = go_ref[...]
    gad = (nt(go, lup_ref[...]).astype(low).astype(single) * picked).astype(low)
    gad_ref[...] = gad
    for copy in copies[12:]:
        copy.wait()
    ga = nn(gad, ldn_ref[...])
    for k, w_ref in enumerate(lasts_w):
        ga = ga + nt(go_ref[:, cols_of(ids_ref, k, part)], w_ref[...])
    gg0 = (slope * (ga * mult)).astype(low)
    gg1 = (ga * gated).astype(low)
    gg_ref[0] = gg0
    gg_ref[1] = gg1
    for k, w_ref in enumerate(ins_w):
        wide_ref[:, cols_of(ids_ref, k, part)] = nn(gg0, w_ref[0]) + nn(gg1, w_ref[1])
    wide_ref[:, width:] = nt(gg0, iu_ref[0]) + nt(gg1, iu_ref[1])
    put_pieces(ids_ref, wide_ref, keep_ref, send_ref)


def feed_body(ids_ref, act_ref, ldn_ref, lts, keep_ref, send_ref, wide_ref):
    part = lts.shape[2]
    act = act_ref[...]
    wide_ref[:, wide_ref.shape[1] - ldn_ref.shape[0] :] = nt(act, ldn_ref[...])
    for k in range(4):
        wide_ref[:, cols_of(ids_ref, k, part)] = nn(act, lts[k])
    put_pieces(ids_ref, wide_ref, keep_ref, send_ref)


def turn_body(
    ids_ref, p0, p1, picked_ref, idn_ref, mid_ref, gain_ref, go_ref, ou_ref, wts, d0, d1, d2, d3,
    a0, a1, a2, a3, gm_ref, gb_ref, gai_ref,
):
    quarter = p0.shape[0]
    width = mid_ref.shape[1]
    part = wts.shape[2]
    rows = rows_of(ids_ref, 0, quarter)
    picked = picked_ref[rows, :].astype(single)
    total = p0[...] + p1[...].astype(single)
    gai = (total[:, width:].astype(low).astype(single) * picked).astype(low)
    gai_ref[...] = gai
    upstream = total[:, :width] + nn(gai, idn_ref[...])
    xhat, rstd = layer_norm_rows(mid_ref[...])
    gm = go_ref[rows, :].astype(single) + layer_norm_back(upstream, gain_ref[...], xhat, rstd)
    gm_ref[...] = gm
    gb = gm.astype(low)
    gb_ref[...] = gb
    gao = (nt(gb, ou_ref[...]).astype(low).astype(single) * picked).astype(low)
    span = d0.shape[1]
    grads = [nn(gao, d_ref[span:, :]) for d_ref in (d0, d1, d2, d3)]
    for k in range(4):
        w_ref = wts.at[k]
        x = gb_ref[:, cols_of(ids_ref, k, part)]
        for r in range(4):
            grads[r] = grads[r] + nt(x, w_ref[r * span : (r + 1) * span, :])
    for k, a_ref in enumerate([a0, a1, a2, a3]):
        a_ref[:, :span] = grads[k].astype(low)
        a_ref[:, span:] = gao


def out_body(ids_ref, p0, p1, picked_ref, mid_ref, lup_ref, out_ref, ad_ref):
    width = mid_ref.shape[1]
    picked = picked_ref[rows_of(ids_ref, 0, p0.shape[0]), :].astype(single)
    total = p0[...] + p1[...].astype(single)
    ad = (picked * total[:, width:]).astype(low)
    ad_ref[...] = ad
    out_ref[...] = (mid_ref[...] + total[:, :width] + nn(ad, lup_ref[...])).astype(low)


def collect_body(ids_ref, a0, a1, a2, a3, att_ref, lcol_ref, msg_ref, dcol_ref, gao_ref):
    quarter = a0.shape[0]
    count, width = att_ref.shape
    for k, a_ref in enumerate([a0, a1, a2, a3]):
        msg_ref[rows_of(ids_ref, k, quarter), :] = a_ref[:, :width]
        gao_ref[rows_of(ids_ref, k, quarter), :] = a_ref[:, width:]
    both = msg_ref[:count, :].astype(single) * att_ref[...]
    heads = width // HEAD_DIM
    lane = lax.broadcasted_iota(jnp.int32, (1, 128), 1)
    dcol = jnp.zeros((count, 128), single)
    pair = lcol_ref[...]
    for h in range(heads):
        delta = jnp.sum(both * head_row(width, h), axis=1, keepdims=True)
        dcol = jnp.where(lane == h, delta, dcol)
        pair = jnp.where(lane == heads + h, delta, pair)
    dcol_ref[...] = dcol
    rows = jnp.transpose(pair)[:8, :]
    first = rows.astype(low).astype(single)
    rest = rows - first
    second = rest.astype(low).astype(single)
    third = rest - second
    tail = jnp.concatenate([first, second, third, jnp.zeros_like(first)], axis=0)
    msg_ref[count:, :] = tail.astype(low)


def query_body(
    ids_ref, q_ref, msg_ref, lcol_ref, dcol_ref, segc_ref, groups_ref, kv_ref, dq_ref, many_ref, more_ref, ds_ref
):
    count, width = q_ref.shape
    heads = width // HEAD_DIM
    chunk = groups_ref.shape[1]
    size = many_ref.shape[0] // heads

    def block(number):
        rows = at_block(number, size)
        for h in range(heads):
            many_ref[h * size : (h + 1) * size, :] = q_ref[rows, :] * (head_row(width, h) * scale).astype(low)
            more_ref[h * size : (h + 1) * size, :] = msg_ref[rows, :] * head_row(width, h).astype(low)

        def scores(j):
            cols = at_block(j, chunk)
            same = segc_ref[rows, :] == groups_ref[pl.ds(ids_ref[5 + j], 1), :]
            s = nt(many_ref[...], kv_ref[cols, :width])
            dp = nt(more_ref[...], kv_ref[cols, width:])
            for h in range(heads):
                mine = slice(h * size, (h + 1) * size)
                p = jnp.exp(jnp.where(same, s[mine] - lcol_ref[rows, h : h + 1], negative))
                ds_ref[mine, cols] = (p * (dp[mine] - dcol_ref[rows, h : h + 1])).astype(low)

        loop(kv_ref.shape[0] // chunk, scores)
        dq = nn(ds_ref[...], kv_ref[:, :width])
        total = jnp.zeros((size, width), single)
        for h in range(heads):
            total = total + dq[h * size : (h + 1) * size] * (head_row(width, h) * scale)
        dq_ref[rows, :] = total

    loop(count // size, block, 1)


def key_body(
    parts_n, ids_ref, own_ref, segc_ref, groups_ref, dq_ref, cos_ref, sin_ref, up_ref, picked_ref, w0, w1, w2, w3, *refs
):
    parts = refs[:parts_n]
    msgs = refs[parts_n : 2 * parts_n]
    keep_ref, send_ref, gp_ref, paq_ref, stat_ref, dk_ref, dv_ref, wide_ref, many_ref, more_ref, p_ref, ds_ref = refs[
        2 * parts_n : 2 * parts_n + 12
    ]
    q_ref, do_ref, tail_ref, sems = refs[2 * parts_n + 12 :]
    count = own_ref.shape[0]
    width = dq_ref.shape[1]
    heads = width // HEAD_DIM
    base = 0
    pairs = []
    for part, msg in zip(parts, msgs):
        held = msg.shape[0]
        pairs.append((part, q_ref.at[base * count : (base + held) * count, :]))
        pairs.append((msg.at[:, :count, :], do_ref.at[base : base + held]))
        pairs.append((msg.at[:, count:, :], tail_ref.at[base : base + held]))
        base += held
    copies = start_copies(pairs, sems)
    for copy in copies:
        copy.wait()
    for j in range(base):
        e = tail_ref[j].astype(single)
        stat_ref[:, j * count : (j + 1) * count] = e[:8] + e[8:16] + e[16:24]

    size = many_ref.shape[0] // heads

    def block(number):
        rows = at_block(number, size)
        for h in range(heads):
            hm = head_row(width, h)
            many_ref[h * size : (h + 1) * size, :] = own_ref[rows, :width] * (hm * scale).astype(low)
            more_ref[h * size : (h + 1) * size, :] = own_ref[rows, width:] * hm.astype(low)

        def scores(j):
            cols = at_block(j, count)
            same = segc_ref[rows, :] == groups_ref[pl.ds(ids_ref[5 + j], 1), :]
            s = nt(many_ref[...], q_ref[cols, :])
            dp = nt(more_ref[...], do_ref[j])
            for h in range(heads):
                mine = slice(h * size, (h + 1) * size)
                p = jnp.exp(jnp.where(same, s[mine] - stat_ref[h : h + 1, cols], negative))
                p_ref[mine, cols] = p.astype(low)
                ds_ref[mine, cols] = (p * (dp[mine] - stat_ref[heads + h : heads + h + 1, cols])).astype(low)

        loop(base, scores)
        dv = nn(p_ref[...], do_ref[...].reshape(base * count, width))
        dk = nn(ds_ref[...], q_ref[...])
        dv_total = jnp.zeros((size, width), single)
        dk_total = jnp.zeros((size, width), single)
        for h in range(heads):
            hm = head_row(width, h)
            dv_total = dv_total + dv[h * size : (h + 1) * size] * hm
            dk_total = dk_total + dk[h * size : (h + 1) * size] * (hm * scale)
        dv_ref[rows, :] = dv_total
        dk_ref[rows, :] = dk_total

    loop(count // size, block, 1)
    cosine = cos_ref[...]
    sine = sin_ref[...]
    gq = (dq_ref[...] * cosine - swap_halves(dq_ref[...]) * sine).astype(low)
    gk = (dk_ref[...] * cosine - swap_halves(dk_ref[...]) * sine).astype(low)
    gv = dv_ref[...].astype(low)
    gp_ref[:, :width] = gq
    gp_ref[:, width : 2 * width] = gk
    gp_ref[:, 2 * width :] = gv
    part = w0.shape[1]
    full = wide_ref.shape[1] - up_ref.shape[1]
    for k, w_ref in enumerate([w0, w1, w2, w3]):
        wide_ref[:, cols_of(ids_ref, k, part)] = nt(gq, w_ref[0]) + nt(gk, w_ref[1]) + nt(gv, w_ref[2])
    adapt = nt(gq, up_ref[0]) + nt(gk, up_ref[1]) + nt(gv, up_ref[2])
    wide_ref[:, full:] = adapt
    paq_ref[...] = (adapt * picked_ref[...].astype(single)).astype(low)
    put_pieces(ids_ref, wide_ref, keep_ref, send_ref)


def last_body(ids_ref, p0, p1, picked_ref, pdn_ref, tokens_ref, gain_ref, gm_ref, gt_ref):
    quarter = p0.shape[0]
    width = gm_ref.shape[1]
    rows = rows_of(ids_ref, 0, quarter)
    picked = picked_ref[rows, :].astype(single)
    total = p0[...] + p1[...].astype(single)
    gaq = (total[:, width:].astype(low).astype(single) * picked).astype(low)
    upstream = total[:, :width] + nn(gaq, pdn_ref[...])
    xhat, rstd = layer_norm_rows(tokens_ref[rows, :].astype(single))
    gt_ref[...] = (gm_ref[...] + layer_norm_back(upstream, gain_ref[...], xhat, rstd)).astype(low)


def assemble_body(ids_ref, p0, p1, p2, p3, out_ref):
    quarter = p0.shape[0]
    width = out_ref.shape[1]
    for k, p_ref in enumerate([p0, p1, p2, p3]):
        out_ref[rows_of(ids_ref, k, quarter), :] = p_ref[:, :width]


def padded(size):
    return -(-size // 128) * 128


def lay_out(ids_ref, values, keep_ref, send_ref, all_ref):
    ranks = all_ref.shape[0]
    at = 0
    for value in values:
        size = value.shape[1]
        all_ref[:, at : at + size] = value
        if padded(size) != size:
            all_ref[:, at + size : at + padded(size)] = jnp.zeros((ranks, padded(size) - size), single)
        at += padded(size)
    half = ranks // 2
    keep_ref[...] = all_ref[pl.ds(pl.multiple_of(ids_ref[3] * half, 16), half), :].astype(low)
    send_ref[...] = all_ref[pl.ds(pl.multiple_of((1 - ids_ref[3]) * half, 16), half), :].astype(low)


def grads_body(
    ids_ref, gai_ref, n2_ref, ao_ref, gb_ref, ad_ref, go_ref, paq_ref, n1_ref, ai_ref, gg_ref, gad_ref, act_ref,
    aq_ref, gp_ref, gao_ref, heads_ref, keep_ref, send_ref, all_ref,
):
    rows = rows_of(ids_ref, 0, gb_ref.shape[0])
    values = [
        tn(gai_ref[...], n2_ref[rows, :]),
        tn(ao_ref[rows, :], gb_ref[...]),
        tn(ad_ref[...], go_ref[rows, :]),
        tn(paq_ref[...], n1_ref[...]),
        tn(ai_ref[...], gg_ref[0]),
        tn(ai_ref[...], gg_ref[1]),
        tn(gad_ref[...], act_ref[...]),
        tn(aq_ref[...], gp_ref[...]),
        tn(gao_ref[...], heads_ref[...]),
    ]
    lay_out(ids_ref, values, keep_ref, send_ref, all_ref)


def fold_body(ids_ref, keep_ref, got_ref, own_ref, send_ref, sum_ref):
    sum_ref[...] = keep_ref[...].astype(single) + got_ref[...].astype(single)
    size = own_ref.shape[1]
    first = 1 + ids_ref[3]
    second = 2 - ids_ref[3]
    for at, (ref, bits) in enumerate([(own_ref, 0), (own_ref, second), (send_ref, first), (send_ref, 3)]):
        block = ids_ref[4] ^ bits
        ref[at % 2] = sum_ref[pl.ds(pl.multiple_of(block * size, 16), size), :].astype(low)


def total_body(ids_ref, mine_ref, got_ref, z_ref, r_ref):
    total = mine_ref[...] + got_ref[...].astype(single)
    shared = z_ref.shape[1]
    z_ref[...] = total[:, :shared].astype(low)
    r_ref[...] = total[:, shared:].astype(low)


def add_body(ids_ref, own_ref, got_ref, out_ref):
    out_ref[...] = (own_ref[...].astype(single) + got_ref[...].astype(single)).astype(low)


def join_body(ids_ref, own_ref, got_ref, r_ref, out_ref):
    shared = own_ref.shape[1]
    out_ref[:, :shared] = (own_ref[...].astype(single) + got_ref[...].astype(single)).astype(low)
    out_ref[:, shared:] = r_ref[...]


def assemble_body(ids_ref, p0, p1, p2, p3, out_ref):
    quarter = p0.shape[0]
    width = out_ref.shape[1]
    for k, p_ref in enumerate([p0, p1, p2, p3]):
        out_ref[rows_of(ids_ref, k, quarter), :] = p_ref[:, :width]


def padded(size):
    return -(-size // 128) * 128


def finish_body(ids_ref, *refs):
    m0, m1, m2, n0, n1, n2 = refs[:6]
    outs = refs[6:]
    size = m0.shape[0]
    core = ids_ref[3]
    first = 1 + core
    second = 2 - core
    pieces = [(core, 0, m0, None), (core, second, m1, None), (core, first, m2, 0), (core, 3, m2, 1)]
    pieces = pieces + [(1 - core, 0, n0, None), (1 - core, first, n1, None), (1 - core, second, n2, 0), (1 - core, 3, n2, 1)]
    for side, bits, p_ref, at in pieces:
        block = side * 4 + (ids_ref[4] ^ bits)
        start = pl.multiple_of(block * size, 16)
        col = 0

        def read(span):
            return (p_ref[:, col : col + span] if at is None else p_ref[at, :, col : col + span]).astype(single)

        for out_ref in outs:
            if len(out_ref.shape) == 4:
                for j in range(3):
                    span = out_ref.shape[3]
                    out_ref[block, j] = read(span)
                    col += span
            elif len(out_ref.shape) == 3:
                for j in range(2):
                    span = out_ref.shape[2]
                    out_ref[pl.ds(start, size), j, :] = read(span)
                    col += padded(span)
            else:
                span = out_ref.shape[1]
                out_ref[pl.ds(start, size), :] = read(span)
                col += padded(span)


def on_device(
    tokens,
    grad_out,
    lengths,
    deal,
    adapter_of,
    attention_gain,
    attention_proj,
    attention_out,
    feed_gain,
    feed_in,
    feed_out,
    attention_proj_down,
    attention_proj_up,
    attention_out_down,
    attention_out_up,
    feed_in_down,
    feed_in_up,
    feed_out_down,
    feed_out_up,
):
    fsdp_size = lax.axis_size("fsdp")
    context_size = lax.axis_size("context")
    tensor_size = lax.axis_size("tensor")
    count, width = tokens.shape
    total = deal.shape[0]
    sets, _, rank = attention_proj_down.shape
    ranks = sets * rank
    local_width = attention_proj.shape[2]
    hidden = feed_in.shape[2]
    f = lax.axis_index("fsdp")
    c = lax.axis_index("context")
    t = lax.axis_index("tensor")
    small = context_size == 2 and fsdp_size == 4
    half_at = c % 2
    chip = (f // 2) * 2 + half_at
    chunks = total // count
    if small:
        order = [(f ^ df) * context_size + (c ^ dc) for df, dc in
                 ((0, 0), (0, 1), (2, 0), (2, 1), (1, 0), (1, 1), (3, 0), (3, 1))]
    else:
        order = list(range(chunks))
    ids = jnp.stack([jnp.asarray(value, jnp.int32) for value in [f, half_at, t, f % 2, chip, *order]])
    quarter = count // tensor_size

    def over(axis, size, bit, value):
        return lax.ppermute(value, axis, swap_pairs(axis, size, bit))

    def near(value):
        return over("fsdp", fsdp_size, 1, value)

    def ahead(value):
        return over("fsdp", fsdp_size, 2, value)

    def across(value):
        return over("context", context_size, 1, value)

    def after(value, *others):
        return lax.optimization_barrier((value, *others))[0]

    def exchange(pieces):
        return [pieces[0]] + [over("tensor", tensor_size, k, pieces[k]) for k in range(1, tensor_size)]

    def spread(piece):
        far = over("tensor", tensor_size, 2, piece)
        return [piece, over("tensor", tensor_size, 1, piece), far, over("tensor", tensor_size, 1, far)]

    def reduce_rows(keep, send, *others):
        got = over("tensor", tensor_size, 1, send)
        got, *others = lax.optimization_barrier((got, *others))
        mine, passed = call(
            pair_body, [(keep.shape[1:], single), (keep.shape[1:], low)], ids, [keep, got], name="pair"
        )
        return [mine, over("tensor", tensor_size, 2, passed)], others

    proj_own = jnp.transpose(attention_proj, (1, 0, 2))
    in_own = jnp.transpose(feed_in, (1, 2, 0))
    proj_down = jnp.transpose(attention_proj_down, (0, 2, 1)).reshape(ranks, width)
    out_down_own = jnp.transpose(attention_out_down, (0, 2, 1)).reshape(ranks, local_width)
    in_down = jnp.transpose(feed_in_down, (0, 2, 1)).reshape(ranks, width)
    last_down = jnp.transpose(feed_out_down, (0, 2, 1)).reshape(ranks, hidden)
    proj_up = jnp.transpose(attention_proj_up, (2, 0, 1, 3)).reshape(3, ranks, local_width)
    out_up = attention_out_up.reshape(ranks, width)
    last_up = feed_out_up.reshape(ranks, width)

    proj_far = ahead(proj_own)
    proj_near = near(proj_own)
    in_half, last_half = call(
        split_body,
        [((1, *in_own.shape[1:]), low), ((hidden, feed_out.shape[1] // 2), low)],
        ids,
        [in_own, feed_out],
        name="split",
        cost=2.0,
    )
    in_far = ahead(in_half)

    seqs = lengths.shape[0]
    before = jnp.arange(seqs)[:, None] >= jnp.arange(seqs)[None, :]
    ends = jnp.sum(jnp.where(before, lengths[None, :], 0), axis=1)
    starts = ends - lengths
    segment_all = jnp.sum((deal[:, None] >= ends[None, :]).astype(jnp.int32), axis=1)
    first = (f * context_size + c) * count
    segment_rows = lax.dynamic_slice_in_dim(segment_all, first, count)
    deal_rows = lax.dynamic_slice_in_dim(deal, first, count)
    member = segment_rows[:, None] == jnp.arange(seqs, dtype=jnp.int32)[None, :]
    place = deal_rows - jnp.sum(jnp.where(member, starts[None, :], 0), axis=1)
    chosen = jnp.sum(jnp.where(member, adapter_of[None, :], 0), axis=1)
    set_of = jnp.arange(ranks, dtype=jnp.int32) // rank
    picked = (chosen[:, None] == set_of[None, :]).astype(low)
    half = HEAD_DIM // 2
    lane = jnp.arange(local_width, dtype=jnp.int32) % HEAD_DIM
    freq = jnp.exp((lane % half).astype(single) * (-math.log(rope_base) / half))
    angle = place.astype(single)[:, None] * freq[None, :]
    cos_full = jnp.cos(angle)
    sin_full = jnp.sin(angle) * jnp.where(lane < half, -1.0, 1.0).astype(single)[None, :]
    gain_one = attention_gain.astype(single)[None, :]
    gain_two = feed_gain.astype(single)[None, :]
    normed_one, adapted_q = call(
        prepare_body,
        [((count, width), low), ((count, ranks), low)],
        ids,
        [after(tokens, in_half), gain_one, proj_down, picked],
        name="prepare",
        cost=5.0,
    )

    packed = spread(jnp.concatenate([after(attention_out, in_half), out_down_own], axis=0))
    proj_w = [proj_own, proj_near, proj_far, near(proj_far)]
    groups = segment_all.reshape(-1, count)
    seg_col = segment_rows[:, None]
    normed_one, groups, seg_col, picked = lax.optimization_barrier((normed_one, groups, seg_col, picked))
    in_up = jnp.transpose(feed_in_up, (2, 0, 1, 3)).reshape(2, ranks, hidden)

    query, keyval = call(
        project_body,
        [((count, local_width), low), ((count, 2 * local_width), low)],
        ids,
        [normed_one, adapted_q, proj_up, cos_full, sin_full, *proj_w],
        name="project",
        cost=3.0,
    )

    def plane_gather(value, other=None):
        if not small:
            return [lax.all_gather(value, token_axes, axis=0, tiled=True)]
        corner = lax.ppermute(value, token_axes, swap_pairs(None, fsdp_size * context_size, 2 * context_size + 1))
        chips = [value, across(value), ahead(value), corner]
        if other is None:
            return chips + [near(piece) for piece in chips]
        return chips + [near(value)] + [near(after(piece, other)) for piece in chips[1:]]

    in_near = near(after(in_own, proj_near))
    keyval, in_far, in_near = lax.optimization_barrier((keyval, in_far, in_near))
    last_near = near(after(feed_out, in_near))
    keyval_all = plane_gather(keyval)
    parts_n = len(keyval_all)
    gathered = keyval_all[1:4]
    out_w_own, out_half = call(
        stack_body,
        [((width, local_width), low), ((width // 2, local_width), low)],
        ids,
        [after(packed[0], keyval), *packed[1:]],
        name="stack",
        cost=3.0,
    )
    in_up, gain_two, last_near = lax.optimization_barrier((after(in_up, keyval), gain_two, last_near))
    out_w_own, out_half, in_far, in_up, *gathered = lax.optimization_barrier(
        (out_w_own, out_half, in_far, in_up, *gathered)
    )
    out_near = near(out_w_own)
    out_far = ahead(out_half)
    in_rest = across(in_far)

    slab = pltpu.VMEM((count, local_width), single)
    held = block_rows(count, total) * (local_width // HEAD_DIM)
    many = pltpu.VMEM((held, local_width), low)
    against = pltpu.VMEM((held, total), low)
    heads_out, attended, lse_col, keyval_joined = call(
        lambda *refs: attend_body(parts_n, *refs),
        [
            ((count, local_width), low),
            ((count, local_width), single),
            ((count, 128), single),
            ((total, 2 * local_width), low),
        ],
        ids,
        [after(query, in_up, gain_two), seg_col, groups, *keyval_all],
        scratch=[many, pltpu.VMEM((held, total), single), pltpu.SemaphoreType.DMA((parts_n,))],
        far=range(3, 3 + parts_n),
        vmem=16 if small else 60,
        name="attend",
        cost=8.0,
    )
    heads_out, out_far, in_rest = lax.optimization_barrier((heads_out, out_far, in_rest))
    heads = spread(heads_out)
    last_far = ahead(after(last_half, heads_out))
    out_rest = across(out_far)
    last_rest = across(last_far)
    out_late, in_late, last_late, in_rest = after((out_far, in_far, last_far, in_rest), heads[1])
    out_w = [out_w_own, out_near, out_far, out_rest, near(out_late), near(out_rest)]
    in_w = [in_own, in_near, in_far, in_rest, near(in_late), near(in_rest)]
    last_w = [feed_out, last_near, last_far, last_rest, near(last_late), near(last_rest)]
    wide = width + ranks
    piece = ((2, quarter, wide), low)
    mid_outs = call(
        middle_body,
        [piece] * 2
        + [((count, ranks), low)] * 3
        + [
            ((count, width), low),
            ((count, hidden), low),
            ((2, count, hidden), low),
            ((quarter, width), single),
            ((4, width, local_width), low),
            ((4, *feed_out.shape), low),
        ],
        ids,
        [*heads, *out_w, *packed, out_up, tokens, gain_two, grad_out, picked, *in_w, in_down, in_up, *last_w,
         last_down, last_up],
        scratch=[
            pltpu.VMEM((count, wide), single),
            pltpu.VMEM((4, *in_own.shape), low),
            pltpu.SemaphoreType.DMA((18,)),
        ],
        far=(*range(4, 10), *range(19, 25), *range(27, 33)),
        vmem=20 if small else 60,
        name="middle",
    )
    adapted_o, adapted_i, grad_adapt_d, normed_two, activity, grad_gates, middle_q, out_all, last_all = mid_outs[2:]
    if small:
        query_late = after(query, activity)
        summed, (query_x, query_y, query_n) = reduce_rows(
            *mid_outs[:2], across(query_late), ahead(query_late), near(query_late)
        )
        query_xy = ahead(query_x)
        query_all = [query, query_x, query_y, query_xy, query_n, near(query_x), near(query_y)]
    else:
        summed, _ = reduce_rows(*mid_outs[:2])
        query_all = plane_gather(query)
    feed_pieces = call(
        feed_body,
        [piece] * 2,
        ids,
        [after(activity, summed[0]), last_down, last_all],
        scratch=[pltpu.VMEM((count, wide), single)],
        name="feed",
    )
    summed, query_all, feed_pieces = lax.optimization_barrier((summed, query_all, feed_pieces))
    turn = ((quarter, local_width + ranks), low)
    *turned, grad_mid, grad_branch, grad_adapt_i = call(
        turn_body,
        [turn] * 4 + [((quarter, width), single), ((quarter, width), low), ((quarter, ranks), low)],
        ids,
        [*summed, picked, in_down, middle_q, gain_two, grad_out, out_up, out_all, *packed],
        vmem=6 if small else 40,
        name="turn",
        cost=3.0,
    )
    if small:
        query_all = query_all + [near(after(query_all[3], grad_mid))]
    arrived = exchange(turned)
    sizes = [width] * 4 + [padded(hidden)] * 3 + [3 * local_width, local_width]
    columns = sum(sizes)
    places = [(i, j) for i in range(fsdp_size) for j in range(context_size)]
    number = {place: at for at, place in enumerate(places)}
    side = {(i, j): (i, j ^ 1) for i, j in places}
    front = {(i, j): (i ^ 2, j) for i, j in places}
    one = [(number[p], number[front[p] if p[0] % 2 else side[p]]) for p in places]
    two = [(number[p], number[side[p] if p[0] % 2 else front[p]]) for p in places]
    rows = ranks // 8

    def fold_strips(keep, send):
        columns = keep.shape[1]
        return call(
            fold_body,
            [((2, rows, columns), low)] * 2,
            ids,
            [keep, near(send)],
            scratch=[pltpu.VMEM((ranks // 2, columns), single)],
            name="fold",
            cost=3.0,
        )

    def reduce_strips(own, got):
        columns = own.shape[2]
        mine, passed = call(
            pair_body,
            [((rows, columns), single), ((rows, columns), low)],
            ids,
            [own, got],
            name="pair_chips",
            cost=3.0,
        )
        return [mine, lax.ppermute(passed, token_axes, two)]

    (feed_mine, feed_got), _ = reduce_rows(*feed_pieces)
    arrived, query_all, feed_mine = lax.optimization_barrier((arrived, query_all, feed_mine))
    tail = 32
    message, delta_col, grad_adapt_o = call(
        collect_body,
        [((count + tail, local_width), low), ((count, 128), single), ((count, ranks), low)],
        ids,
        [*arrived, attended, lse_col],
        name="collect",
        cost=3.0,
    )
    (grad_query,) = call(
        query_body,
        [((count, local_width), single)],
        ids,
        [query, message, lse_col, delta_col, seg_col, groups, keyval_joined],
        scratch=[many, many, against],
        vmem=12 if small else 60,
        name="queries",
        cost=7.0,
    )
    message_all = [value.reshape(-1, count + tail, local_width) for value in plane_gather(message, grad_query)]
    output_q, adapted_d = call(
        out_body,
        [((quarter, width), low), ((quarter, ranks), low)],
        ids,
        [feed_mine, after(feed_got, grad_query), picked, middle_q, last_up],
        name="outputs",
    )
    output_all = spread(output_q)
    *last_pieces, grad_proj, part_adapt_q = call(
        lambda *refs: key_body(parts_n, *refs),
        [piece] * 2 + [((count, 3 * local_width), low), ((count, ranks), low)],
        ids,
        [after(keyval, output_q), seg_col, groups, grad_query, cos_full, sin_full, proj_up, picked, *proj_w, *query_all, *message_all],
        scratch=[
            pltpu.VMEM((8, total), single),
            slab,
            slab,
            pltpu.VMEM((count, wide), single),
            many,
            many,
            against,
            against,
            pltpu.VMEM((total, local_width), low),
            pltpu.VMEM((chunks, count, local_width), low),
            pltpu.VMEM((chunks, tail, local_width), low),
            pltpu.SemaphoreType.DMA((3 * parts_n,)),
        ],
        far=range(12, 12 + 2 * parts_n),
        vmem=22 if small else 60,
        name="keys",
        cost=10.0,
    )
    (last_mine, last_got), (out_two,) = reduce_rows(*last_pieces, output_all[2])
    output_all[2] = out_two
    late = call(
        grads_body,
        [((ranks // 2, columns), low)] * 2,
        ids,
        [grad_adapt_i, normed_two, adapted_o, grad_branch, adapted_d, grad_out,
         part_adapt_q, normed_one, adapted_i,
         grad_gates, grad_adapt_d, activity, adapted_q, grad_proj, grad_adapt_o, heads_out],
        scratch=[pltpu.VMEM((ranks, columns), single)],
        vmem=8 if small else 40,
        name="grads",
        cost=3.0,
    )
    (grad_tokens_q,) = call(
        last_body,
        [((quarter, width), low)],
        ids,
        [last_mine, last_got, picked, proj_down, tokens, gain_one, grad_mid],
        name="last",
    )
    finals = [((ranks, width), single)] * 4 + [((ranks, 2, hidden), single), ((ranks, hidden), single)]
    finals = finals + [((sets, 3, rank, local_width), single), ((ranks, local_width), single)]
    if small:
        late_own, late_out = fold_strips(*late)
        late_mine, late_got = reduce_strips(after(late_own, last_mine), lax.ppermute(late_out, token_axes, one))
        shared, rest = call(
            total_body,
            [((rows, 4 * width), low), ((rows, columns - 4 * width), low)],
            ids,
            [late_mine, after(late_got, last_got)],
            name="total",
        )
        (shared,) = call(
            add_body, [((rows, 4 * width), low)], ids, [shared, over("tensor", tensor_size, 1, shared)], name="add"
        )
        shared_far = over("tensor", tensor_size, 2, shared)
        tokens_all = spread(after(grad_tokens_q, shared))
        (output,) = call(assemble_body, [((count, width), low)], ids, output_all, name="join_output")
        rest, output = lax.optimization_barrier((rest, output))
        (joined,) = call(
            join_body,
            [((rows, columns), low)],
            ids,
            [shared, shared_far, rest],
            name="join",
        )
        beside = lax.ppermute(joined, token_axes, two)
        both = jnp.stack([joined, after(beside, tokens_all[1], tokens_all[2])])
        others = lax.ppermute(both, token_axes, one)
        strips = [joined, beside, after(others, tokens_all[3])]
        strips = strips + [near(value) for value in strips]
        results = call(finish_body, finals, ids, strips, name="finish")
    else:
        tokens_all = spread(grad_tokens_q)
        (output,) = call(assemble_body, [((count, width), low)], ids, output_all, name="join_output")
        pair = jnp.where(f % 2 == 0, jnp.concatenate(late), jnp.concatenate(late[::-1]))
        pair = lax.psum(pair, token_axes)
        joined = jnp.concatenate([lax.psum(pair[:, : 4 * width], "tensor"), pair[:, 4 * width :]], axis=1)
        cut = [0]
        for span in [width] * 4 + [padded(hidden)] * 3 + [3 * local_width, local_width]:
            cut.append(cut[-1] + span)
        slices = [joined[:, lo:hi].astype(single) for lo, hi in zip(cut, cut[1:])]
        *results, gate_up, mult_up, last_grad, proj_up_grad, out_down_grad = slices
        results = [*results, jnp.stack([gate_up[:, :hidden], mult_up[:, :hidden]], axis=1), last_grad[:, :hidden]]
        proj_up_grad = jnp.transpose(proj_up_grad.reshape(sets, rank, 3, local_width), (0, 2, 1, 3))
        results = [*results, proj_up_grad, out_down_grad]

    in_down_grad, out_up_grad, last_up_grad, proj_down_grad, in_up_grad, last_grad, proj_up_grad, out_down_grad = results
    (grad_tokens,) = call(assemble_body, [((count, width), low)], ids, tokens_all, name="join_tokens")


    def down(grad):
        return jnp.transpose(grad.reshape(sets, rank, -1), (0, 2, 1))

    return (
        output,
        grad_tokens,
        down(proj_down_grad),
        jnp.transpose(proj_up_grad, (0, 2, 1, 3)),
        down(out_down_grad),
        out_up_grad.reshape(sets, rank, width),
        down(in_down_grad),
        in_up_grad.reshape(sets, rank, 2, hidden),
        down(last_grad),
        last_up_grad.reshape(sets, rank, width),
    )


def solution(mesh):
    return jax.shard_map(
        on_device,
        mesh=mesh,
        in_specs=(
            P(("fsdp", "context"), None),
            P(("fsdp", "context"), None),
            P(),
            P(),
            P(),
            P(),
            P("fsdp", None, "tensor"),
            P("tensor", "fsdp"),
            P(),
            P("fsdp", None, "tensor"),
            P("tensor", "fsdp"),
            P(),
            P(None, None, None, "tensor"),
            P(None, "tensor", None),
            P(),
            P(),
            P(None, None, None, "tensor"),
            P(None, "tensor", None),
            P(),
        ),
        out_specs=(
            P(("fsdp", "context"), None),
            P(("fsdp", "context"), None),
            P(),
            P(None, None, None, "tensor"),
            P(None, "tensor", None),
            P(),
            P(),
            P(None, None, None, "tensor"),
            P(None, "tensor", None),
            P(),
        ),
        check_vma=False,
    )
```

```python
import math

import jax
import jax.numpy as jnp
from jax import lax
from jax.experimental import pallas as pl
from jax.experimental.pallas import tpu as pltpu
from jax.sharding import PartitionSpec as P

HEAD_DIM = 64


rope_base = 160000.0
epsilon = 1e-05
negative = -1e30
single = jnp.float32
low = jnp.bfloat16
scale = HEAD_DIM ** (-0.5)
token_axes = ("fsdp", "context")
every_axis = ("fsdp", "context", "tensor")


def nn(left, right):
    return lax.dot_general(
        left, right, (((1,), (0,)), ((), ())), preferred_element_type=jnp.float32
    )


def nt(left, right):
    return lax.dot_general(
        left, right, (((1,), (1,)), ((), ())), preferred_element_type=jnp.float32
    )


def tn(left, right):
    return lax.dot_general(
        left, right, (((0,), (0,)), ((), ())), preferred_element_type=jnp.float32
    )


def call(body, outs, ids, args, scratch=(), vmem=6, name=None, far=(), cost=0.0):
    whole = pl.BlockSpec(memory_space=pltpu.VMEM)
    return pl.pallas_call(
        body,
        out_shape=[jax.ShapeDtypeStruct(shape, kind) for shape, kind in outs],
        in_specs=[pl.BlockSpec(memory_space=pltpu.SMEM)]
        + [pl.BlockSpec(memory_space=pltpu.HBM) if at in far else whole for at in range(len(args))],
        out_specs=[whole] * len(outs),
        scratch_shapes=list(scratch),
        compiler_params=pltpu.CompilerParams(vmem_limit_bytes=vmem << 20),
        cost_estimate=pl.CostEstimate(flops=int(cost * 1e12) + 1, bytes_accessed=int(cost * 1e12) + 1, transcendentals=0),
        name=name,
    )(ids, *args)


def swap_pairs(axis, size, bit):
    return [(i, i ^ bit) for i in range(size)]


def layer_norm_rows(values):
    centered = values - jnp.mean(values, axis=1, keepdims=True)
    rstd = lax.rsqrt(jnp.mean(centered * centered, axis=1, keepdims=True) + epsilon)
    return (centered * rstd, rstd)


def layer_norm_back(upstream, gain, xhat, rstd):
    scaled = upstream * gain
    return rstd * (
        scaled
        - jnp.mean(scaled, axis=1, keepdims=True)
        - xhat * jnp.mean(scaled * xhat, axis=1, keepdims=True)
    )


def swap_halves(u):
    width = u.shape[1]
    half = HEAD_DIM // 2
    lane = lax.broadcasted_iota(jnp.int32, (1, width), 1)
    return jnp.where(
        lane % HEAD_DIM < half, pltpu.roll(u, width - half, 1), pltpu.roll(u, half, 1)
    )


def head_row(width, head):
    lane = lax.broadcasted_iota(jnp.int32, (1, width), 1)
    return (lane // HEAD_DIM == head).astype(single)


def start_copies(pairs, sems):
    copies = [pltpu.make_async_copy(src, dst, sems.at[n]) for n, (src, dst) in enumerate(pairs)]
    for copy in copies:
        copy.start()
    return copies


def loop(count, step, most=8):
    if count <= most:
        for number in range(count):
            step(number)
    else:

        def inner(number, carry):
            step(number)
            return carry

        lax.fori_loop(0, count, inner, 0)


def at_block(number, size):
    start = number * size
    return pl.ds(start if isinstance(start, int) else pl.multiple_of(start, 16), size)


def block_rows(count, total):
    return max(16, min(count, 2048 * count // total))


def cols_of(ids_ref, k, width):
    return pl.ds(pl.multiple_of((ids_ref[0] ^ k) * width, 128), width)


def rows_of(ids_ref, k, height):
    return pl.ds(pl.multiple_of((ids_ref[2] ^ k) * height, 16), height)


def join_rows(ids_ref, dst_ref, mine_ref, other_ref):
    size = mine_ref.shape[0]
    dst_ref[pl.ds(ids_ref[1] * size, size)] = mine_ref[...]
    dst_ref[pl.ds((1 - ids_ref[1]) * size, size)] = other_ref[...]


def join_cols(ids_ref, dst_ref, mine_ref, other_ref):
    size = mine_ref.shape[1]
    dst_ref[:, pl.ds(pl.multiple_of(ids_ref[1] * size, 128), size)] = mine_ref[...]
    dst_ref[:, pl.ds(pl.multiple_of((1 - ids_ref[1]) * size, 128), size)] = other_ref[...]


def project_body(ids_ref, x_ref, aq_ref, up_ref, cos_ref, sin_ref, *refs):
    weights, q_ref, kv_ref = (refs[:-2], refs[-2], refs[-1])
    part = weights[0].shape[1]
    width = weights[0].shape[2]
    for j in range(3):
        acc = nn(aq_ref[...], up_ref[j])
        for k, w_ref in enumerate(weights):
            acc = acc + nn(x_ref[:, cols_of(ids_ref, k, part)], w_ref[j])
        if j < 2:
            acc = acc * cos_ref[...] + swap_halves(acc) * sin_ref[...]
        if j == 0:
            q_ref[...] = acc.astype(low)
        else:
            kv_ref[:, (j - 1) * width : j * width] = acc.astype(low)


def prepare_body(ids_ref, tokens_ref, gain_ref, down_ref, picked_ref, n1_ref, aq_ref):
    xhat, _ = layer_norm_rows(tokens_ref[...].astype(single))
    normed = (xhat * gain_ref[...]).astype(low)
    n1_ref[...] = normed
    aq_ref[...] = (picked_ref[...].astype(single) * nt(normed, down_ref[...])).astype(low)


def split_body(ids_ref, in_ref, last_ref, ihalf_ref, lhalf_ref):
    ihalf_ref[...] = in_ref[pl.ds(ids_ref[1], 1)]
    cols = lhalf_ref.shape[1]
    lhalf_ref[...] = last_ref[:, pl.ds(pl.multiple_of(ids_ref[1] * cols, 128), cols)]


def stack_body(ids_ref, p0, p1, p2, p3, full_ref, half_ref):
    rows = p0.shape[1]
    for k, p_ref in enumerate([p0, p1, p2, p3]):
        full_ref[k * rows : (k + 1) * rows, :] = p_ref[:rows, :]
    size = half_ref.shape[0]
    half_ref[...] = full_ref[pl.ds(pl.multiple_of(ids_ref[1] * size, 16), size), :]


def put_pieces(ids_ref, wide_ref, keep_ref, send_ref):
    quarter = keep_ref.shape[1]
    for at, (ref, k) in enumerate([(keep_ref, 0), (keep_ref, 2), (send_ref, 1), (send_ref, 3)]):
        ref[at % 2] = wide_ref[rows_of(ids_ref, k, quarter), :].astype(low)


def pair_body(ids_ref, keep_ref, got_ref, mine_ref, pass_ref):
    mine_ref[...] = keep_ref[0].astype(single) + got_ref[0].astype(single)
    pass_ref[...] = (keep_ref[1].astype(single) + got_ref[1].astype(single)).astype(low)


def attend_body(parts_n, ids_ref, q_ref, segc_ref, groups_ref, *refs):
    parts = refs[:parts_n]
    heads_ref, att_ref, lcol_ref, kv_ref, many_ref, s_ref, sems = refs[parts_n:]
    count, width = q_ref.shape
    heads = width // HEAD_DIM
    chunk = groups_ref.shape[1]
    size = many_ref.shape[0] // heads
    base = 0
    pairs = []
    for part in parts:
        pairs.append((part, kv_ref.at[base : base + part.shape[0], :]))
        base += part.shape[0]
    copies = start_copies(pairs, sems)
    lane = lax.broadcasted_iota(jnp.int32, (1, 128), 1)
    waits = list(copies)

    def block(number):
        rows = at_block(number, size)
        for h in range(heads):
            many_ref[h * size : (h + 1) * size, :] = q_ref[rows, :] * (head_row(width, h) * scale).astype(low)

        def scores(j):
            if isinstance(j, int) and waits and len(copies) > 1:
                waits.pop(0).wait()
            cols = at_block(j, chunk)
            same = segc_ref[rows, :] == groups_ref[pl.ds(ids_ref[5 + j], 1), :]
            s = nt(many_ref[...], kv_ref[cols, :width])
            for h in range(heads):
                s_ref[h * size : (h + 1) * size, cols] = jnp.where(same, s[h * size : (h + 1) * size], negative)

        if len(copies) == 1 and waits:
            waits.pop(0).wait()
        loop(base // chunk, scores)
        total = jnp.zeros((size, width), single)
        lcol = jnp.zeros((size, 128), single)
        for h in range(heads):
            s = s_ref[h * size : (h + 1) * size, :]
            top = jnp.max(s, axis=1, keepdims=True)
            p = jnp.exp(s - top)
            mass = jnp.sum(p, axis=1, keepdims=True)
            total = total + nn(p.astype(low), kv_ref[:, width:]) * (head_row(width, h) / mass)
            lcol = jnp.where(lane == h, top + jnp.log(mass), lcol)
        att_ref[rows, :] = total
        lcol_ref[rows, :] = lcol
        heads_ref[rows, :] = total.astype(low)

    loop(count // size, block, 1)


def middle_body(ids_ref, *refs):
    heads = refs[0:4]
    wown, wnear, wa, wb, wc, wd = refs[4:10]
    packs = refs[10:14]
    refs = refs[3:]
    ou_ref, tokens_ref, gain_ref, go_ref, picked_ref = refs[11:16]
    iown, inear, ia, ib, ic, idd = refs[16:22]
    idn_ref, iu_ref = refs[22:24]
    lown, lnear, la, lb, lc, ld = refs[24:30]
    ldn_ref, lup_ref = refs[30:32]
    keep_ref, send_ref, ao_ref, ai_ref, gad_ref, n2_ref, act_ref, gg_ref, mid_ref, wts, lts = refs[32:43]
    wide_ref, its, sems = refs[43:]
    mine, rest = (ids_ref[1], 1 - ids_ref[1])
    half = wa.shape[0]
    step = la.shape[1]

    def rows(k, at):
        return wts.at[k, pl.ds(pl.multiple_of(at * half, 16), half), :]

    def cols(k, at):
        return lts.at[k, :, pl.ds(pl.multiple_of(at * step, 128), step)]

    pairs = [
        (wown, wts.at[0]),
        (wnear, wts.at[1]),
        (wa, rows(2, mine)),
        (wb, rows(2, rest)),
        (wc, rows(3, mine)),
        (wd, rows(3, rest)),
        (iown, its.at[0]),
        (inear, its.at[1]),
        (ia, its.at[2, pl.ds(mine, 1)]),
        (ib, its.at[2, pl.ds(rest, 1)]),
        (ic, its.at[3, pl.ds(mine, 1)]),
        (idd, its.at[3, pl.ds(rest, 1)]),
        (lown, lts.at[0]),
        (lnear, lts.at[1]),
        (la, cols(2, mine)),
        (lb, cols(2, rest)),
        (lc, cols(3, mine)),
        (ld, cols(3, rest)),
    ]
    copies = [pltpu.make_async_copy(src, dst, sems.at[n]) for n, (src, dst) in enumerate(pairs)]
    for copy in copies:
        copy.start()
    h0 = heads[0]
    w0 = wown
    outs_w = [wts.at[k] for k in range(4)]
    ins_w = [its.at[k] for k in range(4)]
    lasts_w = [lts.at[k] for k in range(4)]
    part = w0.shape[1]
    span = h0.shape[1]
    width = tokens_ref.shape[1]
    picked = picked_ref[...].astype(single)
    span = h0.shape[1]
    adapt = nt(h0[...], packs[0][span:, :])
    for k in range(1, len(heads)):
        adapt = adapt + nt(heads[k][...], packs[k][span:, :])
    ao = (picked * adapt).astype(low)
    ao_ref[...] = ao
    for copy in copies[:6]:
        copy.wait()
    for k, w_ref in enumerate(outs_w):
        acc = nn(h0[...], w_ref[:span, :])
        for r in range(1, len(heads)):
            acc = acc + nn(heads[r][...], w_ref[r * span : (r + 1) * span, :])
        wide_ref[:, cols_of(ids_ref, k, part)] = acc
    middle = tokens_ref[...].astype(single) + wide_ref[:, :width] + nn(ao, ou_ref[...])
    wide_ref[:, :width] = middle
    quarter = mid_ref.shape[0]
    mid_ref[...] = wide_ref[rows_of(ids_ref, 0, quarter), :width]
    xhat, _ = layer_norm_rows(middle)
    n2 = (xhat * gain_ref[...]).astype(low)
    n2_ref[...] = n2
    ai = (picked * nt(n2, idn_ref[...])).astype(low)
    ai_ref[...] = ai
    for copy in copies[6:12]:
        copy.wait()
    gate = nn(ai, iu_ref[0])
    mult = nn(ai, iu_ref[1])
    for k, w_ref in enumerate(ins_w):
        x = n2_ref[:, cols_of(ids_ref, k, part)]
        gate = gate + nt(x, w_ref[0])
        mult = mult + nt(x, w_ref[1])
    phi = 0.5 * (1.0 + lax.erf(gate * (2.0**-0.5)))
    gated = gate * phi
    act_ref[...] = (gated * mult).astype(low)
    slope = phi + gate * jnp.exp(-0.5 * gate * gate) * (1.0 / math.sqrt(2.0 * math.pi))
    go = go_ref[...]
    gad = (nt(go, lup_ref[...]).astype(low).astype(single) * picked).astype(low)
    gad_ref[...] = gad
    for copy in copies[12:]:
        copy.wait()
    ga = nn(gad, ldn_ref[...])
    for k, w_ref in enumerate(lasts_w):
        ga = ga + nt(go_ref[:, cols_of(ids_ref, k, part)], w_ref[...])
    gg0 = (slope * (ga * mult)).astype(low)
    gg1 = (ga * gated).astype(low)
    gg_ref[0] = gg0
    gg_ref[1] = gg1
    for k, w_ref in enumerate(ins_w):
        wide_ref[:, cols_of(ids_ref, k, part)] = nn(gg0, w_ref[0]) + nn(gg1, w_ref[1])
    wide_ref[:, width:] = nt(gg0, iu_ref[0]) + nt(gg1, iu_ref[1])
    put_pieces(ids_ref, wide_ref, keep_ref, send_ref)


def feed_body(ids_ref, act_ref, ldn_ref, lts, keep_ref, send_ref, wide_ref):
    part = lts.shape[2]
    act = act_ref[...]
    wide_ref[:, wide_ref.shape[1] - ldn_ref.shape[0] :] = nt(act, ldn_ref[...])
    for k in range(4):
        wide_ref[:, cols_of(ids_ref, k, part)] = nn(act, lts[k])
    put_pieces(ids_ref, wide_ref, keep_ref, send_ref)


def turn_body(
    ids_ref, p0, p1, picked_ref, idn_ref, mid_ref, gain_ref, go_ref, ou_ref, wts, d0, d1, d2, d3,
    a0, a1, a2, a3, gm_ref, gb_ref, gai_ref,
):
    quarter = p0.shape[0]
    width = mid_ref.shape[1]
    part = wts.shape[2]
    rows = rows_of(ids_ref, 0, quarter)
    picked = picked_ref[rows, :].astype(single)
    total = p0[...] + p1[...].astype(single)
    gai = (total[:, width:].astype(low).astype(single) * picked).astype(low)
    gai_ref[...] = gai
    upstream = total[:, :width] + nn(gai, idn_ref[...])
    xhat, rstd = layer_norm_rows(mid_ref[...])
    gm = go_ref[rows, :].astype(single) + layer_norm_back(upstream, gain_ref[...], xhat, rstd)
    gm_ref[...] = gm
    gb = gm.astype(low)
    gb_ref[...] = gb
    gao = (nt(gb, ou_ref[...]).astype(low).astype(single) * picked).astype(low)
    span = d0.shape[1]
    grads = [nn(gao, d_ref[span:, :]) for d_ref in (d0, d1, d2, d3)]
    for k in range(4):
        w_ref = wts.at[k]
        x = gb_ref[:, cols_of(ids_ref, k, part)]
        for r in range(4):
            grads[r] = grads[r] + nt(x, w_ref[r * span : (r + 1) * span, :])
    for k, a_ref in enumerate([a0, a1, a2, a3]):
        a_ref[:, :span] = grads[k].astype(low)
        a_ref[:, span:] = gao


def out_body(ids_ref, p0, p1, picked_ref, mid_ref, lup_ref, out_ref, ad_ref):
    width = mid_ref.shape[1]
    picked = picked_ref[rows_of(ids_ref, 0, p0.shape[0]), :].astype(single)
    total = p0[...] + p1[...].astype(single)
    ad = (picked * total[:, width:]).astype(low)
    ad_ref[...] = ad
    out_ref[...] = (mid_ref[...] + total[:, :width] + nn(ad, lup_ref[...])).astype(low)


def collect_body(ids_ref, a0, a1, a2, a3, att_ref, lcol_ref, msg_ref, dcol_ref, gao_ref):
    quarter = a0.shape[0]
    count, width = att_ref.shape
    for k, a_ref in enumerate([a0, a1, a2, a3]):
        msg_ref[rows_of(ids_ref, k, quarter), :] = a_ref[:, :width]
        gao_ref[rows_of(ids_ref, k, quarter), :] = a_ref[:, width:]
    both = msg_ref[:count, :].astype(single) * att_ref[...]
    heads = width // HEAD_DIM
    lane = lax.broadcasted_iota(jnp.int32, (1, 128), 1)
    dcol = jnp.zeros((count, 128), single)
    pair = lcol_ref[...]
    for h in range(heads):
        delta = jnp.sum(both * head_row(width, h), axis=1, keepdims=True)
        dcol = jnp.where(lane == h, delta, dcol)
        pair = jnp.where(lane == heads + h, delta, pair)
    dcol_ref[...] = dcol
    rows = jnp.transpose(pair)[:8, :]
    first = rows.astype(low).astype(single)
    rest = rows - first
    second = rest.astype(low).astype(single)
    third = rest - second
    tail = jnp.concatenate([first, second, third, jnp.zeros_like(first)], axis=0)
    msg_ref[count:, :] = tail.astype(low)


def query_body(
    ids_ref, q_ref, msg_ref, lcol_ref, dcol_ref, segc_ref, groups_ref, kv_ref, dq_ref, many_ref, more_ref, ds_ref
):
    count, width = q_ref.shape
    heads = width // HEAD_DIM
    chunk = groups_ref.shape[1]
    size = many_ref.shape[0] // heads

    def block(number):
        rows = at_block(number, size)
        for h in range(heads):
            many_ref[h * size : (h + 1) * size, :] = q_ref[rows, :] * (head_row(width, h) * scale).astype(low)
            more_ref[h * size : (h + 1) * size, :] = msg_ref[rows, :] * head_row(width, h).astype(low)

        def scores(j):
            cols = at_block(j, chunk)
            same = segc_ref[rows, :] == groups_ref[pl.ds(ids_ref[5 + j], 1), :]
            s = nt(many_ref[...], kv_ref[cols, :width])
            dp = nt(more_ref[...], kv_ref[cols, width:])
            for h in range(heads):
                mine = slice(h * size, (h + 1) * size)
                p = jnp.exp(jnp.where(same, s[mine] - lcol_ref[rows, h : h + 1], negative))
                ds_ref[mine, cols] = (p * (dp[mine] - dcol_ref[rows, h : h + 1])).astype(low)

        loop(kv_ref.shape[0] // chunk, scores)
        dq = nn(ds_ref[...], kv_ref[:, :width])
        total = jnp.zeros((size, width), single)
        for h in range(heads):
            total = total + dq[h * size : (h + 1) * size] * (head_row(width, h) * scale)
        dq_ref[rows, :] = total

    loop(count // size, block, 1)


def key_body(
    parts_n, ids_ref, own_ref, segc_ref, groups_ref, dq_ref, cos_ref, sin_ref, up_ref, picked_ref, w0, w1, w2, w3, *refs
):
    parts = refs[:parts_n]
    msgs = refs[parts_n : 2 * parts_n]
    keep_ref, send_ref, gp_ref, paq_ref, stat_ref, dk_ref, dv_ref, wide_ref, many_ref, more_ref, p_ref, ds_ref = refs[
        2 * parts_n : 2 * parts_n + 12
    ]
    q_ref, do_ref, tail_ref, sems = refs[2 * parts_n + 12 :]
    count = own_ref.shape[0]
    width = dq_ref.shape[1]
    heads = width // HEAD_DIM
    base = 0
    pairs = []
    for part, msg in zip(parts, msgs):
        held = msg.shape[0]
        pairs.append((part, q_ref.at[base * count : (base + held) * count, :]))
        pairs.append((msg.at[:, :count, :], do_ref.at[base : base + held]))
        pairs.append((msg.at[:, count:, :], tail_ref.at[base : base + held]))
        base += held
    copies = start_copies(pairs, sems)
    for copy in copies:
        copy.wait()
    for j in range(base):
        e = tail_ref[j].astype(single)
        stat_ref[:, j * count : (j + 1) * count] = e[:8] + e[8:16] + e[16:24]

    size = many_ref.shape[0] // heads

    def block(number):
        rows = at_block(number, size)
        for h in range(heads):
            hm = head_row(width, h)
            many_ref[h * size : (h + 1) * size, :] = own_ref[rows, :width] * (hm * scale).astype(low)
            more_ref[h * size : (h + 1) * size, :] = own_ref[rows, width:] * hm.astype(low)

        def scores(j):
            cols = at_block(j, count)
            same = segc_ref[rows, :] == groups_ref[pl.ds(ids_ref[5 + j], 1), :]
            s = nt(many_ref[...], q_ref[cols, :])
            dp = nt(more_ref[...], do_ref[j])
            for h in range(heads):
                mine = slice(h * size, (h + 1) * size)
                p = jnp.exp(jnp.where(same, s[mine] - stat_ref[h : h + 1, cols], negative))
                p_ref[mine, cols] = p.astype(low)
                ds_ref[mine, cols] = (p * (dp[mine] - stat_ref[heads + h : heads + h + 1, cols])).astype(low)

        loop(base, scores)
        dv = nn(p_ref[...], do_ref[...].reshape(base * count, width))
        dk = nn(ds_ref[...], q_ref[...])
        dv_total = jnp.zeros((size, width), single)
        dk_total = jnp.zeros((size, width), single)
        for h in range(heads):
            hm = head_row(width, h)
            dv_total = dv_total + dv[h * size : (h + 1) * size] * hm
            dk_total = dk_total + dk[h * size : (h + 1) * size] * (hm * scale)
        dv_ref[rows, :] = dv_total
        dk_ref[rows, :] = dk_total

    loop(count // size, block, 1)
    cosine = cos_ref[...]
    sine = sin_ref[...]
    gq = (dq_ref[...] * cosine - swap_halves(dq_ref[...]) * sine).astype(low)
    gk = (dk_ref[...] * cosine - swap_halves(dk_ref[...]) * sine).astype(low)
    gv = dv_ref[...].astype(low)
    gp_ref[:, :width] = gq
    gp_ref[:, width : 2 * width] = gk
    gp_ref[:, 2 * width :] = gv
    part = w0.shape[1]
    full = wide_ref.shape[1] - up_ref.shape[1]
    for k, w_ref in enumerate([w0, w1, w2, w3]):
        wide_ref[:, cols_of(ids_ref, k, part)] = nt(gq, w_ref[0]) + nt(gk, w_ref[1]) + nt(gv, w_ref[2])
    adapt = nt(gq, up_ref[0]) + nt(gk, up_ref[1]) + nt(gv, up_ref[2])
    wide_ref[:, full:] = adapt
    paq_ref[...] = (adapt * picked_ref[...].astype(single)).astype(low)
    put_pieces(ids_ref, wide_ref, keep_ref, send_ref)


def last_body(ids_ref, p0, p1, picked_ref, pdn_ref, tokens_ref, gain_ref, gm_ref, gt_ref):
    quarter = p0.shape[0]
    width = gm_ref.shape[1]
    rows = rows_of(ids_ref, 0, quarter)
    picked = picked_ref[rows, :].astype(single)
    total = p0[...] + p1[...].astype(single)
    gaq = (total[:, width:].astype(low).astype(single) * picked).astype(low)
    upstream = total[:, :width] + nn(gaq, pdn_ref[...])
    xhat, rstd = layer_norm_rows(tokens_ref[rows, :].astype(single))
    gt_ref[...] = (gm_ref[...] + layer_norm_back(upstream, gain_ref[...], xhat, rstd)).astype(low)


def assemble_body(ids_ref, p0, p1, p2, p3, out_ref):
    quarter = p0.shape[0]
    width = out_ref.shape[1]
    for k, p_ref in enumerate([p0, p1, p2, p3]):
        out_ref[rows_of(ids_ref, k, quarter), :] = p_ref[:, :width]


def padded(size):
    return -(-size // 128) * 128


def lay_out(ids_ref, values, keep_ref, send_ref, all_ref):
    ranks = all_ref.shape[0]
    at = 0
    for value in values:
        size = value.shape[1]
        all_ref[:, at : at + size] = value
        if padded(size) != size:
            all_ref[:, at + size : at + padded(size)] = jnp.zeros((ranks, padded(size) - size), single)
        at += padded(size)
    half = ranks // 2
    keep_ref[...] = all_ref[pl.ds(pl.multiple_of(ids_ref[3] * half, 16), half), :].astype(low)
    send_ref[...] = all_ref[pl.ds(pl.multiple_of((1 - ids_ref[3]) * half, 16), half), :].astype(low)


def grads_body(
    ids_ref, gai_ref, n2_ref, ao_ref, gb_ref, ad_ref, go_ref, paq_ref, n1_ref, ai_ref, gg_ref, gad_ref, act_ref,
    aq_ref, gp_ref, gao_ref, heads_ref, keep_ref, send_ref, all_ref,
):
    rows = rows_of(ids_ref, 0, gb_ref.shape[0])
    values = [
        tn(gai_ref[...], n2_ref[rows, :]),
        tn(ao_ref[rows, :], gb_ref[...]),
        tn(ad_ref[...], go_ref[rows, :]),
        tn(paq_ref[...], n1_ref[...]),
        tn(ai_ref[...], gg_ref[0]),
        tn(ai_ref[...], gg_ref[1]),
        tn(gad_ref[...], act_ref[...]),
        tn(aq_ref[...], gp_ref[...]),
        tn(gao_ref[...], heads_ref[...]),
    ]
    lay_out(ids_ref, values, keep_ref, send_ref, all_ref)


def fold_body(ids_ref, keep_ref, got_ref, own_ref, send_ref, sum_ref):
    sum_ref[...] = keep_ref[...].astype(single) + got_ref[...].astype(single)
    size = own_ref.shape[1]
    first = 1 + ids_ref[3]
    second = 2 - ids_ref[3]
    for at, (ref, bits) in enumerate([(own_ref, 0), (own_ref, second), (send_ref, first), (send_ref, 3)]):
        block = ids_ref[4] ^ bits
        ref[at % 2] = sum_ref[pl.ds(pl.multiple_of(block * size, 16), size), :].astype(low)


def total_body(ids_ref, mine_ref, got_ref, z_ref, r_ref):
    total = mine_ref[...] + got_ref[...].astype(single)
    shared = z_ref.shape[1]
    z_ref[...] = total[:, :shared].astype(low)
    r_ref[...] = total[:, shared:].astype(low)


def add_body(ids_ref, own_ref, got_ref, out_ref):
    out_ref[...] = (own_ref[...].astype(single) + got_ref[...].astype(single)).astype(low)


def join_body(ids_ref, own_ref, got_ref, r_ref, out_ref):
    shared = own_ref.shape[1]
    out_ref[:, :shared] = (own_ref[...].astype(single) + got_ref[...].astype(single)).astype(low)
    out_ref[:, shared:] = r_ref[...]


def assemble_body(ids_ref, p0, p1, p2, p3, out_ref):
    quarter = p0.shape[0]
    width = out_ref.shape[1]
    for k, p_ref in enumerate([p0, p1, p2, p3]):
        out_ref[rows_of(ids_ref, k, quarter), :] = p_ref[:, :width]


def padded(size):
    return -(-size // 128) * 128


def finish_body(ids_ref, *refs):
    m0, m1, m2, n0, n1, n2 = refs[:6]
    outs = refs[6:]
    size = m0.shape[0]
    core = ids_ref[3]
    first = 1 + core
    second = 2 - core
    pieces = [(core, 0, m0, None), (core, second, m1, None), (core, first, m2, 0), (core, 3, m2, 1)]
    pieces = pieces + [(1 - core, 0, n0, None), (1 - core, first, n1, None), (1 - core, second, n2, 0), (1 - core, 3, n2, 1)]
    for side, bits, p_ref, at in pieces:
        block = side * 4 + (ids_ref[4] ^ bits)
        start = pl.multiple_of(block * size, 16)
        col = 0

        def read(span):
            return (p_ref[:, col : col + span] if at is None else p_ref[at, :, col : col + span]).astype(single)

        for out_ref in outs:
            if len(out_ref.shape) == 4:
                for j in range(3):
                    span = out_ref.shape[3]
                    out_ref[block, j] = read(span)
                    col += span
            elif len(out_ref.shape) == 3:
                for j in range(2):
                    span = out_ref.shape[2]
                    out_ref[pl.ds(start, size), j, :] = read(span)
                    col += padded(span)
            else:
                span = out_ref.shape[1]
                out_ref[pl.ds(start, size), :] = read(span)
                col += padded(span)


def on_device(
    tokens,
    grad_out,
    lengths,
    deal,
    adapter_of,
    attention_gain,
    attention_proj,
    attention_out,
    feed_gain,
    feed_in,
    feed_out,
    attention_proj_down,
    attention_proj_up,
    attention_out_down,
    attention_out_up,
    feed_in_down,
    feed_in_up,
    feed_out_down,
    feed_out_up,
):
    fsdp_size = lax.axis_size("fsdp")
    context_size = lax.axis_size("context")
    tensor_size = lax.axis_size("tensor")
    count, width = tokens.shape
    total = deal.shape[0]
    sets, _, rank = attention_proj_down.shape
    ranks = sets * rank
    local_width = attention_proj.shape[2]
    hidden = feed_in.shape[2]
    f = lax.axis_index("fsdp")
    c = lax.axis_index("context")
    t = lax.axis_index("tensor")
    small = context_size == 2 and fsdp_size == 4
    half_at = c % 2
    chip = (f // 2) * 2 + half_at
    chunks = total // count
    if small:
        order = [(f ^ df) * context_size + (c ^ dc) for df, dc in
                 ((0, 0), (0, 1), (2, 0), (2, 1), (1, 0), (1, 1), (3, 0), (3, 1))]
    else:
        order = list(range(chunks))
    ids = jnp.stack([jnp.asarray(value, jnp.int32) for value in [f, half_at, t, f % 2, chip, *order]])
    quarter = count // tensor_size

    def over(axis, size, bit, value):
        return lax.ppermute(value, axis, swap_pairs(axis, size, bit))

    def near(value):
        return over("fsdp", fsdp_size, 1, value)

    def ahead(value):
        return over("fsdp", fsdp_size, 2, value)

    def across(value):
        return over("context", context_size, 1, value)

    def after(value, *others):
        return lax.optimization_barrier((value, *others))[0]

    def exchange(pieces):
        return [pieces[0]] + [over("tensor", tensor_size, k, pieces[k]) for k in range(1, tensor_size)]

    def spread(piece):
        far = over("tensor", tensor_size, 2, piece)
        return [piece, over("tensor", tensor_size, 1, piece), far, over("tensor", tensor_size, 1, far)]

    def reduce_rows(keep, send, *others):
        got = over("tensor", tensor_size, 1, send)
        got, *others = lax.optimization_barrier((got, *others))
        mine, passed = call(
            pair_body, [(keep.shape[1:], single), (keep.shape[1:], low)], ids, [keep, got], name="pair"
        )
        return [mine, over("tensor", tensor_size, 2, passed)], others

    proj_own = jnp.transpose(attention_proj, (1, 0, 2))
    in_own = jnp.transpose(feed_in, (1, 2, 0))
    proj_down = jnp.transpose(attention_proj_down, (0, 2, 1)).reshape(ranks, width)
    out_down_own = jnp.transpose(attention_out_down, (0, 2, 1)).reshape(ranks, local_width)
    in_down = jnp.transpose(feed_in_down, (0, 2, 1)).reshape(ranks, width)
    last_down = jnp.transpose(feed_out_down, (0, 2, 1)).reshape(ranks, hidden)
    proj_up = jnp.transpose(attention_proj_up, (2, 0, 1, 3)).reshape(3, ranks, local_width)
    out_up = attention_out_up.reshape(ranks, width)
    last_up = feed_out_up.reshape(ranks, width)

    proj_far = ahead(proj_own)
    proj_near = near(proj_own)
    in_half, last_half = call(
        split_body,
        [((1, *in_own.shape[1:]), low), ((hidden, feed_out.shape[1] // 2), low)],
        ids,
        [in_own, feed_out],
        name="split",
        cost=2.0,
    )
    in_far = ahead(in_half)

    seqs = lengths.shape[0]
    before = jnp.arange(seqs)[:, None] >= jnp.arange(seqs)[None, :]
    ends = jnp.sum(jnp.where(before, lengths[None, :], 0), axis=1)
    starts = ends - lengths
    segment_all = jnp.sum((deal[:, None] >= ends[None, :]).astype(jnp.int32), axis=1)
    first = (f * context_size + c) * count
    segment_rows = lax.dynamic_slice_in_dim(segment_all, first, count)
    deal_rows = lax.dynamic_slice_in_dim(deal, first, count)
    member = segment_rows[:, None] == jnp.arange(seqs, dtype=jnp.int32)[None, :]
    place = deal_rows - jnp.sum(jnp.where(member, starts[None, :], 0), axis=1)
    chosen = jnp.sum(jnp.where(member, adapter_of[None, :], 0), axis=1)
    set_of = jnp.arange(ranks, dtype=jnp.int32) // rank
    picked = (chosen[:, None] == set_of[None, :]).astype(low)
    half = HEAD_DIM // 2
    lane = jnp.arange(local_width, dtype=jnp.int32) % HEAD_DIM
    freq = jnp.exp((lane % half).astype(single) * (-math.log(rope_base) / half))
    angle = place.astype(single)[:, None] * freq[None, :]
    cos_full = jnp.cos(angle)
    sin_full = jnp.sin(angle) * jnp.where(lane < half, -1.0, 1.0).astype(single)[None, :]
    gain_one = attention_gain.astype(single)[None, :]
    gain_two = feed_gain.astype(single)[None, :]
    normed_one, adapted_q = call(
        prepare_body,
        [((count, width), low), ((count, ranks), low)],
        ids,
        [after(tokens, in_half), gain_one, proj_down, picked],
        name="prepare",
        cost=5.0,
    )

    packed = spread(jnp.concatenate([after(attention_out, in_half), out_down_own], axis=0))
    proj_w = [proj_own, proj_near, proj_far, near(proj_far)]
    groups = segment_all.reshape(-1, count)
    seg_col = segment_rows[:, None]
    normed_one, groups, seg_col, picked = lax.optimization_barrier((normed_one, groups, seg_col, picked))
    in_up = jnp.transpose(feed_in_up, (2, 0, 1, 3)).reshape(2, ranks, hidden)

    query, keyval = call(
        project_body,
        [((count, local_width), low), ((count, 2 * local_width), low)],
        ids,
        [normed_one, adapted_q, proj_up, cos_full, sin_full, *proj_w],
        name="project",
        cost=3.0,
    )

    def plane_gather(value, other=None):
        if not small:
            return [lax.all_gather(value, token_axes, axis=0, tiled=True)]
        corner = lax.ppermute(value, token_axes, swap_pairs(None, fsdp_size * context_size, 2 * context_size + 1))
        chips = [value, across(value), ahead(value), corner]
        if other is None:
            return chips + [near(piece) for piece in chips]
        return chips + [near(value)] + [near(after(piece, other)) for piece in chips[1:]]

    in_near = near(after(in_own, proj_near))
    keyval, in_far, in_near = lax.optimization_barrier((keyval, in_far, in_near))
    last_near = near(after(feed_out, in_near))
    keyval_all = plane_gather(keyval)
    parts_n = len(keyval_all)
    gathered = keyval_all[1:4]
    out_w_own, out_half = call(
        stack_body,
        [((width, local_width), low), ((width // 2, local_width), low)],
        ids,
        [after(packed[0], keyval), *packed[1:]],
        name="stack",
        cost=3.0,
    )
    in_up, gain_two, last_near = lax.optimization_barrier((after(in_up, keyval), gain_two, last_near))
    out_w_own, out_half, in_far, in_up, *gathered = lax.optimization_barrier(
        (out_w_own, out_half, in_far, in_up, *gathered)
    )
    out_near = near(out_w_own)
    out_far = ahead(out_half)
    in_rest = across(in_far)

    slab = pltpu.VMEM((count, local_width), single)
    held = block_rows(count, total) * (local_width // HEAD_DIM)
    many = pltpu.VMEM((held, local_width), low)
    against = pltpu.VMEM((held, total), low)
    heads_out, attended, lse_col, keyval_joined = call(
        lambda *refs: attend_body(parts_n, *refs),
        [
            ((count, local_width), low),
            ((count, local_width), single),
            ((count, 128), single),
            ((total, 2 * local_width), low),
        ],
        ids,
        [after(query, in_up, gain_two), seg_col, groups, *keyval_all],
        scratch=[many, pltpu.VMEM((held, total), single), pltpu.SemaphoreType.DMA((parts_n,))],
        far=range(3, 3 + parts_n),
        vmem=16 if small else 60,
        name="attend",
        cost=8.0,
    )
    heads_out, out_far, in_rest = lax.optimization_barrier((heads_out, out_far, in_rest))
    heads = spread(heads_out)
    last_far = ahead(after(last_half, heads_out))
    out_rest = across(out_far)
    last_rest = across(last_far)
    out_late, in_late, last_late, in_rest = after((out_far, in_far, last_far, in_rest), heads[1])
    out_w = [out_w_own, out_near, out_far, out_rest, near(out_late), near(out_rest)]
    in_w = [in_own, in_near, in_far, in_rest, near(in_late), near(in_rest)]
    last_w = [feed_out, last_near, last_far, last_rest, near(last_late), near(last_rest)]
    wide = width + ranks
    piece = ((2, quarter, wide), low)
    mid_outs = call(
        middle_body,
        [piece] * 2
        + [((count, ranks), low)] * 3
        + [
            ((count, width), low),
            ((count, hidden), low),
            ((2, count, hidden), low),
            ((quarter, width), single),
            ((4, width, local_width), low),
            ((4, *feed_out.shape), low),
        ],
        ids,
        [*heads, *out_w, *packed, out_up, tokens, gain_two, grad_out, picked, *in_w, in_down, in_up, *last_w,
         last_down, last_up],
        scratch=[
            pltpu.VMEM((count, wide), single),
            pltpu.VMEM((4, *in_own.shape), low),
            pltpu.SemaphoreType.DMA((18,)),
        ],
        far=(*range(4, 10), *range(19, 25), *range(27, 33)),
        vmem=20 if small else 60,
        name="middle",
    )
    adapted_o, adapted_i, grad_adapt_d, normed_two, activity, grad_gates, middle_q, out_all, last_all = mid_outs[2:]
    if small:
        query_late = after(query, activity)
        summed, (query_x, query_y, query_n) = reduce_rows(
            *mid_outs[:2], across(query_late), ahead(query_late), near(query_late)
        )
        query_xy = ahead(query_x)
        query_all = [query, query_x, query_y, query_xy, query_n, near(query_x), near(query_y)]
    else:
        summed, _ = reduce_rows(*mid_outs[:2])
        query_all = plane_gather(query)
    feed_pieces = call(
        feed_body,
        [piece] * 2,
        ids,
        [after(activity, summed[0]), last_down, last_all],
        scratch=[pltpu.VMEM((count, wide), single)],
        name="feed",
    )
    summed, query_all, feed_pieces = lax.optimization_barrier((summed, query_all, feed_pieces))
    turn = ((quarter, local_width + ranks), low)
    *turned, grad_mid, grad_branch, grad_adapt_i = call(
        turn_body,
        [turn] * 4 + [((quarter, width), single), ((quarter, width), low), ((quarter, ranks), low)],
        ids,
        [*summed, picked, in_down, middle_q, gain_two, grad_out, out_up, out_all, *packed],
        vmem=6 if small else 40,
        name="turn",
        cost=3.0,
    )
    if small:
        query_all = query_all + [near(after(query_all[3], grad_mid))]
    arrived = exchange(turned)
    sizes = [width] * 4 + [padded(hidden)] * 3 + [3 * local_width, local_width]
    columns = sum(sizes)
    places = [(i, j) for i in range(fsdp_size) for j in range(context_size)]
    number = {place: at for at, place in enumerate(places)}
    side = {(i, j): (i, j ^ 1) for i, j in places}
    front = {(i, j): (i ^ 2, j) for i, j in places}
    one = [(number[p], number[front[p] if p[0] % 2 else side[p]]) for p in places]
    two = [(number[p], number[side[p] if p[0] % 2 else front[p]]) for p in places]
    rows = ranks // 8

    def fold_strips(keep, send):
        columns = keep.shape[1]
        return call(
            fold_body,
            [((2, rows, columns), low)] * 2,
            ids,
            [keep, near(send)],
            scratch=[pltpu.VMEM((ranks // 2, columns), single)],
            name="fold",
            cost=3.0,
        )

    def reduce_strips(own, got):
        columns = own.shape[2]
        mine, passed = call(
            pair_body,
            [((rows, columns), single), ((rows, columns), low)],
            ids,
            [own, got],
            name="pair_chips",
            cost=3.0,
        )
        return [mine, lax.ppermute(passed, token_axes, two)]

    (feed_mine, feed_got), _ = reduce_rows(*feed_pieces)
    arrived, query_all, feed_mine = lax.optimization_barrier((arrived, query_all, feed_mine))
    tail = 32
    message, delta_col, grad_adapt_o = call(
        collect_body,
        [((count + tail, local_width), low), ((count, 128), single), ((count, ranks), low)],
        ids,
        [*arrived, attended, lse_col],
        name="collect",
        cost=3.0,
    )
    (grad_query,) = call(
        query_body,
        [((count, local_width), single)],
        ids,
        [query, message, lse_col, delta_col, seg_col, groups, keyval_joined],
        scratch=[many, many, against],
        vmem=12 if small else 60,
        name="queries",
        cost=7.0,
    )
    message_all = [value.reshape(-1, count + tail, local_width) for value in plane_gather(message, grad_query)]
    output_q, adapted_d = call(
        out_body,
        [((quarter, width), low), ((quarter, ranks), low)],
        ids,
        [feed_mine, after(feed_got, grad_query), picked, middle_q, last_up],
        name="outputs",
    )
    output_all = spread(output_q)
    *last_pieces, grad_proj, part_adapt_q = call(
        lambda *refs: key_body(parts_n, *refs),
        [piece] * 2 + [((count, 3 * local_width), low), ((count, ranks), low)],
        ids,
        [after(keyval, output_q), seg_col, groups, grad_query, cos_full, sin_full, proj_up, picked, *proj_w, *query_all, *message_all],
        scratch=[
            pltpu.VMEM((8, total), single),
            slab,
            slab,
            pltpu.VMEM((count, wide), single),
            many,
            many,
            against,
            against,
            pltpu.VMEM((total, local_width), low),
            pltpu.VMEM((chunks, count, local_width), low),
            pltpu.VMEM((chunks, tail, local_width), low),
            pltpu.SemaphoreType.DMA((3 * parts_n,)),
        ],
        far=range(12, 12 + 2 * parts_n),
        vmem=22 if small else 60,
        name="keys",
        cost=10.0,
    )
    part_adapt_q, *output_all[1:3] = lax.optimization_barrier((part_adapt_q, *output_all[1:3]))
    output_all[3] = over("tensor", tensor_size, 1, output_all[2])
    last_mine, last_got = reduce_rows(*last_pieces)[0]
    late = call(
        grads_body,
        [((ranks // 2, columns), low)] * 2,
        ids,
        [grad_adapt_i, normed_two, adapted_o, grad_branch, adapted_d, grad_out,
         part_adapt_q, normed_one, adapted_i,
         grad_gates, grad_adapt_d, activity, adapted_q, grad_proj, grad_adapt_o, heads_out],
        scratch=[pltpu.VMEM((ranks, columns), single)],
        vmem=8 if small else 40,
        name="grads",
        cost=3.0,
    )
    def finish_tokens(got):
        return call(
            last_body,
            [((quarter, width), low)],
            ids,
            [last_mine, got, picked, proj_down, tokens, gain_one, grad_mid],
            name="last",
        )

    finals = [((ranks, width), single)] * 4 + [((ranks, 2, hidden), single), ((ranks, hidden), single)]
    finals = finals + [((sets, 3, rank, local_width), single), ((ranks, local_width), single)]
    if small:
        late_own, late_out = fold_strips(*late)
        late_mine, late_got = reduce_strips(late_own, lax.ppermute(late_out, token_axes, one))
        shared, rest = call(
            total_body,
            [((rows, 4 * width), low), ((rows, columns - 4 * width), low)],
            ids,
            [late_mine, late_got],
            name="total",
            cost=3.0,
        )
        shared_near, last_got = lax.optimization_barrier((over("tensor", tensor_size, 1, shared), last_got))
        (grad_tokens_q,) = finish_tokens(last_got)
        (shared,) = call(add_body, [((rows, 4 * width), low)], ids, [shared, shared_near], name="add")
        shared_far = over("tensor", tensor_size, 2, shared)
        (output,) = call(assemble_body, [((count, width), low)], ids, output_all, name="join_output")
        rest, output, grad_tokens_q = lax.optimization_barrier((rest, output, grad_tokens_q))
        tokens_all = spread(grad_tokens_q)
        (joined,) = call(
            join_body,
            [((rows, columns), low)],
            ids,
            [shared, shared_far, rest],
            name="join",
            cost=3.0,
        )
        beside = lax.ppermute(joined, token_axes, two)
        both = jnp.stack([joined, after(beside, tokens_all[1], tokens_all[2])])
        others = lax.ppermute(both, token_axes, one)
        strips = [joined, beside, after(others, tokens_all[3])]
        strips = strips + [near(value) for value in strips]
        results = call(finish_body, finals, ids, strips, name="finish")
    else:
        (grad_tokens_q,) = finish_tokens(last_got)
        tokens_all = spread(grad_tokens_q)
        (output,) = call(assemble_body, [((count, width), low)], ids, output_all, name="join_output")
        pair = jnp.where(f % 2 == 0, jnp.concatenate(late), jnp.concatenate(late[::-1]))
        pair = lax.psum(pair, token_axes)
        joined = jnp.concatenate([lax.psum(pair[:, : 4 * width], "tensor"), pair[:, 4 * width :]], axis=1)
        cut = [0]
        for span in [width] * 4 + [padded(hidden)] * 3 + [3 * local_width, local_width]:
            cut.append(cut[-1] + span)
        slices = [joined[:, lo:hi].astype(single) for lo, hi in zip(cut, cut[1:])]
        *results, gate_up, mult_up, last_grad, proj_up_grad, out_down_grad = slices
        results = [*results, jnp.stack([gate_up[:, :hidden], mult_up[:, :hidden]], axis=1), last_grad[:, :hidden]]
        proj_up_grad = jnp.transpose(proj_up_grad.reshape(sets, rank, 3, local_width), (0, 2, 1, 3))
        results = [*results, proj_up_grad, out_down_grad]

    in_down_grad, out_up_grad, last_up_grad, proj_down_grad, in_up_grad, last_grad, proj_up_grad, out_down_grad = results
    (grad_tokens,) = call(assemble_body, [((count, width), low)], ids, tokens_all, name="join_tokens")


    def down(grad):
        return jnp.transpose(grad.reshape(sets, rank, -1), (0, 2, 1))

    return (
        output,
        grad_tokens,
        down(proj_down_grad),
        jnp.transpose(proj_up_grad, (0, 2, 1, 3)),
        down(out_down_grad),
        out_up_grad.reshape(sets, rank, width),
        down(in_down_grad),
        in_up_grad.reshape(sets, rank, 2, hidden),
        down(last_grad),
        last_up_grad.reshape(sets, rank, width),
    )


def solution(mesh):
    return jax.shard_map(
        on_device,
        mesh=mesh,
        in_specs=(
            P(("fsdp", "context"), None),
            P(("fsdp", "context"), None),
            P(),
            P(),
            P(),
            P(),
            P("fsdp", None, "tensor"),
            P("tensor", "fsdp"),
            P(),
            P("fsdp", None, "tensor"),
            P("tensor", "fsdp"),
            P(),
            P(None, None, None, "tensor"),
            P(None, "tensor", None),
            P(),
            P(),
            P(None, None, None, "tensor"),
            P(None, "tensor", None),
            P(),
        ),
        out_specs=(
            P(("fsdp", "context"), None),
            P(("fsdp", "context"), None),
            P(),
            P(None, None, None, "tensor"),
            P(None, "tensor", None),
            P(),
            P(),
            P(None, None, None, "tensor"),
            P(None, "tensor", None),
            P(),
        ),
        check_vma=False,
    )
```

```python
import math

import jax
import jax.numpy as jnp
from jax import lax
from jax.experimental import pallas as pl
from jax.experimental.pallas import tpu as pltpu
from jax.sharding import PartitionSpec as P

HEAD_DIM = 64


rope_base = 160000.0
epsilon = 1e-05
negative = -1e30
single = jnp.float32
low = jnp.bfloat16
scale = HEAD_DIM ** (-0.5)
token_axes = ("fsdp", "context")
every_axis = ("fsdp", "context", "tensor")


def nn(left, right):
    return lax.dot_general(
        left, right, (((1,), (0,)), ((), ())), preferred_element_type=jnp.float32
    )


def nt(left, right):
    return lax.dot_general(
        left, right, (((1,), (1,)), ((), ())), preferred_element_type=jnp.float32
    )


def tn(left, right):
    return lax.dot_general(
        left, right, (((0,), (0,)), ((), ())), preferred_element_type=jnp.float32
    )


def call(body, outs, ids, args, scratch=(), vmem=6, name=None, far=(), cost=0.0):
    whole = pl.BlockSpec(memory_space=pltpu.VMEM)
    return pl.pallas_call(
        body,
        out_shape=[jax.ShapeDtypeStruct(shape, kind) for shape, kind in outs],
        in_specs=[pl.BlockSpec(memory_space=pltpu.SMEM)]
        + [pl.BlockSpec(memory_space=pltpu.HBM) if at in far else whole for at in range(len(args))],
        out_specs=[whole] * len(outs),
        scratch_shapes=list(scratch),
        compiler_params=pltpu.CompilerParams(vmem_limit_bytes=vmem << 20),
        cost_estimate=pl.CostEstimate(flops=int(cost * 1e12) + 1, bytes_accessed=int(cost * 1e12) + 1, transcendentals=0),
        name=name,
    )(ids, *args)


def swap_pairs(axis, size, bit):
    return [(i, i ^ bit) for i in range(size)]


def layer_norm_rows(values):
    centered = values - jnp.mean(values, axis=1, keepdims=True)
    rstd = lax.rsqrt(jnp.mean(centered * centered, axis=1, keepdims=True) + epsilon)
    return (centered * rstd, rstd)


def layer_norm_back(upstream, gain, xhat, rstd):
    scaled = upstream * gain
    return rstd * (
        scaled
        - jnp.mean(scaled, axis=1, keepdims=True)
        - xhat * jnp.mean(scaled * xhat, axis=1, keepdims=True)
    )


def swap_halves(u):
    width = u.shape[1]
    half = HEAD_DIM // 2
    lane = lax.broadcasted_iota(jnp.int32, (1, width), 1)
    return jnp.where(
        lane % HEAD_DIM < half, pltpu.roll(u, width - half, 1), pltpu.roll(u, half, 1)
    )


def head_row(width, head):
    lane = lax.broadcasted_iota(jnp.int32, (1, width), 1)
    return (lane // HEAD_DIM == head).astype(single)


def start_copies(pairs, sems):
    copies = [pltpu.make_async_copy(src, dst, sems.at[n]) for n, (src, dst) in enumerate(pairs)]
    for copy in copies:
        copy.start()
    return copies


def loop(count, step, most=8):
    if count <= most:
        for number in range(count):
            step(number)
    else:

        def inner(number, carry):
            step(number)
            return carry

        lax.fori_loop(0, count, inner, 0)


def at_block(number, size):
    start = number * size
    return pl.ds(start if isinstance(start, int) else pl.multiple_of(start, 16), size)


def block_rows(count, total):
    return max(16, min(count, 2048 * count // total))


def cols_of(ids_ref, k, width):
    return pl.ds(pl.multiple_of((ids_ref[0] ^ k) * width, 128), width)


def rows_of(ids_ref, k, height):
    return pl.ds(pl.multiple_of((ids_ref[2] ^ k) * height, 16), height)


def join_rows(ids_ref, dst_ref, mine_ref, other_ref):
    size = mine_ref.shape[0]
    dst_ref[pl.ds(ids_ref[1] * size, size)] = mine_ref[...]
    dst_ref[pl.ds((1 - ids_ref[1]) * size, size)] = other_ref[...]


def join_cols(ids_ref, dst_ref, mine_ref, other_ref):
    size = mine_ref.shape[1]
    dst_ref[:, pl.ds(pl.multiple_of(ids_ref[1] * size, 128), size)] = mine_ref[...]
    dst_ref[:, pl.ds(pl.multiple_of((1 - ids_ref[1]) * size, 128), size)] = other_ref[...]


def project_body(ids_ref, x_ref, aq_ref, up_ref, cos_ref, sin_ref, *refs):
    weights, q_ref, kv_ref = (refs[:-2], refs[-2], refs[-1])
    part = weights[0].shape[1]
    width = weights[0].shape[2]
    for j in range(3):
        acc = nn(aq_ref[...], up_ref[j])
        for k, w_ref in enumerate(weights):
            acc = acc + nn(x_ref[:, cols_of(ids_ref, k, part)], w_ref[j])
        if j < 2:
            acc = acc * cos_ref[...] + swap_halves(acc) * sin_ref[...]
        if j == 0:
            q_ref[...] = acc.astype(low)
        else:
            kv_ref[:, (j - 1) * width : j * width] = acc.astype(low)


def prepare_body(ids_ref, tokens_ref, gain_ref, down_ref, picked_ref, n1_ref, aq_ref):
    xhat, _ = layer_norm_rows(tokens_ref[...].astype(single))
    normed = (xhat * gain_ref[...]).astype(low)
    n1_ref[...] = normed
    aq_ref[...] = (picked_ref[...].astype(single) * nt(normed, down_ref[...])).astype(low)


def split_body(ids_ref, in_ref, last_ref, ihalf_ref, lhalf_ref):
    ihalf_ref[...] = in_ref[pl.ds(ids_ref[1], 1)]
    cols = lhalf_ref.shape[1]
    lhalf_ref[...] = last_ref[:, pl.ds(pl.multiple_of(ids_ref[1] * cols, 128), cols)]


def stack_body(ids_ref, p0, p1, p2, p3, full_ref, half_ref):
    rows = p0.shape[1]
    for k, p_ref in enumerate([p0, p1, p2, p3]):
        full_ref[k * rows : (k + 1) * rows, :] = p_ref[:rows, :]
    size = half_ref.shape[0]
    half_ref[...] = full_ref[pl.ds(pl.multiple_of(ids_ref[1] * size, 16), size), :]


def put_pieces(ids_ref, wide_ref, keep_ref, send_ref):
    quarter = keep_ref.shape[1]
    for at, (ref, k) in enumerate([(keep_ref, 0), (keep_ref, 2), (send_ref, 1), (send_ref, 3)]):
        ref[at % 2] = wide_ref[rows_of(ids_ref, k, quarter), :].astype(low)


def pair_body(ids_ref, keep_ref, got_ref, mine_ref, pass_ref):
    mine_ref[...] = keep_ref[0].astype(single) + got_ref[0].astype(single)
    pass_ref[...] = (keep_ref[1].astype(single) + got_ref[1].astype(single)).astype(low)


def attend_body(parts_n, ids_ref, q_ref, segc_ref, groups_ref, *refs):
    parts = refs[:parts_n]
    heads_ref, att_ref, lcol_ref, kv_ref, many_ref, s_ref, sems = refs[parts_n:]
    count, width = q_ref.shape
    heads = width // HEAD_DIM
    chunk = groups_ref.shape[1]
    size = many_ref.shape[0] // heads
    base = 0
    pairs = []
    for part in parts:
        pairs.append((part, kv_ref.at[base : base + part.shape[0], :]))
        base += part.shape[0]
    copies = start_copies(pairs, sems)
    lane = lax.broadcasted_iota(jnp.int32, (1, 128), 1)
    waits = list(copies)

    def block(number):
        rows = at_block(number, size)
        for h in range(heads):
            many_ref[h * size : (h + 1) * size, :] = q_ref[rows, :] * (head_row(width, h) * scale).astype(low)

        def scores(j):
            cols = at_block(j, chunk)
            same = segc_ref[rows, :] == groups_ref[pl.ds(ids_ref[5 + j], 1), :]
            s = nt(many_ref[...], kv_ref[cols, :width])
            for h in range(heads):
                s_ref[h * size : (h + 1) * size, cols] = jnp.where(same, s[h * size : (h + 1) * size], negative)

        while waits:
            waits.pop(0).wait()
        loop(base // chunk, scores)
        total = jnp.zeros((size, width), single)
        lcol = jnp.zeros((size, 128), single)
        for h in range(heads):
            s = s_ref[h * size : (h + 1) * size, :]
            top = jnp.max(s, axis=1, keepdims=True)
            p = jnp.exp(s - top)
            mass = jnp.sum(p, axis=1, keepdims=True)
            total = total + nn(p.astype(low), kv_ref[:, width:]) * (head_row(width, h) / mass)
            lcol = jnp.where(lane == h, top + jnp.log(mass), lcol)
        att_ref[rows, :] = total
        lcol_ref[rows, :] = lcol
        heads_ref[rows, :] = total.astype(low)

    loop(count // size, block, 1)


def middle_body(ids_ref, *refs):
    heads = refs[0:4]
    wown, wnear, wa, wb, wc, wd = refs[4:10]
    packs = refs[10:14]
    refs = refs[3:]
    ou_ref, tokens_ref, gain_ref, go_ref, picked_ref = refs[11:16]
    iown, inear, ia, ib, ic, idd = refs[16:22]
    idn_ref, iu_ref = refs[22:24]
    lown, lnear, la, lb, lc, ld = refs[24:30]
    ldn_ref, lup_ref = refs[30:32]
    keep_ref, send_ref, ao_ref, ai_ref, gad_ref, n2_ref, act_ref, gg_ref, mid_ref, wts, lts = refs[32:43]
    wide_ref, its, sems = refs[43:]
    mine, rest = (ids_ref[1], 1 - ids_ref[1])
    half = wa.shape[0]
    step = la.shape[1]

    def rows(k, at):
        return wts.at[k, pl.ds(pl.multiple_of(at * half, 16), half), :]

    def cols(k, at):
        return lts.at[k, :, pl.ds(pl.multiple_of(at * step, 128), step)]

    pairs = [
        (wown, wts.at[0]),
        (wnear, wts.at[1]),
        (wa, rows(2, mine)),
        (wb, rows(2, rest)),
        (wc, rows(3, mine)),
        (wd, rows(3, rest)),
        (iown, its.at[0]),
        (inear, its.at[1]),
        (ia, its.at[2, pl.ds(mine, 1)]),
        (ib, its.at[2, pl.ds(rest, 1)]),
        (ic, its.at[3, pl.ds(mine, 1)]),
        (idd, its.at[3, pl.ds(rest, 1)]),
        (lown, lts.at[0]),
        (lnear, lts.at[1]),
        (la, cols(2, mine)),
        (lb, cols(2, rest)),
        (lc, cols(3, mine)),
        (ld, cols(3, rest)),
    ]
    copies = [pltpu.make_async_copy(src, dst, sems.at[n]) for n, (src, dst) in enumerate(pairs)]
    for copy in copies:
        copy.start()
    h0 = heads[0]
    w0 = wown
    outs_w = [wts.at[k] for k in range(4)]
    ins_w = [its.at[k] for k in range(4)]
    lasts_w = [lts.at[k] for k in range(4)]
    part = w0.shape[1]
    span = h0.shape[1]
    width = tokens_ref.shape[1]
    picked = picked_ref[...].astype(single)
    span = h0.shape[1]
    adapt = nt(h0[...], packs[0][span:, :])
    for k in range(1, len(heads)):
        adapt = adapt + nt(heads[k][...], packs[k][span:, :])
    ao = (picked * adapt).astype(low)
    ao_ref[...] = ao
    for copy in copies[:6]:
        copy.wait()
    for k, w_ref in enumerate(outs_w):
        acc = nn(h0[...], w_ref[:span, :])
        for r in range(1, len(heads)):
            acc = acc + nn(heads[r][...], w_ref[r * span : (r + 1) * span, :])
        wide_ref[:, cols_of(ids_ref, k, part)] = acc
    middle = tokens_ref[...].astype(single) + wide_ref[:, :width] + nn(ao, ou_ref[...])
    wide_ref[:, :width] = middle
    quarter = mid_ref.shape[0]
    mid_ref[...] = wide_ref[rows_of(ids_ref, 0, quarter), :width]
    xhat, _ = layer_norm_rows(middle)
    n2 = (xhat * gain_ref[...]).astype(low)
    n2_ref[...] = n2
    ai = (picked * nt(n2, idn_ref[...])).astype(low)
    ai_ref[...] = ai
    for copy in copies[6:12]:
        copy.wait()
    gate = nn(ai, iu_ref[0])
    mult = nn(ai, iu_ref[1])
    for k, w_ref in enumerate(ins_w):
        x = n2_ref[:, cols_of(ids_ref, k, part)]
        gate = gate + nt(x, w_ref[0])
        mult = mult + nt(x, w_ref[1])
    phi = 0.5 * (1.0 + lax.erf(gate * (2.0**-0.5)))
    gated = gate * phi
    act_ref[...] = (gated * mult).astype(low)
    slope = phi + gate * jnp.exp(-0.5 * gate * gate) * (1.0 / math.sqrt(2.0 * math.pi))
    go = go_ref[...]
    gad = (nt(go, lup_ref[...]).astype(low).astype(single) * picked).astype(low)
    gad_ref[...] = gad
    for copy in copies[12:]:
        copy.wait()
    ga = nn(gad, ldn_ref[...])
    for k, w_ref in enumerate(lasts_w):
        ga = ga + nt(go_ref[:, cols_of(ids_ref, k, part)], w_ref[...])
    gg0 = (slope * (ga * mult)).astype(low)
    gg1 = (ga * gated).astype(low)
    gg_ref[0] = gg0
    gg_ref[1] = gg1
    for k, w_ref in enumerate(ins_w):
        wide_ref[:, cols_of(ids_ref, k, part)] = nn(gg0, w_ref[0]) + nn(gg1, w_ref[1])
    wide_ref[:, width:] = nt(gg0, iu_ref[0]) + nt(gg1, iu_ref[1])
    put_pieces(ids_ref, wide_ref, keep_ref, send_ref)


def feed_body(ids_ref, act_ref, ldn_ref, lts, keep_ref, send_ref, wide_ref):
    part = lts.shape[2]
    act = act_ref[...]
    wide_ref[:, wide_ref.shape[1] - ldn_ref.shape[0] :] = nt(act, ldn_ref[...])
    for k in range(4):
        wide_ref[:, cols_of(ids_ref, k, part)] = nn(act, lts[k])
    put_pieces(ids_ref, wide_ref, keep_ref, send_ref)


def turn_body(
    ids_ref, p0, p1, picked_ref, idn_ref, mid_ref, gain_ref, go_ref, ou_ref, wts, d0, d1, d2, d3,
    a0, a1, a2, a3, gm_ref, gb_ref, gai_ref,
):
    quarter = p0.shape[0]
    width = mid_ref.shape[1]
    part = wts.shape[2]
    rows = rows_of(ids_ref, 0, quarter)
    picked = picked_ref[rows, :].astype(single)
    total = p0[...] + p1[...].astype(single)
    gai = (total[:, width:].astype(low).astype(single) * picked).astype(low)
    gai_ref[...] = gai
    upstream = total[:, :width] + nn(gai, idn_ref[...])
    xhat, rstd = layer_norm_rows(mid_ref[...])
    gm = go_ref[rows, :].astype(single) + layer_norm_back(upstream, gain_ref[...], xhat, rstd)
    gm_ref[...] = gm
    gb = gm.astype(low)
    gb_ref[...] = gb
    gao = (nt(gb, ou_ref[...]).astype(low).astype(single) * picked).astype(low)
    span = d0.shape[1]
    grads = [nn(gao, d_ref[span:, :]) for d_ref in (d0, d1, d2, d3)]
    for k in range(4):
        w_ref = wts.at[k]
        x = gb_ref[:, cols_of(ids_ref, k, part)]
        for r in range(4):
            grads[r] = grads[r] + nt(x, w_ref[r * span : (r + 1) * span, :])
    for k, a_ref in enumerate([a0, a1, a2, a3]):
        a_ref[:, :span] = grads[k].astype(low)
        a_ref[:, span:] = gao


def out_body(ids_ref, p0, p1, picked_ref, mid_ref, lup_ref, out_ref, ad_ref):
    width = mid_ref.shape[1]
    picked = picked_ref[rows_of(ids_ref, 0, p0.shape[0]), :].astype(single)
    total = p0[...] + p1[...].astype(single)
    ad = (picked * total[:, width:]).astype(low)
    ad_ref[...] = ad
    out_ref[...] = (mid_ref[...] + total[:, :width] + nn(ad, lup_ref[...])).astype(low)


def collect_body(ids_ref, a0, a1, a2, a3, att_ref, lcol_ref, msg_ref, dcol_ref, gao_ref):
    quarter = a0.shape[0]
    count, width = att_ref.shape
    for k, a_ref in enumerate([a0, a1, a2, a3]):
        msg_ref[rows_of(ids_ref, k, quarter), :] = a_ref[:, :width]
        gao_ref[rows_of(ids_ref, k, quarter), :] = a_ref[:, width:]
    both = msg_ref[:count, :].astype(single) * att_ref[...]
    heads = width // HEAD_DIM
    lane = lax.broadcasted_iota(jnp.int32, (1, 128), 1)
    dcol = jnp.zeros((count, 128), single)
    pair = lcol_ref[...]
    for h in range(heads):
        delta = jnp.sum(both * head_row(width, h), axis=1, keepdims=True)
        dcol = jnp.where(lane == h, delta, dcol)
        pair = jnp.where(lane == heads + h, delta, pair)
    dcol_ref[...] = dcol
    rows = jnp.transpose(pair)[:8, :]
    first = rows.astype(low).astype(single)
    rest = rows - first
    second = rest.astype(low).astype(single)
    third = rest - second
    tail = jnp.concatenate([first, second, third, jnp.zeros_like(first)], axis=0)
    msg_ref[count:, :] = tail.astype(low)


def query_body(
    ids_ref, q_ref, msg_ref, lcol_ref, dcol_ref, segc_ref, groups_ref, kv_ref, dq_ref, many_ref, more_ref, ds_ref
):
    count, width = q_ref.shape
    heads = width // HEAD_DIM
    chunk = groups_ref.shape[1]
    size = many_ref.shape[0] // heads

    def block(number):
        rows = at_block(number, size)
        for h in range(heads):
            many_ref[h * size : (h + 1) * size, :] = q_ref[rows, :] * (head_row(width, h) * scale).astype(low)
            more_ref[h * size : (h + 1) * size, :] = msg_ref[rows, :] * head_row(width, h).astype(low)

        def scores(j):
            cols = at_block(j, chunk)
            same = segc_ref[rows, :] == groups_ref[pl.ds(ids_ref[5 + j], 1), :]
            s = nt(many_ref[...], kv_ref[cols, :width])
            dp = nt(more_ref[...], kv_ref[cols, width:])
            for h in range(heads):
                mine = slice(h * size, (h + 1) * size)
                p = jnp.exp(jnp.where(same, s[mine] - lcol_ref[rows, h : h + 1], negative))
                ds_ref[mine, cols] = (p * (dp[mine] - dcol_ref[rows, h : h + 1])).astype(low)

        loop(kv_ref.shape[0] // chunk, scores)
        dq = nn(ds_ref[...], kv_ref[:, :width])
        total = jnp.zeros((size, width), single)
        for h in range(heads):
            total = total + dq[h * size : (h + 1) * size] * (head_row(width, h) * scale)
        dq_ref[rows, :] = total

    loop(count // size, block, 1)


def key_body(
    parts_n, ids_ref, own_ref, segc_ref, groups_ref, dq_ref, cos_ref, sin_ref, up_ref, picked_ref, w0, w1, w2, w3, *refs
):
    parts = refs[:parts_n]
    msgs = refs[parts_n : 2 * parts_n]
    keep_ref, send_ref, gp_ref, paq_ref, stat_ref, dk_ref, dv_ref, wide_ref, many_ref, more_ref, p_ref, ds_ref = refs[
        2 * parts_n : 2 * parts_n + 12
    ]
    q_ref, do_ref, tail_ref, sems = refs[2 * parts_n + 12 :]
    count = own_ref.shape[0]
    width = dq_ref.shape[1]
    heads = width // HEAD_DIM
    base = 0
    pairs = []
    for part, msg in zip(parts, msgs):
        held = msg.shape[0]
        pairs.append((part, q_ref.at[base * count : (base + held) * count, :]))
        pairs.append((msg.at[:, :count, :], do_ref.at[base : base + held]))
        pairs.append((msg.at[:, count:, :], tail_ref.at[base : base + held]))
        base += held
    copies = start_copies(pairs, sems)
    for copy in copies:
        copy.wait()
    for j in range(base):
        e = tail_ref[j].astype(single)
        stat_ref[:, j * count : (j + 1) * count] = e[:8] + e[8:16] + e[16:24]

    size = many_ref.shape[0] // heads

    def block(number):
        rows = at_block(number, size)
        for h in range(heads):
            hm = head_row(width, h)
            many_ref[h * size : (h + 1) * size, :] = own_ref[rows, :width] * (hm * scale).astype(low)
            more_ref[h * size : (h + 1) * size, :] = own_ref[rows, width:] * hm.astype(low)

        def scores(j):
            cols = at_block(j, count)
            same = segc_ref[rows, :] == groups_ref[pl.ds(ids_ref[5 + j], 1), :]
            s = nt(many_ref[...], q_ref[cols, :])
            dp = nt(more_ref[...], do_ref[j])
            for h in range(heads):
                mine = slice(h * size, (h + 1) * size)
                p = jnp.exp(jnp.where(same, s[mine] - stat_ref[h : h + 1, cols], negative))
                p_ref[mine, cols] = p.astype(low)
                ds_ref[mine, cols] = (p * (dp[mine] - stat_ref[heads + h : heads + h + 1, cols])).astype(low)

        loop(base, scores)
        dv = nn(p_ref[...], do_ref[...].reshape(base * count, width))
        dk = nn(ds_ref[...], q_ref[...])
        dv_total = jnp.zeros((size, width), single)
        dk_total = jnp.zeros((size, width), single)
        for h in range(heads):
            hm = head_row(width, h)
            dv_total = dv_total + dv[h * size : (h + 1) * size] * hm
            dk_total = dk_total + dk[h * size : (h + 1) * size] * (hm * scale)
        dv_ref[rows, :] = dv_total
        dk_ref[rows, :] = dk_total

    loop(count // size, block, 1)
    cosine = cos_ref[...]
    sine = sin_ref[...]
    gq = (dq_ref[...] * cosine - swap_halves(dq_ref[...]) * sine).astype(low)
    gk = (dk_ref[...] * cosine - swap_halves(dk_ref[...]) * sine).astype(low)
    gv = dv_ref[...].astype(low)
    gp_ref[:, :width] = gq
    gp_ref[:, width : 2 * width] = gk
    gp_ref[:, 2 * width :] = gv
    part = w0.shape[1]
    full = wide_ref.shape[1] - up_ref.shape[1]
    for k, w_ref in enumerate([w0, w1, w2, w3]):
        wide_ref[:, cols_of(ids_ref, k, part)] = nt(gq, w_ref[0]) + nt(gk, w_ref[1]) + nt(gv, w_ref[2])
    adapt = nt(gq, up_ref[0]) + nt(gk, up_ref[1]) + nt(gv, up_ref[2])
    wide_ref[:, full:] = adapt
    paq_ref[...] = (adapt * picked_ref[...].astype(single)).astype(low)
    put_pieces(ids_ref, wide_ref, keep_ref, send_ref)


def last_body(ids_ref, p0, p1, picked_ref, pdn_ref, tokens_ref, gain_ref, gm_ref, gt_ref):
    quarter = p0.shape[0]
    width = gm_ref.shape[1]
    rows = rows_of(ids_ref, 0, quarter)
    picked = picked_ref[rows, :].astype(single)
    total = p0[...] + p1[...].astype(single)
    gaq = (total[:, width:].astype(low).astype(single) * picked).astype(low)
    upstream = total[:, :width] + nn(gaq, pdn_ref[...])
    xhat, rstd = layer_norm_rows(tokens_ref[rows, :].astype(single))
    gt_ref[...] = (gm_ref[...] + layer_norm_back(upstream, gain_ref[...], xhat, rstd)).astype(low)


def assemble_body(ids_ref, p0, p1, p2, p3, out_ref):
    quarter = p0.shape[0]
    width = out_ref.shape[1]
    for k, p_ref in enumerate([p0, p1, p2, p3]):
        out_ref[rows_of(ids_ref, k, quarter), :] = p_ref[:, :width]


def padded(size):
    return -(-size // 128) * 128


def lay_out(ids_ref, values, keep_ref, send_ref, all_ref):
    ranks = all_ref.shape[0]
    at = 0
    for value in values:
        size = value.shape[1]
        all_ref[:, at : at + size] = value
        if padded(size) != size:
            all_ref[:, at + size : at + padded(size)] = jnp.zeros((ranks, padded(size) - size), single)
        at += padded(size)
    half = ranks // 2
    keep_ref[...] = all_ref[pl.ds(pl.multiple_of(ids_ref[3] * half, 16), half), :].astype(low)
    send_ref[...] = all_ref[pl.ds(pl.multiple_of((1 - ids_ref[3]) * half, 16), half), :].astype(low)


def grads_body(
    ids_ref, gai_ref, n2_ref, ao_ref, gb_ref, ad_ref, go_ref, paq_ref, n1_ref, ai_ref, gg_ref, gad_ref, act_ref,
    aq_ref, gp_ref, gao_ref, heads_ref, keep_ref, send_ref, all_ref,
):
    rows = rows_of(ids_ref, 0, gb_ref.shape[0])
    values = [
        tn(gai_ref[...], n2_ref[rows, :]),
        tn(ao_ref[rows, :], gb_ref[...]),
        tn(ad_ref[...], go_ref[rows, :]),
        tn(paq_ref[...], n1_ref[...]),
        tn(ai_ref[...], gg_ref[0]),
        tn(ai_ref[...], gg_ref[1]),
        tn(gad_ref[...], act_ref[...]),
        tn(aq_ref[...], gp_ref[...]),
        tn(gao_ref[...], heads_ref[...]),
    ]
    lay_out(ids_ref, values, keep_ref, send_ref, all_ref)


def fold_body(ids_ref, keep_ref, got_ref, own_ref, send_ref, sum_ref):
    sum_ref[...] = keep_ref[...].astype(single) + got_ref[...].astype(single)
    size = own_ref.shape[1]
    first = 1 + ids_ref[3]
    second = 2 - ids_ref[3]
    for at, (ref, bits) in enumerate([(own_ref, 0), (own_ref, second), (send_ref, first), (send_ref, 3)]):
        block = ids_ref[4] ^ bits
        ref[at % 2] = sum_ref[pl.ds(pl.multiple_of(block * size, 16), size), :].astype(low)


def total_body(ids_ref, mine_ref, got_ref, z_ref, r_ref):
    total = mine_ref[...] + got_ref[...].astype(single)
    shared = z_ref.shape[1]
    z_ref[...] = total[:, :shared].astype(low)
    r_ref[...] = total[:, shared:].astype(low)


def add_body(ids_ref, own_ref, got_ref, out_ref):
    out_ref[...] = (own_ref[...].astype(single) + got_ref[...].astype(single)).astype(low)


def join_body(ids_ref, own_ref, got_ref, r_ref, out_ref):
    shared = own_ref.shape[1]
    out_ref[:, :shared] = (own_ref[...].astype(single) + got_ref[...].astype(single)).astype(low)
    out_ref[:, shared:] = r_ref[...]


def assemble_body(ids_ref, p0, p1, p2, p3, out_ref):
    quarter = p0.shape[0]
    width = out_ref.shape[1]
    for k, p_ref in enumerate([p0, p1, p2, p3]):
        out_ref[rows_of(ids_ref, k, quarter), :] = p_ref[:, :width]


def padded(size):
    return -(-size // 128) * 128


def finish_body(ids_ref, *refs):
    m0, m1, m2, n0, n1, n2 = refs[:6]
    outs = refs[6:]
    size = m0.shape[0]
    core = ids_ref[3]
    first = 1 + core
    second = 2 - core
    pieces = [(core, 0, m0, None), (core, second, m1, None), (core, first, m2, 0), (core, 3, m2, 1)]
    pieces = pieces + [(1 - core, 0, n0, None), (1 - core, first, n1, None), (1 - core, second, n2, 0), (1 - core, 3, n2, 1)]
    for side, bits, p_ref, at in pieces:
        block = side * 4 + (ids_ref[4] ^ bits)
        start = pl.multiple_of(block * size, 16)
        col = 0

        def read(span):
            return (p_ref[:, col : col + span] if at is None else p_ref[at, :, col : col + span]).astype(single)

        for out_ref in outs:
            if len(out_ref.shape) == 4:
                for j in range(3):
                    span = out_ref.shape[3]
                    out_ref[block, j] = read(span)
                    col += span
            elif len(out_ref.shape) == 3:
                for j in range(2):
                    span = out_ref.shape[2]
                    out_ref[pl.ds(start, size), j, :] = read(span)
                    col += padded(span)
            else:
                span = out_ref.shape[1]
                out_ref[pl.ds(start, size), :] = read(span)
                col += padded(span)


def on_device(
    tokens,
    grad_out,
    lengths,
    deal,
    adapter_of,
    attention_gain,
    attention_proj,
    attention_out,
    feed_gain,
    feed_in,
    feed_out,
    attention_proj_down,
    attention_proj_up,
    attention_out_down,
    attention_out_up,
    feed_in_down,
    feed_in_up,
    feed_out_down,
    feed_out_up,
):
    fsdp_size = lax.axis_size("fsdp")
    context_size = lax.axis_size("context")
    tensor_size = lax.axis_size("tensor")
    count, width = tokens.shape
    total = deal.shape[0]
    sets, _, rank = attention_proj_down.shape
    ranks = sets * rank
    local_width = attention_proj.shape[2]
    hidden = feed_in.shape[2]
    f = lax.axis_index("fsdp")
    c = lax.axis_index("context")
    t = lax.axis_index("tensor")
    small = context_size == 2 and fsdp_size == 4
    half_at = c % 2
    chip = (f // 2) * 2 + half_at
    chunks = total // count
    if small:
        order = [(f ^ df) * context_size + (c ^ dc) for df, dc in
                 ((0, 0), (0, 1), (2, 0), (2, 1), (1, 0), (1, 1), (3, 0), (3, 1))]
    else:
        order = list(range(chunks))
    ids = jnp.stack([jnp.asarray(value, jnp.int32) for value in [f, half_at, t, f % 2, chip, *order]])
    quarter = count // tensor_size

    def over(axis, size, bit, value):
        return lax.ppermute(value, axis, swap_pairs(axis, size, bit))

    def near(value):
        return over("fsdp", fsdp_size, 1, value)

    def ahead(value):
        return over("fsdp", fsdp_size, 2, value)

    def across(value):
        return over("context", context_size, 1, value)

    def after(value, *others):
        return lax.optimization_barrier((value, *others))[0]

    def exchange(pieces):
        return [pieces[0]] + [over("tensor", tensor_size, k, pieces[k]) for k in range(1, tensor_size)]

    def spread(piece):
        far = over("tensor", tensor_size, 2, piece)
        return [piece, over("tensor", tensor_size, 1, piece), far, over("tensor", tensor_size, 1, far)]

    def reduce_rows(keep, send, *others):
        got = over("tensor", tensor_size, 1, send)
        got, *others = lax.optimization_barrier((got, *others))
        mine, passed = call(
            pair_body, [(keep.shape[1:], single), (keep.shape[1:], low)], ids, [keep, got], name="pair"
        )
        return [mine, over("tensor", tensor_size, 2, passed)], others

    proj_own = jnp.transpose(attention_proj, (1, 0, 2))
    in_own = jnp.transpose(feed_in, (1, 2, 0))
    proj_down = jnp.transpose(attention_proj_down, (0, 2, 1)).reshape(ranks, width)
    out_down_own = jnp.transpose(attention_out_down, (0, 2, 1)).reshape(ranks, local_width)
    in_down = jnp.transpose(feed_in_down, (0, 2, 1)).reshape(ranks, width)
    last_down = jnp.transpose(feed_out_down, (0, 2, 1)).reshape(ranks, hidden)
    proj_up = jnp.transpose(attention_proj_up, (2, 0, 1, 3)).reshape(3, ranks, local_width)
    out_up = attention_out_up.reshape(ranks, width)
    last_up = feed_out_up.reshape(ranks, width)

    proj_far = ahead(proj_own)
    proj_near = near(proj_own)
    in_half, last_half = call(
        split_body,
        [((1, *in_own.shape[1:]), low), ((hidden, feed_out.shape[1] // 2), low)],
        ids,
        [in_own, feed_out],
        name="split",
        cost=2.0,
    )
    in_far = ahead(in_half)

    seqs = lengths.shape[0]
    before = jnp.arange(seqs)[:, None] >= jnp.arange(seqs)[None, :]
    ends = jnp.sum(jnp.where(before, lengths[None, :], 0), axis=1)
    starts = ends - lengths
    segment_all = jnp.sum((deal[:, None] >= ends[None, :]).astype(jnp.int32), axis=1)
    first = (f * context_size + c) * count
    segment_rows = lax.dynamic_slice_in_dim(segment_all, first, count)
    deal_rows = lax.dynamic_slice_in_dim(deal, first, count)
    member = segment_rows[:, None] == jnp.arange(seqs, dtype=jnp.int32)[None, :]
    place = deal_rows - jnp.sum(jnp.where(member, starts[None, :], 0), axis=1)
    chosen = jnp.sum(jnp.where(member, adapter_of[None, :], 0), axis=1)
    set_of = jnp.arange(ranks, dtype=jnp.int32) // rank
    picked = (chosen[:, None] == set_of[None, :]).astype(low)
    half = HEAD_DIM // 2
    lane = jnp.arange(local_width, dtype=jnp.int32) % HEAD_DIM
    freq = jnp.exp((lane % half).astype(single) * (-math.log(rope_base) / half))
    angle = place.astype(single)[:, None] * freq[None, :]
    cos_full = jnp.cos(angle)
    sin_full = jnp.sin(angle) * jnp.where(lane < half, -1.0, 1.0).astype(single)[None, :]
    gain_one = attention_gain.astype(single)[None, :]
    gain_two = feed_gain.astype(single)[None, :]
    normed_one, adapted_q = call(
        prepare_body,
        [((count, width), low), ((count, ranks), low)],
        ids,
        [after(tokens, in_half), gain_one, proj_down, picked],
        name="prepare",
        cost=5.0,
    )

    packed = spread(jnp.concatenate([after(attention_out, in_half), out_down_own], axis=0))
    proj_w = [proj_own, proj_near, proj_far, near(proj_far)]
    groups = segment_all.reshape(-1, count)
    seg_col = segment_rows[:, None]
    normed_one, groups, seg_col, picked = lax.optimization_barrier((normed_one, groups, seg_col, picked))
    in_up = jnp.transpose(feed_in_up, (2, 0, 1, 3)).reshape(2, ranks, hidden)

    query, keyval = call(
        project_body,
        [((count, local_width), low), ((count, 2 * local_width), low)],
        ids,
        [normed_one, adapted_q, proj_up, cos_full, sin_full, *proj_w],
        name="project",
        cost=3.0,
    )

    def plane_gather(value, other=None):
        if not small:
            return [lax.all_gather(value, token_axes, axis=0, tiled=True)]
        corner = lax.ppermute(value, token_axes, swap_pairs(None, fsdp_size * context_size, 2 * context_size + 1))
        chips = [value, across(value), ahead(value), corner]
        if other is None:
            return chips + [near(piece) for piece in chips]
        return chips + [near(value)] + [near(after(piece, other)) for piece in chips[1:]]

    in_near = near(after(in_own, proj_near))
    keyval, in_far, in_near = lax.optimization_barrier((keyval, in_far, in_near))
    last_near = near(after(feed_out, in_near))
    keyval_all = plane_gather(keyval)
    parts_n = len(keyval_all)
    gathered = keyval_all[1:4]
    out_w_own, out_half = call(
        stack_body,
        [((width, local_width), low), ((width // 2, local_width), low)],
        ids,
        [after(packed[0], keyval), *packed[1:]],
        name="stack",
        cost=3.0,
    )
    in_up, gain_two, last_near = lax.optimization_barrier((after(in_up, keyval), gain_two, last_near))
    out_w_own, out_half, in_far, in_up, *gathered = lax.optimization_barrier(
        (out_w_own, out_half, in_far, in_up, *gathered)
    )
    out_near = near(out_w_own)
    out_far = ahead(out_half)
    in_rest = across(in_far)

    slab = pltpu.VMEM((count, local_width), single)
    held = block_rows(count, total) * (local_width // HEAD_DIM)
    many = pltpu.VMEM((held, local_width), low)
    against = pltpu.VMEM((held, total), low)
    heads_out, attended, lse_col, keyval_joined = call(
        lambda *refs: attend_body(parts_n, *refs),
        [
            ((count, local_width), low),
            ((count, local_width), single),
            ((count, 128), single),
            ((total, 2 * local_width), low),
        ],
        ids,
        [after(query, in_up, gain_two), seg_col, groups, *keyval_all],
        scratch=[many, pltpu.VMEM((held, total), single), pltpu.SemaphoreType.DMA((parts_n,))],
        far=range(3, 3 + parts_n),
        vmem=16 if small else 60,
        name="attend",
        cost=8.0,
    )
    heads_out, out_far = lax.optimization_barrier((heads_out, out_far))
    heads = spread(heads_out)
    heads[1], heads[2], in_rest = lax.optimization_barrier((heads[1], heads[2], in_rest))
    last_far = ahead(after(last_half, heads_out))
    out_rest = across(out_far)
    last_rest = across(last_far)
    out_late, in_late, last_late, in_rest = after((out_far, in_far, last_far, in_rest), heads[1])
    out_w = [out_w_own, out_near, out_far, out_rest, near(out_late), near(out_rest)]
    in_w = [in_own, in_near, in_far, in_rest, near(in_late), near(in_rest)]
    last_w = [feed_out, last_near, last_far, last_rest, near(last_late), near(last_rest)]
    wide = width + ranks
    piece = ((2, quarter, wide), low)
    mid_outs = call(
        middle_body,
        [piece] * 2
        + [((count, ranks), low)] * 3
        + [
            ((count, width), low),
            ((count, hidden), low),
            ((2, count, hidden), low),
            ((quarter, width), single),
            ((4, width, local_width), low),
            ((4, *feed_out.shape), low),
        ],
        ids,
        [*heads, *out_w, *packed, out_up, tokens, gain_two, grad_out, picked, *in_w, in_down, in_up, *last_w,
         last_down, last_up],
        scratch=[
            pltpu.VMEM((count, wide), single),
            pltpu.VMEM((4, *in_own.shape), low),
            pltpu.SemaphoreType.DMA((18,)),
        ],
        far=(*range(4, 10), *range(19, 25), *range(27, 33)),
        vmem=20 if small else 60,
        name="middle",
    )
    adapted_o, adapted_i, grad_adapt_d, normed_two, activity, grad_gates, middle_q, out_all, last_all = mid_outs[2:]
    if small:
        query_late = after(query, activity)
        summed, (query_x, query_y, query_n) = reduce_rows(
            *mid_outs[:2], across(query_late), ahead(query_late), near(query_late)
        )
        query_xy = ahead(query_x)
        query_all = [query, query_x, query_y, query_xy, query_n, near(query_x), near(query_y)]
    else:
        summed, _ = reduce_rows(*mid_outs[:2])
        query_all = plane_gather(query)
    feed_pieces = call(
        feed_body,
        [piece] * 2,
        ids,
        [after(activity, summed[0]), last_down, last_all],
        scratch=[pltpu.VMEM((count, wide), single)],
        name="feed",
    )
    summed, query_all, feed_pieces = lax.optimization_barrier((summed, query_all, feed_pieces))
    turn = ((quarter, local_width + ranks), low)
    *turned, grad_mid, grad_branch, grad_adapt_i = call(
        turn_body,
        [turn] * 4 + [((quarter, width), single), ((quarter, width), low), ((quarter, ranks), low)],
        ids,
        [*summed, picked, in_down, middle_q, gain_two, grad_out, out_up, out_all, *packed],
        vmem=6 if small else 40,
        name="turn",
        cost=3.0,
    )
    if small:
        query_all = query_all + [near(after(query_all[3], grad_mid))]
    arrived = exchange(turned)
    sizes = [width] * 4 + [padded(hidden)] * 3 + [3 * local_width, local_width]
    columns = sum(sizes)
    places = [(i, j) for i in range(fsdp_size) for j in range(context_size)]
    number = {place: at for at, place in enumerate(places)}
    side = {(i, j): (i, j ^ 1) for i, j in places}
    front = {(i, j): (i ^ 2, j) for i, j in places}
    one = [(number[p], number[front[p] if p[0] % 2 else side[p]]) for p in places]
    two = [(number[p], number[side[p] if p[0] % 2 else front[p]]) for p in places]
    rows = ranks // 8

    def fold_strips(keep, send):
        columns = keep.shape[1]
        return call(
            fold_body,
            [((2, rows, columns), low)] * 2,
            ids,
            [keep, near(send)],
            scratch=[pltpu.VMEM((ranks // 2, columns), single)],
            name="fold",
            cost=3.0,
        )

    def reduce_strips(own, got):
        columns = own.shape[2]
        mine, passed = call(
            pair_body,
            [((rows, columns), single), ((rows, columns), low)],
            ids,
            [own, got],
            name="pair_chips",
            cost=3.0,
        )
        return [mine, lax.ppermute(passed, token_axes, two)]

    (feed_mine, feed_got), _ = reduce_rows(*feed_pieces)
    arrived, query_all, feed_mine = lax.optimization_barrier((arrived, query_all, feed_mine))
    tail = 32
    message, delta_col, grad_adapt_o = call(
        collect_body,
        [((count + tail, local_width), low), ((count, 128), single), ((count, ranks), low)],
        ids,
        [*arrived, attended, lse_col],
        name="collect",
        cost=3.0,
    )
    (grad_query,) = call(
        query_body,
        [((count, local_width), single)],
        ids,
        [query, message, lse_col, delta_col, seg_col, groups, keyval_joined],
        scratch=[many, many, against],
        vmem=12 if small else 60,
        name="queries",
        cost=7.0,
    )
    message_all = [value.reshape(-1, count + tail, local_width) for value in plane_gather(message, grad_query)]
    output_q, adapted_d = call(
        out_body,
        [((quarter, width), low), ((quarter, ranks), low)],
        ids,
        [feed_mine, after(feed_got, grad_query), picked, middle_q, last_up],
        name="outputs",
    )
    output_all = spread(output_q)
    *last_pieces, grad_proj, part_adapt_q = call(
        lambda *refs: key_body(parts_n, *refs),
        [piece] * 2 + [((count, 3 * local_width), low), ((count, ranks), low)],
        ids,
        [after(keyval, output_q), seg_col, groups, grad_query, cos_full, sin_full, proj_up, picked, *proj_w, *query_all, *message_all],
        scratch=[
            pltpu.VMEM((8, total), single),
            slab,
            slab,
            pltpu.VMEM((count, wide), single),
            many,
            many,
            against,
            against,
            pltpu.VMEM((total, local_width), low),
            pltpu.VMEM((chunks, count, local_width), low),
            pltpu.VMEM((chunks, tail, local_width), low),
            pltpu.SemaphoreType.DMA((3 * parts_n,)),
        ],
        far=range(12, 12 + 2 * parts_n),
        vmem=22 if small else 60,
        name="keys",
        cost=10.0,
    )
    part_adapt_q, *output_all[1:3] = lax.optimization_barrier((part_adapt_q, *output_all[1:3]))
    output_all[3] = over("tensor", tensor_size, 1, output_all[2])
    last_mine, last_got = reduce_rows(*last_pieces)[0]
    late = call(
        grads_body,
        [((ranks // 2, columns), low)] * 2,
        ids,
        [grad_adapt_i, normed_two, adapted_o, grad_branch, adapted_d, grad_out,
         part_adapt_q, normed_one, adapted_i,
         grad_gates, grad_adapt_d, activity, adapted_q, grad_proj, grad_adapt_o, heads_out],
        scratch=[pltpu.VMEM((ranks, columns), single)],
        vmem=8 if small else 40,
        name="grads",
        cost=3.0,
    )
    def finish_tokens(got):
        return call(
            last_body,
            [((quarter, width), low)],
            ids,
            [last_mine, got, picked, proj_down, tokens, gain_one, grad_mid],
            name="last",
        )

    finals = [((ranks, width), single)] * 4 + [((ranks, 2, hidden), single), ((ranks, hidden), single)]
    finals = finals + [((sets, 3, rank, local_width), single), ((ranks, local_width), single)]
    if small:
        late_own, late_out = fold_strips(*late)
        late_mine, late_got = reduce_strips(late_own, lax.ppermute(late_out, token_axes, one))
        shared, rest = call(
            total_body,
            [((rows, 4 * width), low), ((rows, columns - 4 * width), low)],
            ids,
            [late_mine, late_got],
            name="total",
            cost=3.0,
        )
        shared_near, last_got = lax.optimization_barrier((over("tensor", tensor_size, 1, shared), last_got))
        (grad_tokens_q,) = finish_tokens(last_got)
        (shared,) = call(add_body, [((rows, 4 * width), low)], ids, [shared, shared_near], name="add")
        shared_far = over("tensor", tensor_size, 2, shared)
        (output,) = call(assemble_body, [((count, width), low)], ids, output_all, name="join_output")
        rest, output, grad_tokens_q = lax.optimization_barrier((rest, output, grad_tokens_q))
        tokens_all = spread(grad_tokens_q)
        (joined,) = call(
            join_body,
            [((rows, columns), low)],
            ids,
            [shared, shared_far, rest],
            name="join",
            cost=3.0,
        )
        beside = lax.ppermute(joined, token_axes, two)
        both = jnp.stack([joined, after(beside, tokens_all[1], tokens_all[2])])
        others = lax.ppermute(both, token_axes, one)
        strips = [joined, beside, after(others, tokens_all[3])]
        strips = strips + [near(value) for value in strips]
        results = call(finish_body, finals, ids, strips, name="finish")
    else:
        (grad_tokens_q,) = finish_tokens(last_got)
        tokens_all = spread(grad_tokens_q)
        (output,) = call(assemble_body, [((count, width), low)], ids, output_all, name="join_output")
        pair = jnp.where(f % 2 == 0, jnp.concatenate(late), jnp.concatenate(late[::-1]))
        pair = lax.psum(pair, token_axes)
        joined = jnp.concatenate([lax.psum(pair[:, : 4 * width], "tensor"), pair[:, 4 * width :]], axis=1)
        cut = [0]
        for span in [width] * 4 + [padded(hidden)] * 3 + [3 * local_width, local_width]:
            cut.append(cut[-1] + span)
        slices = [joined[:, lo:hi].astype(single) for lo, hi in zip(cut, cut[1:])]
        *results, gate_up, mult_up, last_grad, proj_up_grad, out_down_grad = slices
        results = [*results, jnp.stack([gate_up[:, :hidden], mult_up[:, :hidden]], axis=1), last_grad[:, :hidden]]
        proj_up_grad = jnp.transpose(proj_up_grad.reshape(sets, rank, 3, local_width), (0, 2, 1, 3))
        results = [*results, proj_up_grad, out_down_grad]

    in_down_grad, out_up_grad, last_up_grad, proj_down_grad, in_up_grad, last_grad, proj_up_grad, out_down_grad = results
    (grad_tokens,) = call(assemble_body, [((count, width), low)], ids, tokens_all, name="join_tokens")


    def down(grad):
        return jnp.transpose(grad.reshape(sets, rank, -1), (0, 2, 1))

    return (
        output,
        grad_tokens,
        down(proj_down_grad),
        jnp.transpose(proj_up_grad, (0, 2, 1, 3)),
        down(out_down_grad),
        out_up_grad.reshape(sets, rank, width),
        down(in_down_grad),
        in_up_grad.reshape(sets, rank, 2, hidden),
        down(last_grad),
        last_up_grad.reshape(sets, rank, width),
    )


def solution(mesh):
    return jax.shard_map(
        on_device,
        mesh=mesh,
        in_specs=(
            P(("fsdp", "context"), None),
            P(("fsdp", "context"), None),
            P(),
            P(),
            P(),
            P(),
            P("fsdp", None, "tensor"),
            P("tensor", "fsdp"),
            P(),
            P("fsdp", None, "tensor"),
            P("tensor", "fsdp"),
            P(),
            P(None, None, None, "tensor"),
            P(None, "tensor", None),
            P(),
            P(),
            P(None, None, None, "tensor"),
            P(None, "tensor", None),
            P(),
        ),
        out_specs=(
            P(("fsdp", "context"), None),
            P(("fsdp", "context"), None),
            P(),
            P(None, None, None, "tensor"),
            P(None, "tensor", None),
            P(),
            P(),
            P(None, None, None, "tensor"),
            P(None, "tensor", None),
            P(),
        ),
        check_vma=False,
    )
```

```python
import math

import jax
import jax.numpy as jnp
from jax import lax
from jax.experimental import pallas as pl
from jax.experimental.pallas import tpu as pltpu
from jax.sharding import PartitionSpec as P

HEAD_DIM = 64


rope_base = 160000.0
epsilon = 1e-05
negative = -1e30
single = jnp.float32
low = jnp.bfloat16
scale = HEAD_DIM ** (-0.5)
token_axes = ("fsdp", "context")
every_axis = ("fsdp", "context", "tensor")


def nn(left, right):
    return lax.dot_general(
        left, right, (((1,), (0,)), ((), ())), preferred_element_type=jnp.float32
    )


def nt(left, right):
    return lax.dot_general(
        left, right, (((1,), (1,)), ((), ())), preferred_element_type=jnp.float32
    )


def tn(left, right):
    return lax.dot_general(
        left, right, (((0,), (0,)), ((), ())), preferred_element_type=jnp.float32
    )


def call(body, outs, ids, args, scratch=(), vmem=6, name=None, far=(), cost=0.0):
    whole = pl.BlockSpec(memory_space=pltpu.VMEM)
    return pl.pallas_call(
        body,
        out_shape=[jax.ShapeDtypeStruct(shape, kind) for shape, kind in outs],
        in_specs=[pl.BlockSpec(memory_space=pltpu.SMEM)]
        + [pl.BlockSpec(memory_space=pltpu.HBM) if at in far else whole for at in range(len(args))],
        out_specs=[whole] * len(outs),
        scratch_shapes=list(scratch),
        compiler_params=pltpu.CompilerParams(vmem_limit_bytes=vmem << 20),
        cost_estimate=pl.CostEstimate(flops=int(cost * 1e12) + 1, bytes_accessed=int(cost * 1e12) + 1, transcendentals=0),
        name=name,
    )(ids, *args)


def swap_pairs(axis, size, bit):
    return [(i, i ^ bit) for i in range(size)]


def layer_norm_rows(values):
    centered = values - jnp.mean(values, axis=1, keepdims=True)
    rstd = lax.rsqrt(jnp.mean(centered * centered, axis=1, keepdims=True) + epsilon)
    return (centered * rstd, rstd)


def layer_norm_back(upstream, gain, xhat, rstd):
    scaled = upstream * gain
    return rstd * (
        scaled
        - jnp.mean(scaled, axis=1, keepdims=True)
        - xhat * jnp.mean(scaled * xhat, axis=1, keepdims=True)
    )


def swap_halves(u):
    width = u.shape[1]
    half = HEAD_DIM // 2
    lane = lax.broadcasted_iota(jnp.int32, (1, width), 1)
    return jnp.where(
        lane % HEAD_DIM < half, pltpu.roll(u, width - half, 1), pltpu.roll(u, half, 1)
    )


def head_row(width, head):
    lane = lax.broadcasted_iota(jnp.int32, (1, width), 1)
    return (lane // HEAD_DIM == head).astype(single)


def start_copies(pairs, sems):
    copies = [pltpu.make_async_copy(src, dst, sems.at[n]) for n, (src, dst) in enumerate(pairs)]
    for copy in copies:
        copy.start()
    return copies


def loop(count, step, most=8):
    if count <= most:
        for number in range(count):
            step(number)
    else:

        def inner(number, carry):
            step(number)
            return carry

        lax.fori_loop(0, count, inner, 0)


def at_block(number, size):
    start = number * size
    return pl.ds(start if isinstance(start, int) else pl.multiple_of(start, 16), size)


def block_rows(count, total):
    return max(16, min(count, 2048 * count // total))


def cols_of(ids_ref, k, width):
    return pl.ds(pl.multiple_of((ids_ref[0] ^ k) * width, 128), width)


def rows_of(ids_ref, k, height):
    return pl.ds(pl.multiple_of((ids_ref[2] ^ k) * height, 16), height)


def join_rows(ids_ref, dst_ref, mine_ref, other_ref):
    size = mine_ref.shape[0]
    dst_ref[pl.ds(ids_ref[1] * size, size)] = mine_ref[...]
    dst_ref[pl.ds((1 - ids_ref[1]) * size, size)] = other_ref[...]


def join_cols(ids_ref, dst_ref, mine_ref, other_ref):
    size = mine_ref.shape[1]
    dst_ref[:, pl.ds(pl.multiple_of(ids_ref[1] * size, 128), size)] = mine_ref[...]
    dst_ref[:, pl.ds(pl.multiple_of((1 - ids_ref[1]) * size, 128), size)] = other_ref[...]


def project_body(ids_ref, x_ref, aq_ref, up_ref, cos_ref, sin_ref, *refs):
    weights, q_ref, kv_ref = (refs[:-2], refs[-2], refs[-1])
    part = weights[0].shape[1]
    width = weights[0].shape[2]
    for j in range(3):
        acc = nn(aq_ref[...], up_ref[j])
        for k, w_ref in enumerate(weights):
            acc = acc + nn(x_ref[:, cols_of(ids_ref, k, part)], w_ref[j])
        if j < 2:
            acc = acc * cos_ref[...] + swap_halves(acc) * sin_ref[...]
        if j == 0:
            q_ref[...] = acc.astype(low)
        else:
            kv_ref[:, (j - 1) * width : j * width] = acc.astype(low)


def prepare_body(ids_ref, tokens_ref, gain_ref, down_ref, picked_ref, n1_ref, aq_ref):
    xhat, _ = layer_norm_rows(tokens_ref[...].astype(single))
    normed = (xhat * gain_ref[...]).astype(low)
    n1_ref[...] = normed
    aq_ref[...] = (picked_ref[...].astype(single) * nt(normed, down_ref[...])).astype(low)


def split_body(ids_ref, in_ref, last_ref, ihalf_ref, lhalf_ref):
    ihalf_ref[...] = in_ref[pl.ds(ids_ref[1], 1)]
    cols = lhalf_ref.shape[1]
    lhalf_ref[...] = last_ref[:, pl.ds(pl.multiple_of(ids_ref[1] * cols, 128), cols)]


def stack_body(ids_ref, p0, p1, p2, p3, full_ref, half_ref):
    rows = p0.shape[1]
    for k, p_ref in enumerate([p0, p1, p2, p3]):
        full_ref[k * rows : (k + 1) * rows, :] = p_ref[:rows, :]
    size = half_ref.shape[0]
    half_ref[...] = full_ref[pl.ds(pl.multiple_of(ids_ref[1] * size, 16), size), :]


def put_pieces(ids_ref, wide_ref, keep_ref, send_ref):
    quarter = keep_ref.shape[1]
    for at, (ref, k) in enumerate([(keep_ref, 0), (keep_ref, 2), (send_ref, 1), (send_ref, 3)]):
        ref[at % 2] = wide_ref[rows_of(ids_ref, k, quarter), :].astype(low)


def pair_body(ids_ref, keep_ref, got_ref, mine_ref, pass_ref):
    mine_ref[...] = keep_ref[0].astype(single) + got_ref[0].astype(single)
    pass_ref[...] = (keep_ref[1].astype(single) + got_ref[1].astype(single)).astype(low)


def attend_body(parts_n, ids_ref, q_ref, segc_ref, groups_ref, *refs):
    parts = refs[:parts_n]
    heads_ref, att_ref, lcol_ref, kv_ref, many_ref, s_ref, sems = refs[parts_n:]
    count, width = q_ref.shape
    heads = width // HEAD_DIM
    chunk = groups_ref.shape[1]
    size = many_ref.shape[0] // heads
    base = 0
    pairs = []
    for part in parts:
        pairs.append((part, kv_ref.at[base : base + part.shape[0], :]))
        base += part.shape[0]
    copies = start_copies(pairs, sems)
    lane = lax.broadcasted_iota(jnp.int32, (1, 128), 1)
    waits = list(copies)

    def block(number):
        rows = at_block(number, size)
        for h in range(heads):
            many_ref[h * size : (h + 1) * size, :] = q_ref[rows, :] * (head_row(width, h) * scale).astype(low)

        def scores(j):
            cols = at_block(j, chunk)
            same = segc_ref[rows, :] == groups_ref[pl.ds(ids_ref[5 + j], 1), :]
            s = nt(many_ref[...], kv_ref[cols, :width])
            for h in range(heads):
                s_ref[h * size : (h + 1) * size, cols] = jnp.where(same, s[h * size : (h + 1) * size], negative)

        while waits:
            waits.pop(0).wait()
        loop(base // chunk, scores)
        total = jnp.zeros((size, width), single)
        lcol = jnp.zeros((size, 128), single)
        for h in range(heads):
            s = s_ref[h * size : (h + 1) * size, :]
            top = jnp.max(s, axis=1, keepdims=True)
            p = jnp.exp(s - top)
            mass = jnp.sum(p, axis=1, keepdims=True)
            total = total + nn(p.astype(low), kv_ref[:, width:]) * (head_row(width, h) / mass)
            lcol = jnp.where(lane == h, top + jnp.log(mass), lcol)
        att_ref[rows, :] = total
        lcol_ref[rows, :] = lcol
        heads_ref[rows, :] = total.astype(low)

    loop(count // size, block, 1)


def middle_body(ids_ref, *refs):
    heads = refs[0:4]
    wown, wnear, wa, wb, wc, wd = refs[4:10]
    packs = refs[10:14]
    refs = refs[3:]
    ou_ref, tokens_ref, gain_ref, go_ref, picked_ref = refs[11:16]
    iown, inear, ia, ib, ic, idd = refs[16:22]
    idn_ref, iu_ref = refs[22:24]
    lown, lnear, la, lb, lc, ld = refs[24:30]
    ldn_ref, lup_ref = refs[30:32]
    keep_ref, send_ref, ao_ref, ai_ref, gad_ref, n2_ref, act_ref, gg_ref, mid_ref, wts, lts = refs[32:43]
    wide_ref, its, sems = refs[43:]
    mine, rest = (ids_ref[1], 1 - ids_ref[1])
    half = wa.shape[0]
    step = la.shape[1]

    def rows(k, at):
        return wts.at[k, pl.ds(pl.multiple_of(at * half, 16), half), :]

    def cols(k, at):
        return lts.at[k, :, pl.ds(pl.multiple_of(at * step, 128), step)]

    pairs = [
        (wown, wts.at[0]),
        (wnear, wts.at[1]),
        (wa, rows(2, mine)),
        (wb, rows(2, rest)),
        (wc, rows(3, mine)),
        (wd, rows(3, rest)),
        (iown, its.at[0]),
        (inear, its.at[1]),
        (ia, its.at[2, pl.ds(mine, 1)]),
        (ib, its.at[2, pl.ds(rest, 1)]),
        (ic, its.at[3, pl.ds(mine, 1)]),
        (idd, its.at[3, pl.ds(rest, 1)]),
        (lown, lts.at[0]),
        (lnear, lts.at[1]),
        (la, cols(2, mine)),
        (lb, cols(2, rest)),
        (lc, cols(3, mine)),
        (ld, cols(3, rest)),
    ]
    copies = [pltpu.make_async_copy(src, dst, sems.at[n]) for n, (src, dst) in enumerate(pairs)]
    for copy in copies:
        copy.start()
    h0 = heads[0]
    w0 = wown
    outs_w = [wts.at[k] for k in range(4)]
    ins_w = [its.at[k] for k in range(4)]
    lasts_w = [lts.at[k] for k in range(4)]
    part = w0.shape[1]
    span = h0.shape[1]
    width = tokens_ref.shape[1]
    picked = picked_ref[...].astype(single)
    span = h0.shape[1]
    adapt = nt(h0[...], packs[0][span:, :])
    for k in range(1, len(heads)):
        adapt = adapt + nt(heads[k][...], packs[k][span:, :])
    ao = (picked * adapt).astype(low)
    ao_ref[...] = ao
    for copy in copies[:6]:
        copy.wait()
    for k, w_ref in enumerate(outs_w):
        acc = nn(h0[...], w_ref[:span, :])
        for r in range(1, len(heads)):
            acc = acc + nn(heads[r][...], w_ref[r * span : (r + 1) * span, :])
        wide_ref[:, cols_of(ids_ref, k, part)] = acc
    middle = tokens_ref[...].astype(single) + wide_ref[:, :width] + nn(ao, ou_ref[...])
    wide_ref[:, :width] = middle
    quarter = mid_ref.shape[0]
    mid_ref[...] = wide_ref[rows_of(ids_ref, 0, quarter), :width]
    xhat, _ = layer_norm_rows(middle)
    n2 = (xhat * gain_ref[...]).astype(low)
    n2_ref[...] = n2
    ai = (picked * nt(n2, idn_ref[...])).astype(low)
    ai_ref[...] = ai
    for copy in copies[6:]:
        copy.wait()
    gate = nn(ai, iu_ref[0])
    mult = nn(ai, iu_ref[1])
    for k, w_ref in enumerate(ins_w):
        x = n2_ref[:, cols_of(ids_ref, k, part)]
        gate = gate + nt(x, w_ref[0])
        mult = mult + nt(x, w_ref[1])
    phi = 0.5 * (1.0 + lax.erf(gate * (2.0**-0.5)))
    gated = gate * phi
    act_ref[...] = (gated * mult).astype(low)
    slope = phi + gate * jnp.exp(-0.5 * gate * gate) * (1.0 / math.sqrt(2.0 * math.pi))
    go = go_ref[...]
    gad = (nt(go, lup_ref[...]).astype(low).astype(single) * picked).astype(low)
    gad_ref[...] = gad
    ga = nn(gad, ldn_ref[...])
    for k, w_ref in enumerate(lasts_w):
        ga = ga + nt(go_ref[:, cols_of(ids_ref, k, part)], w_ref[...])
    gg0 = (slope * (ga * mult)).astype(low)
    gg1 = (ga * gated).astype(low)
    gg_ref[0] = gg0
    gg_ref[1] = gg1
    for k, w_ref in enumerate(ins_w):
        wide_ref[:, cols_of(ids_ref, k, part)] = nn(gg0, w_ref[0]) + nn(gg1, w_ref[1])
    wide_ref[:, width:] = nt(gg0, iu_ref[0]) + nt(gg1, iu_ref[1])
    put_pieces(ids_ref, wide_ref, keep_ref, send_ref)


def feed_body(ids_ref, act_ref, ldn_ref, lts, keep_ref, send_ref, wide_ref):
    part = lts.shape[2]
    act = act_ref[...]
    wide_ref[:, wide_ref.shape[1] - ldn_ref.shape[0] :] = nt(act, ldn_ref[...])
    for k in range(4):
        wide_ref[:, cols_of(ids_ref, k, part)] = nn(act, lts[k])
    put_pieces(ids_ref, wide_ref, keep_ref, send_ref)


def turn_body(
    ids_ref, p0, p1, picked_ref, idn_ref, mid_ref, gain_ref, go_ref, ou_ref, wts, d0, d1, d2, d3,
    a0, a1, a2, a3, gm_ref, gb_ref, gai_ref,
):
    quarter = p0.shape[0]
    width = mid_ref.shape[1]
    part = wts.shape[2]
    rows = rows_of(ids_ref, 0, quarter)
    picked = picked_ref[rows, :].astype(single)
    total = p0[...] + p1[...].astype(single)
    gai = (total[:, width:].astype(low).astype(single) * picked).astype(low)
    gai_ref[...] = gai
    upstream = total[:, :width] + nn(gai, idn_ref[...])
    xhat, rstd = layer_norm_rows(mid_ref[...])
    gm = go_ref[rows, :].astype(single) + layer_norm_back(upstream, gain_ref[...], xhat, rstd)
    gm_ref[...] = gm
    gb = gm.astype(low)
    gb_ref[...] = gb
    gao = (nt(gb, ou_ref[...]).astype(low).astype(single) * picked).astype(low)
    span = d0.shape[1]
    grads = [nn(gao, d_ref[span:, :]) for d_ref in (d0, d1, d2, d3)]
    for k in range(4):
        w_ref = wts.at[k]
        x = gb_ref[:, cols_of(ids_ref, k, part)]
        for r in range(4):
            grads[r] = grads[r] + nt(x, w_ref[r * span : (r + 1) * span, :])
    for k, a_ref in enumerate([a0, a1, a2, a3]):
        a_ref[:, :span] = grads[k].astype(low)
        a_ref[:, span:] = gao


def out_body(ids_ref, p0, p1, picked_ref, mid_ref, lup_ref, out_ref, ad_ref):
    width = mid_ref.shape[1]
    picked = picked_ref[rows_of(ids_ref, 0, p0.shape[0]), :].astype(single)
    total = p0[...] + p1[...].astype(single)
    ad = (picked * total[:, width:]).astype(low)
    ad_ref[...] = ad
    out_ref[...] = (mid_ref[...] + total[:, :width] + nn(ad, lup_ref[...])).astype(low)


def collect_body(ids_ref, a0, a1, a2, a3, att_ref, lcol_ref, msg_ref, dcol_ref, gao_ref):
    quarter = a0.shape[0]
    count, width = att_ref.shape
    for k, a_ref in enumerate([a0, a1, a2, a3]):
        msg_ref[rows_of(ids_ref, k, quarter), :] = a_ref[:, :width]
        gao_ref[rows_of(ids_ref, k, quarter), :] = a_ref[:, width:]
    both = msg_ref[:count, :].astype(single) * att_ref[...]
    heads = width // HEAD_DIM
    lane = lax.broadcasted_iota(jnp.int32, (1, 128), 1)
    dcol = jnp.zeros((count, 128), single)
    pair = lcol_ref[...]
    for h in range(heads):
        delta = jnp.sum(both * head_row(width, h), axis=1, keepdims=True)
        dcol = jnp.where(lane == h, delta, dcol)
        pair = jnp.where(lane == heads + h, delta, pair)
    dcol_ref[...] = dcol
    rows = jnp.transpose(pair)[:8, :]
    first = rows.astype(low).astype(single)
    rest = rows - first
    second = rest.astype(low).astype(single)
    third = rest - second
    tail = jnp.concatenate([first, second, third, jnp.zeros_like(first)], axis=0)
    msg_ref[count:, :] = tail.astype(low)


def query_body(
    ids_ref, q_ref, msg_ref, lcol_ref, dcol_ref, segc_ref, groups_ref, kv_ref, dq_ref, many_ref, more_ref, ds_ref
):
    count, width = q_ref.shape
    heads = width // HEAD_DIM
    chunk = groups_ref.shape[1]
    size = many_ref.shape[0] // heads

    def block(number):
        rows = at_block(number, size)
        for h in range(heads):
            many_ref[h * size : (h + 1) * size, :] = q_ref[rows, :] * (head_row(width, h) * scale).astype(low)
            more_ref[h * size : (h + 1) * size, :] = msg_ref[rows, :] * head_row(width, h).astype(low)

        def scores(j):
            cols = at_block(j, chunk)
            same = segc_ref[rows, :] == groups_ref[pl.ds(ids_ref[5 + j], 1), :]
            s = nt(many_ref[...], kv_ref[cols, :width])
            dp = nt(more_ref[...], kv_ref[cols, width:])
            for h in range(heads):
                mine = slice(h * size, (h + 1) * size)
                p = jnp.exp(jnp.where(same, s[mine] - lcol_ref[rows, h : h + 1], negative))
                ds_ref[mine, cols] = (p * (dp[mine] - dcol_ref[rows, h : h + 1])).astype(low)

        loop(kv_ref.shape[0] // chunk, scores)
        dq = nn(ds_ref[...], kv_ref[:, :width])
        total = jnp.zeros((size, width), single)
        for h in range(heads):
            total = total + dq[h * size : (h + 1) * size] * (head_row(width, h) * scale)
        dq_ref[rows, :] = total

    loop(count // size, block, 1)


def key_body(
    parts_n, ids_ref, own_ref, segc_ref, groups_ref, dq_ref, cos_ref, sin_ref, up_ref, picked_ref, w0, w1, w2, w3, *refs
):
    parts = refs[:parts_n]
    msgs = refs[parts_n : 2 * parts_n]
    keep_ref, send_ref, gp_ref, paq_ref, stat_ref, dk_ref, dv_ref, wide_ref, many_ref, more_ref, p_ref, ds_ref = refs[
        2 * parts_n : 2 * parts_n + 12
    ]
    q_ref, do_ref, tail_ref, sems = refs[2 * parts_n + 12 :]
    count = own_ref.shape[0]
    width = dq_ref.shape[1]
    heads = width // HEAD_DIM
    base = 0
    pairs = []
    for part, msg in zip(parts, msgs):
        held = msg.shape[0]
        pairs.append((part, q_ref.at[base * count : (base + held) * count, :]))
        pairs.append((msg.at[:, :count, :], do_ref.at[base : base + held]))
        pairs.append((msg.at[:, count:, :], tail_ref.at[base : base + held]))
        base += held
    copies = start_copies(pairs, sems)
    for copy in copies:
        copy.wait()
    for j in range(base):
        e = tail_ref[j].astype(single)
        stat_ref[:, j * count : (j + 1) * count] = e[:8] + e[8:16] + e[16:24]

    size = many_ref.shape[0] // heads

    def block(number):
        rows = at_block(number, size)
        for h in range(heads):
            hm = head_row(width, h)
            many_ref[h * size : (h + 1) * size, :] = own_ref[rows, :width] * (hm * scale).astype(low)
            more_ref[h * size : (h + 1) * size, :] = own_ref[rows, width:] * hm.astype(low)

        def scores(j):
            cols = at_block(j, count)
            same = segc_ref[rows, :] == groups_ref[pl.ds(ids_ref[5 + j], 1), :]
            s = nt(many_ref[...], q_ref[cols, :])
            dp = nt(more_ref[...], do_ref[j])
            for h in range(heads):
                mine = slice(h * size, (h + 1) * size)
                p = jnp.exp(jnp.where(same, s[mine] - stat_ref[h : h + 1, cols], negative))
                p_ref[mine, cols] = p.astype(low)
                ds_ref[mine, cols] = (p * (dp[mine] - stat_ref[heads + h : heads + h + 1, cols])).astype(low)

        loop(base, scores)
        dv = nn(p_ref[...], do_ref[...].reshape(base * count, width))
        dk = nn(ds_ref[...], q_ref[...])
        dv_total = jnp.zeros((size, width), single)
        dk_total = jnp.zeros((size, width), single)
        for h in range(heads):
            hm = head_row(width, h)
            dv_total = dv_total + dv[h * size : (h + 1) * size] * hm
            dk_total = dk_total + dk[h * size : (h + 1) * size] * (hm * scale)
        dv_ref[rows, :] = dv_total
        dk_ref[rows, :] = dk_total

    loop(count // size, block, 1)
    cosine = cos_ref[...]
    sine = sin_ref[...]
    gq = (dq_ref[...] * cosine - swap_halves(dq_ref[...]) * sine).astype(low)
    gk = (dk_ref[...] * cosine - swap_halves(dk_ref[...]) * sine).astype(low)
    gv = dv_ref[...].astype(low)
    gp_ref[:, :width] = gq
    gp_ref[:, width : 2 * width] = gk
    gp_ref[:, 2 * width :] = gv
    part = w0.shape[1]
    full = wide_ref.shape[1] - up_ref.shape[1]
    for k, w_ref in enumerate([w0, w1, w2, w3]):
        wide_ref[:, cols_of(ids_ref, k, part)] = nt(gq, w_ref[0]) + nt(gk, w_ref[1]) + nt(gv, w_ref[2])
    adapt = nt(gq, up_ref[0]) + nt(gk, up_ref[1]) + nt(gv, up_ref[2])
    wide_ref[:, full:] = adapt
    paq_ref[...] = (adapt * picked_ref[...].astype(single)).astype(low)
    put_pieces(ids_ref, wide_ref, keep_ref, send_ref)


def last_body(ids_ref, p0, p1, picked_ref, pdn_ref, tokens_ref, gain_ref, gm_ref, gt_ref):
    quarter = p0.shape[0]
    width = gm_ref.shape[1]
    rows = rows_of(ids_ref, 0, quarter)
    picked = picked_ref[rows, :].astype(single)
    total = p0[...] + p1[...].astype(single)
    gaq = (total[:, width:].astype(low).astype(single) * picked).astype(low)
    upstream = total[:, :width] + nn(gaq, pdn_ref[...])
    xhat, rstd = layer_norm_rows(tokens_ref[rows, :].astype(single))
    gt_ref[...] = (gm_ref[...] + layer_norm_back(upstream, gain_ref[...], xhat, rstd)).astype(low)


def assemble_body(ids_ref, p0, p1, p2, p3, out_ref):
    quarter = p0.shape[0]
    width = out_ref.shape[1]
    for k, p_ref in enumerate([p0, p1, p2, p3]):
        out_ref[rows_of(ids_ref, k, quarter), :] = p_ref[:, :width]


def padded(size):
    return -(-size // 128) * 128


def lay_out(ids_ref, values, keep_ref, send_ref, all_ref):
    ranks = all_ref.shape[0]
    at = 0
    for value in values:
        size = value.shape[1]
        all_ref[:, at : at + size] = value
        if padded(size) != size:
            all_ref[:, at + size : at + padded(size)] = jnp.zeros((ranks, padded(size) - size), single)
        at += padded(size)
    half = ranks // 2
    keep_ref[...] = all_ref[pl.ds(pl.multiple_of(ids_ref[3] * half, 16), half), :].astype(low)
    send_ref[...] = all_ref[pl.ds(pl.multiple_of((1 - ids_ref[3]) * half, 16), half), :].astype(low)


def grads_body(
    ids_ref, gai_ref, n2_ref, ao_ref, gb_ref, ad_ref, go_ref, paq_ref, n1_ref, ai_ref, gg_ref, gad_ref, act_ref,
    aq_ref, gp_ref, gao_ref, heads_ref, keep_ref, send_ref, all_ref,
):
    rows = rows_of(ids_ref, 0, gb_ref.shape[0])
    values = [
        tn(gai_ref[...], n2_ref[rows, :]),
        tn(ao_ref[rows, :], gb_ref[...]),
        tn(ad_ref[...], go_ref[rows, :]),
        tn(paq_ref[...], n1_ref[...]),
        tn(ai_ref[...], gg_ref[0]),
        tn(ai_ref[...], gg_ref[1]),
        tn(gad_ref[...], act_ref[...]),
        tn(aq_ref[...], gp_ref[...]),
        tn(gao_ref[...], heads_ref[...]),
    ]
    lay_out(ids_ref, values, keep_ref, send_ref, all_ref)


def fold_body(ids_ref, keep_ref, got_ref, own_ref, send_ref, sum_ref):
    sum_ref[...] = keep_ref[...].astype(single) + got_ref[...].astype(single)
    size = own_ref.shape[1]
    first = 1 + ids_ref[3]
    second = 2 - ids_ref[3]
    for at, (ref, bits) in enumerate([(own_ref, 0), (own_ref, second), (send_ref, first), (send_ref, 3)]):
        block = ids_ref[4] ^ bits
        ref[at % 2] = sum_ref[pl.ds(pl.multiple_of(block * size, 16), size), :].astype(low)


def total_body(ids_ref, mine_ref, got_ref, z_ref, r_ref):
    total = mine_ref[...] + got_ref[...].astype(single)
    shared = z_ref.shape[1]
    z_ref[...] = total[:, :shared].astype(low)
    r_ref[...] = total[:, shared:].astype(low)


def add_body(ids_ref, own_ref, got_ref, out_ref):
    out_ref[...] = (own_ref[...].astype(single) + got_ref[...].astype(single)).astype(low)


def join_body(ids_ref, own_ref, got_ref, r_ref, out_ref):
    shared = own_ref.shape[1]
    out_ref[:, :shared] = (own_ref[...].astype(single) + got_ref[...].astype(single)).astype(low)
    out_ref[:, shared:] = r_ref[...]


def assemble_body(ids_ref, p0, p1, p2, p3, out_ref):
    quarter = p0.shape[0]
    width = out_ref.shape[1]
    for k, p_ref in enumerate([p0, p1, p2, p3]):
        out_ref[rows_of(ids_ref, k, quarter), :] = p_ref[:, :width]


def padded(size):
    return -(-size // 128) * 128


def finish_body(ids_ref, *refs):
    m0, m1, m2, n0, n1, n2 = refs[:6]
    outs = refs[6:]
    size = m0.shape[0]
    core = ids_ref[3]
    first = 1 + core
    second = 2 - core
    pieces = [(core, 0, m0, None), (core, second, m1, None), (core, first, m2, 0), (core, 3, m2, 1)]
    pieces = pieces + [(1 - core, 0, n0, None), (1 - core, first, n1, None), (1 - core, second, n2, 0), (1 - core, 3, n2, 1)]
    for side, bits, p_ref, at in pieces:
        block = side * 4 + (ids_ref[4] ^ bits)
        start = pl.multiple_of(block * size, 16)
        col = 0

        def read(span):
            return (p_ref[:, col : col + span] if at is None else p_ref[at, :, col : col + span]).astype(single)

        for out_ref in outs:
            if len(out_ref.shape) == 4:
                for j in range(3):
                    span = out_ref.shape[3]
                    out_ref[block, j] = read(span)
                    col += span
            elif len(out_ref.shape) == 3:
                for j in range(2):
                    span = out_ref.shape[2]
                    out_ref[pl.ds(start, size), j, :] = read(span)
                    col += padded(span)
            else:
                span = out_ref.shape[1]
                out_ref[pl.ds(start, size), :] = read(span)
                col += padded(span)


def on_device(
    tokens,
    grad_out,
    lengths,
    deal,
    adapter_of,
    attention_gain,
    attention_proj,
    attention_out,
    feed_gain,
    feed_in,
    feed_out,
    attention_proj_down,
    attention_proj_up,
    attention_out_down,
    attention_out_up,
    feed_in_down,
    feed_in_up,
    feed_out_down,
    feed_out_up,
):
    fsdp_size = lax.axis_size("fsdp")
    context_size = lax.axis_size("context")
    tensor_size = lax.axis_size("tensor")
    count, width = tokens.shape
    total = deal.shape[0]
    sets, _, rank = attention_proj_down.shape
    ranks = sets * rank
    local_width = attention_proj.shape[2]
    hidden = feed_in.shape[2]
    f = lax.axis_index("fsdp")
    c = lax.axis_index("context")
    t = lax.axis_index("tensor")
    small = context_size == 2 and fsdp_size == 4
    half_at = c % 2
    chip = (f // 2) * 2 + half_at
    chunks = total // count
    if small:
        order = [(f ^ df) * context_size + (c ^ dc) for df, dc in
                 ((0, 0), (0, 1), (2, 0), (2, 1), (1, 0), (1, 1), (3, 0), (3, 1))]
    else:
        order = list(range(chunks))
    ids = jnp.stack([jnp.asarray(value, jnp.int32) for value in [f, half_at, t, f % 2, chip, *order]])
    quarter = count // tensor_size

    def over(axis, size, bit, value):
        return lax.ppermute(value, axis, swap_pairs(axis, size, bit))

    def near(value):
        return over("fsdp", fsdp_size, 1, value)

    def ahead(value):
        return over("fsdp", fsdp_size, 2, value)

    def across(value):
        return over("context", context_size, 1, value)

    def after(value, *others):
        return lax.optimization_barrier((value, *others))[0]

    def exchange(pieces):
        return [pieces[0]] + [over("tensor", tensor_size, k, pieces[k]) for k in range(1, tensor_size)]

    def spread(piece):
        far = over("tensor", tensor_size, 2, piece)
        return [piece, over("tensor", tensor_size, 1, piece), far, over("tensor", tensor_size, 1, far)]

    def reduce_rows(keep, send, *others):
        got = over("tensor", tensor_size, 1, send)
        got, *others = lax.optimization_barrier((got, *others))
        mine, passed = call(
            pair_body, [(keep.shape[1:], single), (keep.shape[1:], low)], ids, [keep, got], name="pair"
        )
        return [mine, over("tensor", tensor_size, 2, passed)], others

    proj_own = jnp.transpose(attention_proj, (1, 0, 2))
    in_own = jnp.transpose(feed_in, (1, 2, 0))
    proj_down = jnp.transpose(attention_proj_down, (0, 2, 1)).reshape(ranks, width)
    out_down_own = jnp.transpose(attention_out_down, (0, 2, 1)).reshape(ranks, local_width)
    in_down = jnp.transpose(feed_in_down, (0, 2, 1)).reshape(ranks, width)
    last_down = jnp.transpose(feed_out_down, (0, 2, 1)).reshape(ranks, hidden)
    proj_up = jnp.transpose(attention_proj_up, (2, 0, 1, 3)).reshape(3, ranks, local_width)
    out_up = attention_out_up.reshape(ranks, width)
    last_up = feed_out_up.reshape(ranks, width)

    proj_far = ahead(proj_own)
    proj_near = near(proj_own)
    in_half, last_half = call(
        split_body,
        [((1, *in_own.shape[1:]), low), ((hidden, feed_out.shape[1] // 2), low)],
        ids,
        [in_own, feed_out],
        name="split",
        cost=2.0,
    )
    in_far = ahead(in_half)

    seqs = lengths.shape[0]
    before = jnp.arange(seqs)[:, None] >= jnp.arange(seqs)[None, :]
    ends = jnp.sum(jnp.where(before, lengths[None, :], 0), axis=1)
    starts = ends - lengths
    segment_all = jnp.sum((deal[:, None] >= ends[None, :]).astype(jnp.int32), axis=1)
    first = (f * context_size + c) * count
    segment_rows = lax.dynamic_slice_in_dim(segment_all, first, count)
    deal_rows = lax.dynamic_slice_in_dim(deal, first, count)
    member = segment_rows[:, None] == jnp.arange(seqs, dtype=jnp.int32)[None, :]
    place = deal_rows - jnp.sum(jnp.where(member, starts[None, :], 0), axis=1)
    chosen = jnp.sum(jnp.where(member, adapter_of[None, :], 0), axis=1)
    set_of = jnp.arange(ranks, dtype=jnp.int32) // rank
    picked = (chosen[:, None] == set_of[None, :]).astype(low)
    half = HEAD_DIM // 2
    lane = jnp.arange(local_width, dtype=jnp.int32) % HEAD_DIM
    freq = jnp.exp((lane % half).astype(single) * (-math.log(rope_base) / half))
    angle = place.astype(single)[:, None] * freq[None, :]
    cos_full = jnp.cos(angle)
    sin_full = jnp.sin(angle) * jnp.where(lane < half, -1.0, 1.0).astype(single)[None, :]
    gain_one = attention_gain.astype(single)[None, :]
    gain_two = feed_gain.astype(single)[None, :]
    normed_one, adapted_q = call(
        prepare_body,
        [((count, width), low), ((count, ranks), low)],
        ids,
        [after(tokens, in_half), gain_one, proj_down, picked],
        name="prepare",
        cost=5.0,
    )

    packed = spread(jnp.concatenate([after(attention_out, in_half), out_down_own], axis=0))
    proj_w = [proj_own, proj_near, proj_far, near(proj_far)]
    groups = segment_all.reshape(-1, count)
    seg_col = segment_rows[:, None]
    normed_one, groups, seg_col, picked = lax.optimization_barrier((normed_one, groups, seg_col, picked))
    in_up = jnp.transpose(feed_in_up, (2, 0, 1, 3)).reshape(2, ranks, hidden)

    query, keyval = call(
        project_body,
        [((count, local_width), low), ((count, 2 * local_width), low)],
        ids,
        [normed_one, adapted_q, proj_up, cos_full, sin_full, *proj_w],
        name="project",
        cost=3.0,
    )

    def plane_gather(value, other=None):
        if not small:
            return [lax.all_gather(value, token_axes, axis=0, tiled=True)]
        corner = lax.ppermute(value, token_axes, swap_pairs(None, fsdp_size * context_size, 2 * context_size + 1))
        chips = [value, across(value), ahead(value), corner]
        if other is None:
            return chips + [near(piece) for piece in chips]
        return chips + [near(value)] + [near(after(piece, other)) for piece in chips[1:]]

    in_near = near(after(in_own, proj_near))
    keyval, in_far, in_near = lax.optimization_barrier((keyval, in_far, in_near))
    last_near = near(after(feed_out, in_near))
    keyval_all = plane_gather(keyval)
    parts_n = len(keyval_all)
    gathered = keyval_all[1:4]
    out_w_own, out_half = call(
        stack_body,
        [((width, local_width), low), ((width // 2, local_width), low)],
        ids,
        [after(packed[0], keyval), *packed[1:]],
        name="stack",
        cost=3.0,
    )
    in_up, gain_two, last_near = lax.optimization_barrier((after(in_up, keyval), gain_two, last_near))
    out_w_own, out_half, in_far, in_up, *gathered = lax.optimization_barrier(
        (out_w_own, out_half, in_far, in_up, *gathered)
    )
    out_near = near(out_w_own)
    out_far = ahead(out_half)
    in_rest = across(in_far)

    slab = pltpu.VMEM((count, local_width), single)
    held = block_rows(count, total) * (local_width // HEAD_DIM)
    many = pltpu.VMEM((held, local_width), low)
    against = pltpu.VMEM((held, total), low)
    heads_out, attended, lse_col, keyval_joined = call(
        lambda *refs: attend_body(parts_n, *refs),
        [
            ((count, local_width), low),
            ((count, local_width), single),
            ((count, 128), single),
            ((total, 2 * local_width), low),
        ],
        ids,
        [after(query, in_up, gain_two), seg_col, groups, *keyval_all],
        scratch=[many, pltpu.VMEM((held, total), single), pltpu.SemaphoreType.DMA((parts_n,))],
        far=range(3, 3 + parts_n),
        vmem=10 if small else 60,
        name="attend",
        cost=8.0,
    )
    heads_out, out_far = lax.optimization_barrier((heads_out, out_far))
    heads = spread(heads_out)
    heads[1], heads[2], in_rest = lax.optimization_barrier((heads[1], heads[2], in_rest))
    last_far = ahead(after(last_half, heads_out))
    out_rest = across(out_far)
    last_rest = across(last_far)
    out_late, in_late, last_late, in_rest = after((out_far, in_far, last_far, in_rest), heads[1])
    out_w = [out_w_own, out_near, out_far, out_rest, near(out_late), near(out_rest)]
    in_w = [in_own, in_near, in_far, in_rest, near(in_late), near(in_rest)]
    last_w = [feed_out, last_near, last_far, last_rest, near(last_late), near(last_rest)]
    wide = width + ranks
    piece = ((2, quarter, wide), low)
    mid_outs = call(
        middle_body,
        [piece] * 2
        + [((count, ranks), low)] * 3
        + [
            ((count, width), low),
            ((count, hidden), low),
            ((2, count, hidden), low),
            ((quarter, width), single),
            ((4, width, local_width), low),
            ((4, *feed_out.shape), low),
        ],
        ids,
        [*heads, *out_w, *packed, out_up, tokens, gain_two, grad_out, picked, *in_w, in_down, in_up, *last_w,
         last_down, last_up],
        scratch=[
            pltpu.VMEM((count, wide), single),
            pltpu.VMEM((4, *in_own.shape), low),
            pltpu.SemaphoreType.DMA((18,)),
        ],
        far=(*range(4, 10), *range(19, 25), *range(27, 33)),
        vmem=10 if small else 60,
        name="middle",
    )
    adapted_o, adapted_i, grad_adapt_d, normed_two, activity, grad_gates, middle_q, out_all, last_all = mid_outs[2:]
    if small:
        query_late = after(query, activity)
        summed, (query_x, query_y, query_n) = reduce_rows(
            *mid_outs[:2], across(query_late), ahead(query_late), near(query_late)
        )
        query_xy = ahead(query_x)
        query_all = [query, query_x, query_y, query_xy, query_n, near(query_x), near(query_y)]
    else:
        summed, _ = reduce_rows(*mid_outs[:2])
        query_all = plane_gather(query)
    feed_pieces = call(
        feed_body,
        [piece] * 2,
        ids,
        [after(activity, summed[0]), last_down, last_all],
        scratch=[pltpu.VMEM((count, wide), single)],
        name="feed",
    )
    summed, query_all, feed_pieces = lax.optimization_barrier((summed, query_all, feed_pieces))
    turn = ((quarter, local_width + ranks), low)
    *turned, grad_mid, grad_branch, grad_adapt_i = call(
        turn_body,
        [turn] * 4 + [((quarter, width), single), ((quarter, width), low), ((quarter, ranks), low)],
        ids,
        [*summed, picked, in_down, middle_q, gain_two, grad_out, out_up, out_all, *packed],
        vmem=6 if small else 40,
        name="turn",
        cost=3.0,
    )
    if small:
        query_all = query_all + [near(after(query_all[3], grad_mid))]
    arrived = exchange(turned)
    sizes = [width] * 4 + [padded(hidden)] * 3 + [3 * local_width, local_width]
    columns = sum(sizes)
    places = [(i, j) for i in range(fsdp_size) for j in range(context_size)]
    number = {place: at for at, place in enumerate(places)}
    side = {(i, j): (i, j ^ 1) for i, j in places}
    front = {(i, j): (i ^ 2, j) for i, j in places}
    one = [(number[p], number[front[p] if p[0] % 2 else side[p]]) for p in places]
    two = [(number[p], number[side[p] if p[0] % 2 else front[p]]) for p in places]
    rows = ranks // 8

    def fold_strips(keep, send):
        columns = keep.shape[1]
        return call(
            fold_body,
            [((2, rows, columns), low)] * 2,
            ids,
            [keep, near(send)],
            scratch=[pltpu.VMEM((ranks // 2, columns), single)],
            name="fold",
            cost=3.0,
        )

    def reduce_strips(own, got):
        columns = own.shape[2]
        mine, passed = call(
            pair_body,
            [((rows, columns), single), ((rows, columns), low)],
            ids,
            [own, got],
            name="pair_chips",
            cost=3.0,
        )
        return [mine, lax.ppermute(passed, token_axes, two)]

    (feed_mine, feed_got), _ = reduce_rows(*feed_pieces)
    arrived, query_all, feed_mine = lax.optimization_barrier((arrived, query_all, feed_mine))
    tail = 32
    message, delta_col, grad_adapt_o = call(
        collect_body,
        [((count + tail, local_width), low), ((count, 128), single), ((count, ranks), low)],
        ids,
        [*arrived, attended, lse_col],
        name="collect",
        cost=3.0,
    )
    (grad_query,) = call(
        query_body,
        [((count, local_width), single)],
        ids,
        [query, message, lse_col, delta_col, seg_col, groups, keyval_joined],
        scratch=[many, many, against],
        vmem=11 if small else 60,
        name="queries",
        cost=7.0,
    )
    message_all = [value.reshape(-1, count + tail, local_width) for value in plane_gather(message, grad_query)]
    output_q, adapted_d = call(
        out_body,
        [((quarter, width), low), ((quarter, ranks), low)],
        ids,
        [feed_mine, after(feed_got, grad_query), picked, middle_q, last_up],
        name="outputs",
    )
    output_all = spread(output_q)
    *last_pieces, grad_proj, part_adapt_q = call(
        lambda *refs: key_body(parts_n, *refs),
        [piece] * 2 + [((count, 3 * local_width), low), ((count, ranks), low)],
        ids,
        [after(keyval, output_q), seg_col, groups, grad_query, cos_full, sin_full, proj_up, picked, *proj_w, *query_all, *message_all],
        scratch=[
            pltpu.VMEM((8, total), single),
            slab,
            slab,
            pltpu.VMEM((count, wide), single),
            many,
            many,
            against,
            against,
            pltpu.VMEM((total, local_width), low),
            pltpu.VMEM((chunks, count, local_width), low),
            pltpu.VMEM((chunks, tail, local_width), low),
            pltpu.SemaphoreType.DMA((3 * parts_n,)),
        ],
        far=range(12, 12 + 2 * parts_n),
        vmem=21 if small else 60,
        name="keys",
        cost=10.0,
    )
    part_adapt_q, *output_all[1:3] = lax.optimization_barrier((part_adapt_q, *output_all[1:3]))
    output_all[3] = over("tensor", tensor_size, 1, output_all[2])
    last_mine, last_got = reduce_rows(*last_pieces)[0]
    late = call(
        grads_body,
        [((ranks // 2, columns), low)] * 2,
        ids,
        [grad_adapt_i, normed_two, adapted_o, grad_branch, adapted_d, grad_out,
         part_adapt_q, normed_one, adapted_i,
         grad_gates, grad_adapt_d, activity, adapted_q, grad_proj, grad_adapt_o, heads_out],
        scratch=[pltpu.VMEM((ranks, columns), single)],
        vmem=5 if small else 40,
        name="grads",
        cost=3.0,
    )
    def finish_tokens(got):
        return call(
            last_body,
            [((quarter, width), low)],
            ids,
            [last_mine, got, picked, proj_down, tokens, gain_one, grad_mid],
            name="last",
        )

    finals = [((ranks, width), single)] * 4 + [((ranks, 2, hidden), single), ((ranks, hidden), single)]
    finals = finals + [((sets, 3, rank, local_width), single), ((ranks, local_width), single)]
    if small:
        late_own, late_out = fold_strips(*late)
        late_mine, late_got = reduce_strips(late_own, lax.ppermute(late_out, token_axes, one))
        shared, rest = call(
            total_body,
            [((rows, 4 * width), low), ((rows, columns - 4 * width), low)],
            ids,
            [late_mine, late_got],
            name="total",
            cost=3.0,
        )
        shared_near, last_got = lax.optimization_barrier((over("tensor", tensor_size, 1, shared), last_got))
        (grad_tokens_q,) = finish_tokens(last_got)
        (shared,) = call(add_body, [((rows, 4 * width), low)], ids, [shared, shared_near], name="add")
        shared_far = over("tensor", tensor_size, 2, shared)
        (output,) = call(assemble_body, [((count, width), low)], ids, output_all, name="join_output")
        rest, output, grad_tokens_q = lax.optimization_barrier((rest, output, grad_tokens_q))
        tokens_all = spread(grad_tokens_q)
        (joined,) = call(
            join_body,
            [((rows, columns), low)],
            ids,
            [shared, shared_far, rest],
            name="join",
            cost=3.0,
        )
        beside = lax.ppermute(joined, token_axes, two)
        both = jnp.stack([joined, after(beside, tokens_all[1], tokens_all[2])])
        others = lax.ppermute(both, token_axes, one)
        strips = [joined, beside, after(others, tokens_all[3])]
        strips = strips + [near(value) for value in strips]
        results = call(finish_body, finals, ids, strips, name="finish")
    else:
        (grad_tokens_q,) = finish_tokens(last_got)
        tokens_all = spread(grad_tokens_q)
        (output,) = call(assemble_body, [((count, width), low)], ids, output_all, name="join_output")
        pair = jnp.where(f % 2 == 0, jnp.concatenate(late), jnp.concatenate(late[::-1]))
        pair = lax.psum(pair, token_axes)
        joined = jnp.concatenate([lax.psum(pair[:, : 4 * width], "tensor"), pair[:, 4 * width :]], axis=1)
        cut = [0]
        for span in [width] * 4 + [padded(hidden)] * 3 + [3 * local_width, local_width]:
            cut.append(cut[-1] + span)
        slices = [joined[:, lo:hi].astype(single) for lo, hi in zip(cut, cut[1:])]
        *results, gate_up, mult_up, last_grad, proj_up_grad, out_down_grad = slices
        results = [*results, jnp.stack([gate_up[:, :hidden], mult_up[:, :hidden]], axis=1), last_grad[:, :hidden]]
        proj_up_grad = jnp.transpose(proj_up_grad.reshape(sets, rank, 3, local_width), (0, 2, 1, 3))
        results = [*results, proj_up_grad, out_down_grad]

    in_down_grad, out_up_grad, last_up_grad, proj_down_grad, in_up_grad, last_grad, proj_up_grad, out_down_grad = results
    (grad_tokens,) = call(assemble_body, [((count, width), low)], ids, tokens_all, name="join_tokens")


    def down(grad):
        return jnp.transpose(grad.reshape(sets, rank, -1), (0, 2, 1))

    return (
        output,
        grad_tokens,
        down(proj_down_grad),
        jnp.transpose(proj_up_grad, (0, 2, 1, 3)),
        down(out_down_grad),
        out_up_grad.reshape(sets, rank, width),
        down(in_down_grad),
        in_up_grad.reshape(sets, rank, 2, hidden),
        down(last_grad),
        last_up_grad.reshape(sets, rank, width),
    )


def solution(mesh):
    return jax.shard_map(
        on_device,
        mesh=mesh,
        in_specs=(
            P(("fsdp", "context"), None),
            P(("fsdp", "context"), None),
            P(),
            P(),
            P(),
            P(),
            P("fsdp", None, "tensor"),
            P("tensor", "fsdp"),
            P(),
            P("fsdp", None, "tensor"),
            P("tensor", "fsdp"),
            P(),
            P(None, None, None, "tensor"),
            P(None, "tensor", None),
            P(),
            P(),
            P(None, None, None, "tensor"),
            P(None, "tensor", None),
            P(),
        ),
        out_specs=(
            P(("fsdp", "context"), None),
            P(("fsdp", "context"), None),
            P(),
            P(None, None, None, "tensor"),
            P(None, "tensor", None),
            P(),
            P(),
            P(None, None, None, "tensor"),
            P(None, "tensor", None),
            P(),
        ),
        check_vma=False,
    )
```

```python
import math

import jax
import jax.numpy as jnp
from jax import lax
from jax.experimental import pallas as pl
from jax.experimental.pallas import tpu as pltpu
from jax.sharding import PartitionSpec as P

HEAD_DIM = 64


rope_base = 160000.0
epsilon = 1e-05
negative = -1e30
single = jnp.float32
low = jnp.bfloat16
scale = HEAD_DIM ** (-0.5)
token_axes = ("fsdp", "context")
every_axis = ("fsdp", "context", "tensor")


def nn(left, right):
    return lax.dot_general(
        left, right, (((1,), (0,)), ((), ())), preferred_element_type=jnp.float32
    )


def nt(left, right):
    return lax.dot_general(
        left, right, (((1,), (1,)), ((), ())), preferred_element_type=jnp.float32
    )


def tn(left, right):
    return lax.dot_general(
        left, right, (((0,), (0,)), ((), ())), preferred_element_type=jnp.float32
    )


def call(body, outs, ids, args, scratch=(), vmem=6, name=None, far=(), cost=0.0):
    whole = pl.BlockSpec(memory_space=pltpu.VMEM)
    return pl.pallas_call(
        body,
        out_shape=[jax.ShapeDtypeStruct(shape, kind) for shape, kind in outs],
        in_specs=[pl.BlockSpec(memory_space=pltpu.SMEM)]
        + [pl.BlockSpec(memory_space=pltpu.HBM) if at in far else whole for at in range(len(args))],
        out_specs=[whole] * len(outs),
        scratch_shapes=list(scratch),
        compiler_params=pltpu.CompilerParams(vmem_limit_bytes=vmem << 20),
        cost_estimate=pl.CostEstimate(flops=int(cost * 1e12) + 1, bytes_accessed=int(cost * 1e12) + 1, transcendentals=0),
        name=name,
    )(ids, *args)


def swap_pairs(axis, size, bit):
    return [(i, i ^ bit) for i in range(size)]


def layer_norm_rows(values):
    centered = values - jnp.mean(values, axis=1, keepdims=True)
    rstd = lax.rsqrt(jnp.mean(centered * centered, axis=1, keepdims=True) + epsilon)
    return (centered * rstd, rstd)


def layer_norm_back(upstream, gain, xhat, rstd):
    scaled = upstream * gain
    return rstd * (
        scaled
        - jnp.mean(scaled, axis=1, keepdims=True)
        - xhat * jnp.mean(scaled * xhat, axis=1, keepdims=True)
    )


def swap_halves(u):
    width = u.shape[1]
    half = HEAD_DIM // 2
    lane = lax.broadcasted_iota(jnp.int32, (1, width), 1)
    return jnp.where(
        lane % HEAD_DIM < half, pltpu.roll(u, width - half, 1), pltpu.roll(u, half, 1)
    )


def head_row(width, head):
    lane = lax.broadcasted_iota(jnp.int32, (1, width), 1)
    return (lane // HEAD_DIM == head).astype(single)


def start_copies(pairs, sems):
    copies = [pltpu.make_async_copy(src, dst, sems.at[n]) for n, (src, dst) in enumerate(pairs)]
    for copy in copies:
        copy.start()
    return copies


def loop(count, step, most=8):
    if count <= most:
        for number in range(count):
            step(number)
    else:

        def inner(number, carry):
            step(number)
            return carry

        lax.fori_loop(0, count, inner, 0)


def at_block(number, size):
    start = number * size
    return pl.ds(start if isinstance(start, int) else pl.multiple_of(start, 16), size)


def block_rows(count, total):
    return max(16, min(count, 2048 * count // total))


def cols_of(ids_ref, k, width):
    return pl.ds(pl.multiple_of((ids_ref[0] ^ k) * width, 128), width)


def rows_of(ids_ref, k, height):
    return pl.ds(pl.multiple_of((ids_ref[2] ^ k) * height, 16), height)


def join_rows(ids_ref, dst_ref, mine_ref, other_ref):
    size = mine_ref.shape[0]
    dst_ref[pl.ds(ids_ref[1] * size, size)] = mine_ref[...]
    dst_ref[pl.ds((1 - ids_ref[1]) * size, size)] = other_ref[...]


def join_cols(ids_ref, dst_ref, mine_ref, other_ref):
    size = mine_ref.shape[1]
    dst_ref[:, pl.ds(pl.multiple_of(ids_ref[1] * size, 128), size)] = mine_ref[...]
    dst_ref[:, pl.ds(pl.multiple_of((1 - ids_ref[1]) * size, 128), size)] = other_ref[...]


def project_body(ids_ref, x_ref, aq_ref, up_ref, cos_ref, sin_ref, *refs):
    weights, q_ref, kv_ref = (refs[:-2], refs[-2], refs[-1])
    part = weights[0].shape[1]
    width = weights[0].shape[2]
    for j in range(3):
        acc = nn(aq_ref[...], up_ref[j])
        for k, w_ref in enumerate(weights):
            acc = acc + nn(x_ref[:, cols_of(ids_ref, k, part)], w_ref[j])
        if j < 2:
            acc = acc * cos_ref[...] + swap_halves(acc) * sin_ref[...]
        if j == 0:
            q_ref[...] = acc.astype(low)
        else:
            kv_ref[:, (j - 1) * width : j * width] = acc.astype(low)


def prepare_body(ids_ref, tokens_ref, gain_ref, down_ref, picked_ref, n1_ref, aq_ref):
    xhat, _ = layer_norm_rows(tokens_ref[...].astype(single))
    normed = (xhat * gain_ref[...]).astype(low)
    n1_ref[...] = normed
    aq_ref[...] = (picked_ref[...].astype(single) * nt(normed, down_ref[...])).astype(low)


def split_body(ids_ref, in_ref, last_ref, ihalf_ref, lhalf_ref):
    ihalf_ref[...] = in_ref[pl.ds(ids_ref[1], 1)]
    cols = lhalf_ref.shape[1]
    lhalf_ref[...] = last_ref[:, pl.ds(pl.multiple_of(ids_ref[1] * cols, 128), cols)]


def stack_body(ids_ref, p0, p1, p2, p3, full_ref, half_ref):
    rows = p0.shape[1]
    for k, p_ref in enumerate([p0, p1, p2, p3]):
        full_ref[k * rows : (k + 1) * rows, :] = p_ref[:rows, :]
    size = half_ref.shape[0]
    half_ref[...] = full_ref[pl.ds(pl.multiple_of(ids_ref[1] * size, 16), size), :]


def put_pieces(ids_ref, wide_ref, keep_ref, send_ref):
    quarter = keep_ref.shape[1]
    for at, (ref, k) in enumerate([(keep_ref, 0), (keep_ref, 2), (send_ref, 1), (send_ref, 3)]):
        ref[at % 2] = wide_ref[rows_of(ids_ref, k, quarter), :].astype(low)


def pair_body(ids_ref, keep_ref, got_ref, mine_ref, pass_ref):
    mine_ref[...] = keep_ref[0].astype(single) + got_ref[0].astype(single)
    pass_ref[...] = (keep_ref[1].astype(single) + got_ref[1].astype(single)).astype(low)


def attend_body(parts_n, ids_ref, q_ref, segc_ref, groups_ref, *refs):
    parts = refs[:parts_n]
    heads_ref, att_ref, lcol_ref, kv_ref, many_ref, s_ref, sems = refs[parts_n:]
    count, width = q_ref.shape
    heads = width // HEAD_DIM
    chunk = groups_ref.shape[1]
    size = many_ref.shape[0] // heads
    base = 0
    pairs = []
    for part in parts:
        pairs.append((part, kv_ref.at[base : base + part.shape[0], :]))
        base += part.shape[0]
    copies = start_copies(pairs, sems)
    lane = lax.broadcasted_iota(jnp.int32, (1, 128), 1)
    waits = list(copies)

    def block(number):
        rows = at_block(number, size)
        for h in range(heads):
            many_ref[h * size : (h + 1) * size, :] = q_ref[rows, :] * (head_row(width, h) * scale).astype(low)

        def scores(j):
            cols = at_block(j, chunk)
            same = segc_ref[rows, :] == groups_ref[pl.ds(ids_ref[5 + j], 1), :]
            s = nt(many_ref[...], kv_ref[cols, :width])
            for h in range(heads):
                s_ref[h * size : (h + 1) * size, cols] = jnp.where(same, s[h * size : (h + 1) * size], negative)

        while waits:
            waits.pop(0).wait()
        loop(base // chunk, scores)
        total = jnp.zeros((size, width), single)
        lcol = jnp.zeros((size, 128), single)
        for h in range(heads):
            s = s_ref[h * size : (h + 1) * size, :]
            top = jnp.max(s, axis=1, keepdims=True)
            p = jnp.exp(s - top)
            mass = jnp.sum(p, axis=1, keepdims=True)
            total = total + nn(p.astype(low), kv_ref[:, width:]) * (head_row(width, h) / mass)
            lcol = jnp.where(lane == h, top + jnp.log(mass), lcol)
        att_ref[rows, :] = total
        lcol_ref[rows, :] = lcol
        heads_ref[rows, :] = total.astype(low)

    loop(count // size, block, 1)


def middle_body(ids_ref, *refs):
    heads = refs[0:4]
    wown, wnear, wa, wb, wc, wd = refs[4:10]
    packs = refs[10:14]
    refs = refs[3:]
    ou_ref, tokens_ref, gain_ref, go_ref, picked_ref = refs[11:16]
    iown, inear, ia, ib, ic, idd = refs[16:22]
    idn_ref, iu_ref = refs[22:24]
    lown, lnear, la, lb, lc, ld = refs[24:30]
    ldn_ref, lup_ref = refs[30:32]
    keep_ref, send_ref, ao_ref, ai_ref, gad_ref, n2_ref, act_ref, gg_ref, mid_ref, wts, lts = refs[32:43]
    wide_ref, its, sems = refs[43:]
    mine, rest = (ids_ref[1], 1 - ids_ref[1])
    half = wa.shape[0]
    step = la.shape[1]

    def rows(k, at):
        return wts.at[k, pl.ds(pl.multiple_of(at * half, 16), half), :]

    def cols(k, at):
        return lts.at[k, :, pl.ds(pl.multiple_of(at * step, 128), step)]

    pairs = [
        (wown, wts.at[0]),
        (wnear, wts.at[1]),
        (wa, rows(2, mine)),
        (wb, rows(2, rest)),
        (wc, rows(3, mine)),
        (wd, rows(3, rest)),
        (iown, its.at[0]),
        (inear, its.at[1]),
        (ia, its.at[2, pl.ds(mine, 1)]),
        (ib, its.at[2, pl.ds(rest, 1)]),
        (ic, its.at[3, pl.ds(mine, 1)]),
        (idd, its.at[3, pl.ds(rest, 1)]),
        (lown, lts.at[0]),
        (lnear, lts.at[1]),
        (la, cols(2, mine)),
        (lb, cols(2, rest)),
        (lc, cols(3, mine)),
        (ld, cols(3, rest)),
    ]
    copies = [pltpu.make_async_copy(src, dst, sems.at[n]) for n, (src, dst) in enumerate(pairs)]
    for copy in copies:
        copy.start()
    h0 = heads[0]
    w0 = wown
    outs_w = [wts.at[k] for k in range(4)]
    ins_w = [its.at[k] for k in range(4)]
    lasts_w = [lts.at[k] for k in range(4)]
    part = w0.shape[1]
    span = h0.shape[1]
    width = tokens_ref.shape[1]
    picked = picked_ref[...].astype(single)
    span = h0.shape[1]
    adapt = nt(h0[...], packs[0][span:, :])
    for k in range(1, len(heads)):
        adapt = adapt + nt(heads[k][...], packs[k][span:, :])
    ao = (picked * adapt).astype(low)
    ao_ref[...] = ao
    for copy in copies[:6]:
        copy.wait()
    for k, w_ref in enumerate(outs_w):
        acc = nn(h0[...], w_ref[:span, :])
        for r in range(1, len(heads)):
            acc = acc + nn(heads[r][...], w_ref[r * span : (r + 1) * span, :])
        wide_ref[:, cols_of(ids_ref, k, part)] = acc
    middle = tokens_ref[...].astype(single) + wide_ref[:, :width] + nn(ao, ou_ref[...])
    wide_ref[:, :width] = middle
    quarter = mid_ref.shape[0]
    mid_ref[...] = wide_ref[rows_of(ids_ref, 0, quarter), :width]
    xhat, _ = layer_norm_rows(middle)
    n2 = (xhat * gain_ref[...]).astype(low)
    n2_ref[...] = n2
    ai = (picked * nt(n2, idn_ref[...])).astype(low)
    ai_ref[...] = ai
    for copy in copies[6:]:
        copy.wait()
    gate = nn(ai, iu_ref[0])
    mult = nn(ai, iu_ref[1])
    for k, w_ref in enumerate(ins_w):
        x = n2_ref[:, cols_of(ids_ref, k, part)]
        gate = gate + nt(x, w_ref[0])
        mult = mult + nt(x, w_ref[1])
    phi = 0.5 * (1.0 + lax.erf(gate * (2.0**-0.5)))
    gated = gate * phi
    act_ref[...] = (gated * mult).astype(low)
    slope = phi + gate * jnp.exp(-0.5 * gate * gate) * (1.0 / math.sqrt(2.0 * math.pi))
    go = go_ref[...]
    gad = (nt(go, lup_ref[...]).astype(low).astype(single) * picked).astype(low)
    gad_ref[...] = gad
    ga = nn(gad, ldn_ref[...])
    for k, w_ref in enumerate(lasts_w):
        ga = ga + nt(go_ref[:, cols_of(ids_ref, k, part)], w_ref[...])
    gg0 = (slope * (ga * mult)).astype(low)
    gg1 = (ga * gated).astype(low)
    gg_ref[0] = gg0
    gg_ref[1] = gg1
    for k, w_ref in enumerate(ins_w):
        wide_ref[:, cols_of(ids_ref, k, part)] = nn(gg0, w_ref[0]) + nn(gg1, w_ref[1])
    wide_ref[:, width:] = nt(gg0, iu_ref[0]) + nt(gg1, iu_ref[1])
    put_pieces(ids_ref, wide_ref, keep_ref, send_ref)


def feed_body(ids_ref, act_ref, ldn_ref, lts, keep_ref, send_ref, wide_ref):
    part = lts.shape[2]
    act = act_ref[...]
    wide_ref[:, wide_ref.shape[1] - ldn_ref.shape[0] :] = nt(act, ldn_ref[...])
    for k in range(4):
        wide_ref[:, cols_of(ids_ref, k, part)] = nn(act, lts[k])
    put_pieces(ids_ref, wide_ref, keep_ref, send_ref)


def turn_body(
    ids_ref, p0, p1, picked_ref, idn_ref, mid_ref, gain_ref, go_ref, ou_ref, wts, d0, d1, d2, d3,
    a0, a1, a2, a3, gm_ref, gb_ref, gai_ref,
):
    quarter = p0.shape[0]
    width = mid_ref.shape[1]
    part = wts.shape[2]
    rows = rows_of(ids_ref, 0, quarter)
    picked = picked_ref[rows, :].astype(single)
    total = p0[...] + p1[...].astype(single)
    gai = (total[:, width:].astype(low).astype(single) * picked).astype(low)
    gai_ref[...] = gai
    upstream = total[:, :width] + nn(gai, idn_ref[...])
    xhat, rstd = layer_norm_rows(mid_ref[...])
    gm = go_ref[rows, :].astype(single) + layer_norm_back(upstream, gain_ref[...], xhat, rstd)
    gm_ref[...] = gm
    gb = gm.astype(low)
    gb_ref[...] = gb
    gao = (nt(gb, ou_ref[...]).astype(low).astype(single) * picked).astype(low)
    span = d0.shape[1]
    grads = [nn(gao, d_ref[span:, :]) for d_ref in (d0, d1, d2, d3)]
    for k in range(4):
        w_ref = wts.at[k]
        x = gb_ref[:, cols_of(ids_ref, k, part)]
        for r in range(4):
            grads[r] = grads[r] + nt(x, w_ref[r * span : (r + 1) * span, :])
    for k, a_ref in enumerate([a0, a1, a2, a3]):
        a_ref[:, :span] = grads[k].astype(low)
        a_ref[:, span:] = gao


def out_body(ids_ref, p0, p1, picked_ref, mid_ref, lup_ref, out_ref, ad_ref):
    width = mid_ref.shape[1]
    picked = picked_ref[rows_of(ids_ref, 0, p0.shape[0]), :].astype(single)
    total = p0[...] + p1[...].astype(single)
    ad = (picked * total[:, width:]).astype(low)
    ad_ref[...] = ad
    out_ref[...] = (mid_ref[...] + total[:, :width] + nn(ad, lup_ref[...])).astype(low)


def collect_body(ids_ref, a0, a1, a2, a3, att_ref, lcol_ref, msg_ref, dcol_ref, gao_ref):
    quarter = a0.shape[0]
    count, width = att_ref.shape
    for k, a_ref in enumerate([a0, a1, a2, a3]):
        msg_ref[rows_of(ids_ref, k, quarter), :] = a_ref[:, :width]
        gao_ref[rows_of(ids_ref, k, quarter), :] = a_ref[:, width:]
    both = msg_ref[:count, :].astype(single) * att_ref[...]
    heads = width // HEAD_DIM
    lane = lax.broadcasted_iota(jnp.int32, (1, 128), 1)
    dcol = jnp.zeros((count, 128), single)
    pair = lcol_ref[...]
    for h in range(heads):
        delta = jnp.sum(both * head_row(width, h), axis=1, keepdims=True)
        dcol = jnp.where(lane == h, delta, dcol)
        pair = jnp.where(lane == heads + h, delta, pair)
    dcol_ref[...] = dcol
    rows = jnp.transpose(pair)[:8, :]
    first = rows.astype(low).astype(single)
    rest = rows - first
    second = rest.astype(low).astype(single)
    third = rest - second
    tail = jnp.concatenate([first, second, third, jnp.zeros_like(first)], axis=0)
    msg_ref[count:, :] = tail.astype(low)


def query_body(
    ids_ref, q_ref, msg_ref, lcol_ref, dcol_ref, segc_ref, groups_ref, kv_ref, dq_ref, many_ref, more_ref, ds_ref
):
    count, width = q_ref.shape
    heads = width // HEAD_DIM
    chunk = groups_ref.shape[1]
    size = many_ref.shape[0] // heads

    def block(number):
        rows = at_block(number, size)
        for h in range(heads):
            many_ref[h * size : (h + 1) * size, :] = q_ref[rows, :] * (head_row(width, h) * scale).astype(low)
            more_ref[h * size : (h + 1) * size, :] = msg_ref[rows, :] * head_row(width, h).astype(low)

        def scores(j):
            cols = at_block(j, chunk)
            same = segc_ref[rows, :] == groups_ref[pl.ds(ids_ref[5 + j], 1), :]
            s = nt(many_ref[...], kv_ref[cols, :width])
            dp = nt(more_ref[...], kv_ref[cols, width:])
            for h in range(heads):
                mine = slice(h * size, (h + 1) * size)
                p = jnp.exp(jnp.where(same, s[mine] - lcol_ref[rows, h : h + 1], negative))
                ds_ref[mine, cols] = (p * (dp[mine] - dcol_ref[rows, h : h + 1])).astype(low)

        loop(kv_ref.shape[0] // chunk, scores)
        dq = nn(ds_ref[...], kv_ref[:, :width])
        total = jnp.zeros((size, width), single)
        for h in range(heads):
            total = total + dq[h * size : (h + 1) * size] * (head_row(width, h) * scale)
        dq_ref[rows, :] = total

    loop(count // size, block, 1)


def key_body(
    parts_n, ids_ref, own_ref, segc_ref, groups_ref, dq_ref, cos_ref, sin_ref, up_ref, picked_ref, w0, w1, w2, w3, *refs
):
    parts = refs[:parts_n]
    msgs = refs[parts_n : 2 * parts_n]
    keep_ref, send_ref, gp_ref, paq_ref, stat_ref, dk_ref, dv_ref, wide_ref, many_ref, more_ref, p_ref, ds_ref = refs[
        2 * parts_n : 2 * parts_n + 12
    ]
    q_ref, do_ref, tail_ref, sems = refs[2 * parts_n + 12 :]
    count = own_ref.shape[0]
    width = dq_ref.shape[1]
    heads = width // HEAD_DIM
    base = 0
    pairs = []
    for part, msg in zip(parts, msgs):
        held = msg.shape[0]
        pairs.append((part, q_ref.at[base * count : (base + held) * count, :]))
        pairs.append((msg.at[:, :count, :], do_ref.at[base : base + held]))
        pairs.append((msg.at[:, count:, :], tail_ref.at[base : base + held]))
        base += held
    copies = start_copies(pairs, sems)
    for copy in copies:
        copy.wait()
    for j in range(base):
        e = tail_ref[j].astype(single)
        stat_ref[:, j * count : (j + 1) * count] = e[:8] + e[8:16] + e[16:24]

    size = many_ref.shape[0] // heads

    def block(number):
        rows = at_block(number, size)
        for h in range(heads):
            hm = head_row(width, h)
            many_ref[h * size : (h + 1) * size, :] = own_ref[rows, :width] * (hm * scale).astype(low)
            more_ref[h * size : (h + 1) * size, :] = own_ref[rows, width:] * hm.astype(low)

        def scores(j):
            cols = at_block(j, count)
            same = segc_ref[rows, :] == groups_ref[pl.ds(ids_ref[5 + j], 1), :]
            s = nt(many_ref[...], q_ref[cols, :])
            dp = nt(more_ref[...], do_ref[j])
            for h in range(heads):
                mine = slice(h * size, (h + 1) * size)
                p = jnp.exp(jnp.where(same, s[mine] - stat_ref[h : h + 1, cols], negative))
                p_ref[mine, cols] = p.astype(low)
                ds_ref[mine, cols] = (p * (dp[mine] - stat_ref[heads + h : heads + h + 1, cols])).astype(low)

        loop(base, scores)
        dv = nn(p_ref[...], do_ref[...].reshape(base * count, width))
        dk = nn(ds_ref[...], q_ref[...])
        dv_total = jnp.zeros((size, width), single)
        dk_total = jnp.zeros((size, width), single)
        for h in range(heads):
            hm = head_row(width, h)
            dv_total = dv_total + dv[h * size : (h + 1) * size] * hm
            dk_total = dk_total + dk[h * size : (h + 1) * size] * (hm * scale)
        dv_ref[rows, :] = dv_total
        dk_ref[rows, :] = dk_total

    loop(count // size, block, 1)
    cosine = cos_ref[...]
    sine = sin_ref[...]
    gq = (dq_ref[...] * cosine - swap_halves(dq_ref[...]) * sine).astype(low)
    gk = (dk_ref[...] * cosine - swap_halves(dk_ref[...]) * sine).astype(low)
    gv = dv_ref[...].astype(low)
    gp_ref[:, :width] = gq
    gp_ref[:, width : 2 * width] = gk
    gp_ref[:, 2 * width :] = gv
    part = w0.shape[1]
    full = wide_ref.shape[1] - up_ref.shape[1]
    for k, w_ref in enumerate([w0, w1, w2, w3]):
        wide_ref[:, cols_of(ids_ref, k, part)] = nt(gq, w_ref[0]) + nt(gk, w_ref[1]) + nt(gv, w_ref[2])
    adapt = nt(gq, up_ref[0]) + nt(gk, up_ref[1]) + nt(gv, up_ref[2])
    wide_ref[:, full:] = adapt
    paq_ref[...] = (adapt * picked_ref[...].astype(single)).astype(low)
    put_pieces(ids_ref, wide_ref, keep_ref, send_ref)


def last_body(ids_ref, p0, p1, picked_ref, pdn_ref, tokens_ref, gain_ref, gm_ref, gt_ref):
    quarter = p0.shape[0]
    width = gm_ref.shape[1]
    rows = rows_of(ids_ref, 0, quarter)
    picked = picked_ref[rows, :].astype(single)
    total = p0[...] + p1[...].astype(single)
    gaq = (total[:, width:].astype(low).astype(single) * picked).astype(low)
    upstream = total[:, :width] + nn(gaq, pdn_ref[...])
    xhat, rstd = layer_norm_rows(tokens_ref[rows, :].astype(single))
    gt_ref[...] = (gm_ref[...] + layer_norm_back(upstream, gain_ref[...], xhat, rstd)).astype(low)


def assemble_body(ids_ref, p0, p1, p2, p3, out_ref):
    quarter = p0.shape[0]
    width = out_ref.shape[1]
    for k, p_ref in enumerate([p0, p1, p2, p3]):
        out_ref[rows_of(ids_ref, k, quarter), :] = p_ref[:, :width]


def padded(size):
    return -(-size // 128) * 128


def lay_out(ids_ref, values, keep_ref, send_ref, all_ref):
    ranks = all_ref.shape[0]
    at = 0
    for value in values:
        size = value.shape[1]
        all_ref[:, at : at + size] = value
        if padded(size) != size:
            all_ref[:, at + size : at + padded(size)] = jnp.zeros((ranks, padded(size) - size), single)
        at += padded(size)
    half = ranks // 2
    keep_ref[...] = all_ref[pl.ds(pl.multiple_of(ids_ref[3] * half, 16), half), :].astype(low)
    send_ref[...] = all_ref[pl.ds(pl.multiple_of((1 - ids_ref[3]) * half, 16), half), :].astype(low)


def grads_body(
    ids_ref, gai_ref, n2_ref, ao_ref, gb_ref, ad_ref, go_ref, paq_ref, n1_ref, ai_ref, gg_ref, gad_ref, act_ref,
    aq_ref, gp_ref, gao_ref, heads_ref, keep_ref, send_ref, all_ref,
):
    rows = rows_of(ids_ref, 0, gb_ref.shape[0])
    values = [
        tn(gai_ref[...], n2_ref[rows, :]),
        tn(ao_ref[rows, :], gb_ref[...]),
        tn(ad_ref[...], go_ref[rows, :]),
        tn(paq_ref[...], n1_ref[...]),
        tn(ai_ref[...], gg_ref[0]),
        tn(ai_ref[...], gg_ref[1]),
        tn(gad_ref[...], act_ref[...]),
        tn(aq_ref[...], gp_ref[...]),
        tn(gao_ref[...], heads_ref[...]),
    ]
    lay_out(ids_ref, values, keep_ref, send_ref, all_ref)


def fold_body(ids_ref, keep_ref, got_ref, own_ref, send_ref, sum_ref):
    sum_ref[...] = keep_ref[...].astype(single) + got_ref[...].astype(single)
    size = own_ref.shape[1]
    first = 1 + ids_ref[3]
    second = 2 - ids_ref[3]
    for at, (ref, bits) in enumerate([(own_ref, 0), (own_ref, second), (send_ref, first), (send_ref, 3)]):
        block = ids_ref[4] ^ bits
        ref[at % 2] = sum_ref[pl.ds(pl.multiple_of(block * size, 16), size), :].astype(low)


def total_body(ids_ref, mine_ref, got_ref, z_ref, r_ref):
    total = mine_ref[...] + got_ref[...].astype(single)
    shared = z_ref.shape[1]
    z_ref[...] = total[:, :shared].astype(low)
    r_ref[...] = total[:, shared:].astype(low)


def add_body(ids_ref, own_ref, got_ref, out_ref):
    out_ref[...] = (own_ref[...].astype(single) + got_ref[...].astype(single)).astype(low)


def join_body(ids_ref, own_ref, got_ref, r_ref, out_ref):
    shared = own_ref.shape[1]
    out_ref[:, :shared] = (own_ref[...].astype(single) + got_ref[...].astype(single)).astype(low)
    out_ref[:, shared:] = r_ref[...]


def assemble_body(ids_ref, p0, p1, p2, p3, out_ref):
    quarter = p0.shape[0]
    width = out_ref.shape[1]
    for k, p_ref in enumerate([p0, p1, p2, p3]):
        out_ref[rows_of(ids_ref, k, quarter), :] = p_ref[:, :width]


def padded(size):
    return -(-size // 128) * 128


def finish_body(ids_ref, *refs):
    m0, m1, m2, n0, n1, n2 = refs[:6]
    outs = refs[6:]
    size = m0.shape[0]
    core = ids_ref[3]
    first = 1 + core
    second = 2 - core
    pieces = [(core, 0, m0, None), (core, second, m1, None), (core, first, m2, 0), (core, 3, m2, 1)]
    pieces = pieces + [(1 - core, 0, n0, None), (1 - core, first, n1, None), (1 - core, second, n2, 0), (1 - core, 3, n2, 1)]
    for side, bits, p_ref, at in pieces:
        block = side * 4 + (ids_ref[4] ^ bits)
        start = pl.multiple_of(block * size, 16)
        col = 0

        def read(span):
            return (p_ref[:, col : col + span] if at is None else p_ref[at, :, col : col + span]).astype(single)

        for out_ref in outs:
            if len(out_ref.shape) == 4:
                for j in range(3):
                    span = out_ref.shape[3]
                    out_ref[block, j] = read(span)
                    col += span
            elif len(out_ref.shape) == 3:
                for j in range(2):
                    span = out_ref.shape[2]
                    out_ref[pl.ds(start, size), j, :] = read(span)
                    col += padded(span)
            else:
                span = out_ref.shape[1]
                out_ref[pl.ds(start, size), :] = read(span)
                col += padded(span)


def on_device(
    tokens,
    grad_out,
    lengths,
    deal,
    adapter_of,
    attention_gain,
    attention_proj,
    attention_out,
    feed_gain,
    feed_in,
    feed_out,
    attention_proj_down,
    attention_proj_up,
    attention_out_down,
    attention_out_up,
    feed_in_down,
    feed_in_up,
    feed_out_down,
    feed_out_up,
):
    fsdp_size = lax.axis_size("fsdp")
    context_size = lax.axis_size("context")
    tensor_size = lax.axis_size("tensor")
    count, width = tokens.shape
    total = deal.shape[0]
    sets, _, rank = attention_proj_down.shape
    ranks = sets * rank
    local_width = attention_proj.shape[2]
    hidden = feed_in.shape[2]
    f = lax.axis_index("fsdp")
    c = lax.axis_index("context")
    t = lax.axis_index("tensor")
    small = context_size == 2 and fsdp_size == 4
    half_at = c % 2
    chip = (f // 2) * 2 + half_at
    chunks = total // count
    if small:
        order = [(f ^ df) * context_size + (c ^ dc) for df, dc in
                 ((0, 0), (0, 1), (2, 0), (2, 1), (1, 0), (1, 1), (3, 0), (3, 1))]
    else:
        order = list(range(chunks))
    ids = jnp.stack([jnp.asarray(value, jnp.int32) for value in [f, half_at, t, f % 2, chip, *order]])
    quarter = count // tensor_size

    def over(axis, size, bit, value):
        return lax.ppermute(value, axis, swap_pairs(axis, size, bit))

    def near(value):
        return over("fsdp", fsdp_size, 1, value)

    def ahead(value):
        return over("fsdp", fsdp_size, 2, value)

    def across(value):
        return over("context", context_size, 1, value)

    def after(value, *others):
        return lax.optimization_barrier((value, *others))[0]

    def exchange(pieces):
        return [pieces[0]] + [over("tensor", tensor_size, k, pieces[k]) for k in range(1, tensor_size)]

    def spread(piece):
        far = over("tensor", tensor_size, 2, piece)
        return [piece, over("tensor", tensor_size, 1, piece), far, over("tensor", tensor_size, 1, far)]

    def reduce_rows(keep, send, *others):
        got = over("tensor", tensor_size, 1, send)
        got, *others = lax.optimization_barrier((got, *others))
        mine, passed = call(
            pair_body, [(keep.shape[1:], single), (keep.shape[1:], low)], ids, [keep, got], name="pair"
        )
        return [mine, over("tensor", tensor_size, 2, passed)], others

    proj_own = jnp.transpose(attention_proj, (1, 0, 2))
    in_own = jnp.transpose(feed_in, (1, 2, 0))
    proj_down = jnp.transpose(attention_proj_down, (0, 2, 1)).reshape(ranks, width)
    out_down_own = jnp.transpose(attention_out_down, (0, 2, 1)).reshape(ranks, local_width)
    in_down = jnp.transpose(feed_in_down, (0, 2, 1)).reshape(ranks, width)
    last_down = jnp.transpose(feed_out_down, (0, 2, 1)).reshape(ranks, hidden)
    proj_up = jnp.transpose(attention_proj_up, (2, 0, 1, 3)).reshape(3, ranks, local_width)
    out_up = attention_out_up.reshape(ranks, width)
    last_up = feed_out_up.reshape(ranks, width)

    proj_far = ahead(proj_own)
    proj_near = near(proj_own)
    in_half, last_half = call(
        split_body,
        [((1, *in_own.shape[1:]), low), ((hidden, feed_out.shape[1] // 2), low)],
        ids,
        [in_own, feed_out],
        name="split",
        cost=2.0,
    )
    in_far = ahead(in_half)

    seqs = lengths.shape[0]
    before = jnp.arange(seqs)[:, None] >= jnp.arange(seqs)[None, :]
    ends = jnp.sum(jnp.where(before, lengths[None, :], 0), axis=1)
    starts = ends - lengths
    segment_all = jnp.sum((deal[:, None] >= ends[None, :]).astype(jnp.int32), axis=1)
    first = (f * context_size + c) * count
    segment_rows = lax.dynamic_slice_in_dim(segment_all, first, count)
    deal_rows = lax.dynamic_slice_in_dim(deal, first, count)
    member = segment_rows[:, None] == jnp.arange(seqs, dtype=jnp.int32)[None, :]
    place = deal_rows - jnp.sum(jnp.where(member, starts[None, :], 0), axis=1)
    chosen = jnp.sum(jnp.where(member, adapter_of[None, :], 0), axis=1)
    set_of = jnp.arange(ranks, dtype=jnp.int32) // rank
    picked = (chosen[:, None] == set_of[None, :]).astype(low)
    half = HEAD_DIM // 2
    lane = jnp.arange(local_width, dtype=jnp.int32) % HEAD_DIM
    freq = jnp.exp((lane % half).astype(single) * (-math.log(rope_base) / half))
    angle = place.astype(single)[:, None] * freq[None, :]
    cos_full = jnp.cos(angle)
    sin_full = jnp.sin(angle) * jnp.where(lane < half, -1.0, 1.0).astype(single)[None, :]
    gain_one = attention_gain.astype(single)[None, :]
    gain_two = feed_gain.astype(single)[None, :]
    normed_one, adapted_q = call(
        prepare_body,
        [((count, width), low), ((count, ranks), low)],
        ids,
        [after(tokens, in_half), gain_one, proj_down, picked],
        name="prepare",
        cost=5.0,
    )

    packed = spread(jnp.concatenate([after(attention_out, in_half), out_down_own], axis=0))
    proj_w = [proj_own, proj_near, proj_far, near(proj_far)]
    groups = segment_all.reshape(-1, count)
    seg_col = segment_rows[:, None]
    normed_one, groups, seg_col, picked = lax.optimization_barrier((normed_one, groups, seg_col, picked))
    in_up = jnp.transpose(feed_in_up, (2, 0, 1, 3)).reshape(2, ranks, hidden)

    query, keyval = call(
        project_body,
        [((count, local_width), low), ((count, 2 * local_width), low)],
        ids,
        [normed_one, adapted_q, proj_up, cos_full, sin_full, *proj_w],
        name="project",
        cost=3.0,
    )

    def plane_gather(value, other=None):
        if not small:
            return [lax.all_gather(value, token_axes, axis=0, tiled=True)]
        corner = lax.ppermute(value, token_axes, swap_pairs(None, fsdp_size * context_size, 2 * context_size + 1))
        chips = [value, across(value), ahead(value), corner]
        if other is None:
            return chips + [near(after(value, chips[3]))] + [near(piece) for piece in chips[1:]]
        return chips + [near(value)] + [near(after(piece, other)) for piece in chips[1:]]

    in_near = near(after(in_own, proj_near))
    keyval, in_far, in_near = lax.optimization_barrier((keyval, in_far, in_near))
    last_near = near(after(feed_out, in_near))
    keyval_all = plane_gather(keyval)
    parts_n = len(keyval_all)
    gathered = keyval_all[1:4]
    out_w_own, out_half = call(
        stack_body,
        [((width, local_width), low), ((width // 2, local_width), low)],
        ids,
        [after(packed[0], keyval), *packed[1:]],
        name="stack",
        cost=3.0,
    )
    in_up, gain_two, last_near = lax.optimization_barrier((after(in_up, keyval), gain_two, last_near))
    out_w_own, out_half, in_far, in_up, *gathered = lax.optimization_barrier(
        (out_w_own, out_half, in_far, in_up, *gathered)
    )
    out_near = near(out_w_own)
    out_far = ahead(out_half)
    in_rest = across(in_far)

    slab = pltpu.VMEM((count, local_width), single)
    held = block_rows(count, total) * (local_width // HEAD_DIM)
    many = pltpu.VMEM((held, local_width), low)
    against = pltpu.VMEM((held, total), low)
    heads_out, attended, lse_col, keyval_joined = call(
        lambda *refs: attend_body(parts_n, *refs),
        [
            ((count, local_width), low),
            ((count, local_width), single),
            ((count, 128), single),
            ((total, 2 * local_width), low),
        ],
        ids,
        [after(query, in_up, gain_two), seg_col, groups, *keyval_all],
        scratch=[many, pltpu.VMEM((held, total), single), pltpu.SemaphoreType.DMA((parts_n,))],
        far=range(3, 3 + parts_n),
        vmem=10 if small else 60,
        name="attend",
        cost=8.0,
    )
    heads_out, out_far = lax.optimization_barrier((heads_out, out_far))
    heads = spread(heads_out)
    heads[1], heads[2], in_rest = lax.optimization_barrier((heads[1], heads[2], in_rest))
    last_far = ahead(after(last_half, heads_out))
    out_rest = across(out_far)
    last_rest = across(last_far)
    out_late, in_late, last_late, in_rest = after((out_far, in_far, last_far, in_rest), heads[1])
    out_w = [out_w_own, out_near, out_far, out_rest, near(out_late), near(out_rest)]
    in_w = [in_own, in_near, in_far, in_rest, near(in_late), near(in_rest)]
    last_w = [feed_out, last_near, last_far, last_rest, near(last_late), near(last_rest)]
    wide = width + ranks
    piece = ((2, quarter, wide), low)
    mid_outs = call(
        middle_body,
        [piece] * 2
        + [((count, ranks), low)] * 3
        + [
            ((count, width), low),
            ((count, hidden), low),
            ((2, count, hidden), low),
            ((quarter, width), single),
            ((4, width, local_width), low),
            ((4, *feed_out.shape), low),
        ],
        ids,
        [*heads, *out_w, *packed, out_up, tokens, gain_two, grad_out, picked, *in_w, in_down, in_up, *last_w,
         last_down, last_up],
        scratch=[
            pltpu.VMEM((count, wide), single),
            pltpu.VMEM((4, *in_own.shape), low),
            pltpu.SemaphoreType.DMA((18,)),
        ],
        far=(*range(4, 10), *range(19, 25), *range(27, 33)),
        vmem=10 if small else 60,
        name="middle",
    )
    adapted_o, adapted_i, grad_adapt_d, normed_two, activity, grad_gates, middle_q, out_all, last_all = mid_outs[2:]
    if small:
        query_late = after(query, activity)
        summed, (query_x, query_y, query_n) = reduce_rows(
            *mid_outs[:2], across(query_late), ahead(query_late), near(query_late)
        )
        query_xy = ahead(query_x)
        query_all = [query, query_x, query_y, query_xy, query_n, near(query_x), near(query_y)]
    else:
        summed, _ = reduce_rows(*mid_outs[:2])
        query_all = plane_gather(query)
    feed_pieces = call(
        feed_body,
        [piece] * 2,
        ids,
        [after(activity, summed[0]), last_down, last_all],
        scratch=[pltpu.VMEM((count, wide), single)],
        name="feed",
    )
    summed, query_all, feed_pieces = lax.optimization_barrier((summed, query_all, feed_pieces))
    turn = ((quarter, local_width + ranks), low)
    *turned, grad_mid, grad_branch, grad_adapt_i = call(
        turn_body,
        [turn] * 4 + [((quarter, width), single), ((quarter, width), low), ((quarter, ranks), low)],
        ids,
        [*summed, picked, in_down, middle_q, gain_two, grad_out, out_up, out_all, *packed],
        vmem=6 if small else 40,
        name="turn",
        cost=3.0,
    )
    if small:
        query_all = query_all + [near(after(query_all[3], grad_mid))]
    arrived = exchange(turned)
    sizes = [width] * 4 + [padded(hidden)] * 3 + [3 * local_width, local_width]
    columns = sum(sizes)
    places = [(i, j) for i in range(fsdp_size) for j in range(context_size)]
    number = {place: at for at, place in enumerate(places)}
    side = {(i, j): (i, j ^ 1) for i, j in places}
    front = {(i, j): (i ^ 2, j) for i, j in places}
    one = [(number[p], number[front[p] if p[0] % 2 else side[p]]) for p in places]
    two = [(number[p], number[side[p] if p[0] % 2 else front[p]]) for p in places]
    rows = ranks // 8

    def fold_strips(keep, send):
        columns = keep.shape[1]
        return call(
            fold_body,
            [((2, rows, columns), low)] * 2,
            ids,
            [keep, near(send)],
            scratch=[pltpu.VMEM((ranks // 2, columns), single)],
            name="fold",
            cost=3.0,
        )

    def reduce_strips(own, got):
        columns = own.shape[2]
        mine, passed = call(
            pair_body,
            [((rows, columns), single), ((rows, columns), low)],
            ids,
            [own, got],
            name="pair_chips",
            cost=3.0,
        )
        return [mine, lax.ppermute(passed, token_axes, two)]

    (feed_mine, feed_got), _ = reduce_rows(*feed_pieces)
    arrived, query_all, feed_mine = lax.optimization_barrier((arrived, query_all, feed_mine))
    tail = 32
    message, delta_col, grad_adapt_o = call(
        collect_body,
        [((count + tail, local_width), low), ((count, 128), single), ((count, ranks), low)],
        ids,
        [*arrived, attended, lse_col],
        name="collect",
        cost=0.0,
    )
    (grad_query,) = call(
        query_body,
        [((count, local_width), single)],
        ids,
        [query, message, lse_col, delta_col, seg_col, groups, keyval_joined],
        scratch=[many, many, against],
        vmem=11 if small else 60,
        name="queries",
        cost=7.0,
    )
    message_all = [value.reshape(-1, count + tail, local_width) for value in plane_gather(message, grad_query)]
    output_q, adapted_d = call(
        out_body,
        [((quarter, width), low), ((quarter, ranks), low)],
        ids,
        [feed_mine, after(feed_got, grad_query), picked, middle_q, last_up],
        name="outputs",
    )
    output_all = spread(output_q)
    *last_pieces, grad_proj, part_adapt_q = call(
        lambda *refs: key_body(parts_n, *refs),
        [piece] * 2 + [((count, 3 * local_width), low), ((count, ranks), low)],
        ids,
        [after(keyval, output_q), seg_col, groups, grad_query, cos_full, sin_full, proj_up, picked, *proj_w, *query_all, *message_all],
        scratch=[
            pltpu.VMEM((8, total), single),
            slab,
            slab,
            pltpu.VMEM((count, wide), single),
            many,
            many,
            against,
            against,
            pltpu.VMEM((total, local_width), low),
            pltpu.VMEM((chunks, count, local_width), low),
            pltpu.VMEM((chunks, tail, local_width), low),
            pltpu.SemaphoreType.DMA((3 * parts_n,)),
        ],
        far=range(12, 12 + 2 * parts_n),
        vmem=21 if small else 60,
        name="keys",
        cost=10.0,
    )
    part_adapt_q, *output_all[1:3] = lax.optimization_barrier((part_adapt_q, *output_all[1:3]))
    output_all[3] = over("tensor", tensor_size, 1, output_all[2])
    last_mine, last_got = reduce_rows(*last_pieces)[0]
    late = call(
        grads_body,
        [((ranks // 2, columns), low)] * 2,
        ids,
        [grad_adapt_i, normed_two, adapted_o, grad_branch, adapted_d, grad_out,
         part_adapt_q, normed_one, adapted_i,
         grad_gates, grad_adapt_d, activity, adapted_q, grad_proj, grad_adapt_o, heads_out],
        scratch=[pltpu.VMEM((ranks, columns), single)],
        vmem=5 if small else 40,
        name="grads",
        cost=3.0,
    )
    def finish_tokens(got):
        return call(
            last_body,
            [((quarter, width), low)],
            ids,
            [last_mine, got, picked, proj_down, tokens, gain_one, grad_mid],
            name="last",
        )

    finals = [((ranks, width), single)] * 4 + [((ranks, 2, hidden), single), ((ranks, hidden), single)]
    finals = finals + [((sets, 3, rank, local_width), single), ((ranks, local_width), single)]
    if small:
        late_own, late_out = fold_strips(*late)
        late_mine, late_got = reduce_strips(late_own, lax.ppermute(late_out, token_axes, one))
        shared, rest = call(
            total_body,
            [((rows, 4 * width), low), ((rows, columns - 4 * width), low)],
            ids,
            [late_mine, late_got],
            name="total",
            cost=3.0,
        )
        shared_near, last_got = lax.optimization_barrier((over("tensor", tensor_size, 1, shared), last_got))
        (grad_tokens_q,) = finish_tokens(last_got)
        (shared,) = call(add_body, [((rows, 4 * width), low)], ids, [shared, shared_near], name="add")
        shared_far = over("tensor", tensor_size, 2, shared)
        (output,) = call(assemble_body, [((count, width), low)], ids, output_all, name="join_output")
        rest, output, grad_tokens_q = lax.optimization_barrier((rest, output, grad_tokens_q))
        tokens_all = spread(grad_tokens_q)
        (joined,) = call(
            join_body,
            [((rows, columns), low)],
            ids,
            [shared, shared_far, rest],
            name="join",
            cost=3.0,
        )
        beside = lax.ppermute(joined, token_axes, two)
        both = jnp.stack([joined, after(beside, tokens_all[1], tokens_all[2])])
        others = lax.ppermute(both, token_axes, one)
        strips = [joined, beside, after(others, tokens_all[3])]
        strips = strips + [near(value) for value in strips]
        results = call(finish_body, finals, ids, strips, name="finish")
    else:
        (grad_tokens_q,) = finish_tokens(last_got)
        tokens_all = spread(grad_tokens_q)
        (output,) = call(assemble_body, [((count, width), low)], ids, output_all, name="join_output")
        pair = jnp.where(f % 2 == 0, jnp.concatenate(late), jnp.concatenate(late[::-1]))
        pair = lax.psum(pair, token_axes)
        joined = jnp.concatenate([lax.psum(pair[:, : 4 * width], "tensor"), pair[:, 4 * width :]], axis=1)
        cut = [0]
        for span in [width] * 4 + [padded(hidden)] * 3 + [3 * local_width, local_width]:
            cut.append(cut[-1] + span)
        slices = [joined[:, lo:hi].astype(single) for lo, hi in zip(cut, cut[1:])]
        *results, gate_up, mult_up, last_grad, proj_up_grad, out_down_grad = slices
        results = [*results, jnp.stack([gate_up[:, :hidden], mult_up[:, :hidden]], axis=1), last_grad[:, :hidden]]
        proj_up_grad = jnp.transpose(proj_up_grad.reshape(sets, rank, 3, local_width), (0, 2, 1, 3))
        results = [*results, proj_up_grad, out_down_grad]

    in_down_grad, out_up_grad, last_up_grad, proj_down_grad, in_up_grad, last_grad, proj_up_grad, out_down_grad = results
    (grad_tokens,) = call(assemble_body, [((count, width), low)], ids, tokens_all, name="join_tokens")


    def down(grad):
        return jnp.transpose(grad.reshape(sets, rank, -1), (0, 2, 1))

    return (
        output,
        grad_tokens,
        down(proj_down_grad),
        jnp.transpose(proj_up_grad, (0, 2, 1, 3)),
        down(out_down_grad),
        out_up_grad.reshape(sets, rank, width),
        down(in_down_grad),
        in_up_grad.reshape(sets, rank, 2, hidden),
        down(last_grad),
        last_up_grad.reshape(sets, rank, width),
    )


def solution(mesh):
    return jax.shard_map(
        on_device,
        mesh=mesh,
        in_specs=(
            P(("fsdp", "context"), None),
            P(("fsdp", "context"), None),
            P(),
            P(),
            P(),
            P(),
            P("fsdp", None, "tensor"),
            P("tensor", "fsdp"),
            P(),
            P("fsdp", None, "tensor"),
            P("tensor", "fsdp"),
            P(),
            P(None, None, None, "tensor"),
            P(None, "tensor", None),
            P(),
            P(),
            P(None, None, None, "tensor"),
            P(None, "tensor", None),
            P(),
        ),
        out_specs=(
            P(("fsdp", "context"), None),
            P(("fsdp", "context"), None),
            P(),
            P(None, None, None, "tensor"),
            P(None, "tensor", None),
            P(),
            P(),
            P(None, None, None, "tensor"),
            P(None, "tensor", None),
            P(),
        ),
        check_vma=False,
    )
```
